32 devices in a mesh: planes: 16 (over z, y, x), elem: 2 (over core).
Axes of the slice: x: 2, y: 2, z: 4, core: 2. Of those that a mesh axis runs over, the one named last changes fastest.
Arguments:
- velocity: float32 [3, 256, 20736], P(None, 'planes', 'elem'), may hold values from -6 to 6
- geometry: float32 [4, 20736], P(None, 'elem'), may hold values from -1.5 to 1.5
- element_kind: int32 [256], P('elem'), may hold values from 0 to 1
- element_scale: float32 [256], P('elem'), may hold values from 0.5 to 2
- dirichlet: int32 [2, 9, 256], P(None, None, 'elem'), may hold values 0 or 1
- schur_stiffness: float32 [2, 36, 36], replicated, may hold values from -0.2 to 8.5, as said below
- schur_mass: float32 [2, 36, 36], replicated, may hold values from -0.1 to 4.5, as said below
- lift: float32 [2, 36, 81], replicated, may hold values from -0.625 to 0.625
- recover: float32 [2, 81, 36], replicated, may hold values from -1 to 1
Outputs:
- new_velocity: float32 [3, 256, 20736], P(None, 'planes', 'elem')
The draws below stay inside these ranges and needn't reach their ends.
Inputs may be any that keep to these rules, and one draw needn't show every extreme that they name: `schur_stiffness`: each of the two matrices is symmetric and positive definite. `schur_mass`: each of the two matrices is symmetric and positive definite.
All inputs are finite; a program needn't handle non-finite values. No bound on the sum of `dirichlet` on one device may be relied on, other than what follows from the above.
Results may differ from the reference program's by a relative error of at most 0.0001.
Values sent between devices are 32-bit elements; how exact they have to be, the bound alone decides.
A program may use at most 128 MiB of HBM per device.

```python
import math
import jax
import jax.numpy as jnp
import numpy as np
from jax import lax

PLANES = 256
QUAD = 9
COLUMN_ELEMS = 32
CG_STEPS = 4
ELEMS = 256
NODES = 20736


def symmetric_dominant(key, off_scale, lo, hi):
    size = 4 * QUAD
    keys = jax.random.split(key, 2)
    upper = jnp.triu(jax.random.uniform(keys[0], (2, size, size), jnp.float32, -off_scale, off_scale), 1)
    off_part = upper + jnp.swapaxes(upper, 1, 2)
    rowsum = jnp.sum(jnp.abs(off_part), axis=2)
    extra = jax.random.uniform(keys[1], (2, size), jnp.float32, lo, hi)
    return off_part + jnp.eye(size, dtype=jnp.float32)[None] * (rowsum + extra)[:, :, None]


def draw_schur_stiffness(key, part):
    return symmetric_dominant(jax.random.fold_in(key, 11), 0.2, 0.5, 1.5)


def draw_schur_mass(key, part):
    return symmetric_dominant(jax.random.fold_in(key, 23), 0.1, 0.5, 1.0)


def place_ends(result, stream_key, low, largest):
    index_at = [jax.random.randint(jax.random.fold_in(stream_key, axis), (), 0, length) for axis, length in enumerate(result.shape)]
    longest = result.shape.index(max(result.shape))
    neighbour = index_at[:longest] + [(index_at[longest] + 1) % result.shape[longest]] + index_at[longest + 1:]
    return result.at[tuple(index_at)].set(low).at[tuple(neighbour)].set(largest)


def block_levels(key, dims, cuts, least, largest):
    def one(position, blocks):
        steps = jax.random.uniform(jax.random.fold_in(jax.random.fold_in(key, 6), position), (blocks,), jnp.float32, least / len(cuts), largest / len(cuts))
        return jnp.repeat(jnp.exp(steps), dims[position] // blocks).reshape((-1,) + (1,) * (len(dims) - position - 1))

    gain = one(*cuts[0])
    for cut in cuts[1:]:
        gain = gain * one(*cut)
    return gain


def centred(stream_key, extent, deviation, bound, shards=(), kind=jnp.bfloat16):
    factor_of = block_levels(stream_key, extent, shards, -0.22, 0.18) if shards else 1.0
    result = jax.random.normal(stream_key, extent, jnp.float32) * deviation * factor_of
    return jnp.minimum(jnp.maximum(result, -bound), bound).astype(kind)


def setup_inputs(seed: int = 0) -> dict:
    streams_of = jax.random.split(jax.random.key(seed), 10)
    velocity = centred(streams_of[0], (3, PLANES, NODES), 1.0, 6.0, ((1, 16), (2, 2)), jnp.float32)
    geometry = jnp.clip(jax.random.uniform(streams_of[1], (4, NODES), jnp.float32, -1.5, 1.5) * block_levels(streams_of[1], (4, NODES), ((1, 2),), -0.4, 0.0), -1.5, 1.5)
    element_kind = place_ends(jax.random.randint(streams_of[2], (ELEMS,), 0, 2), jax.random.fold_in(streams_of[2], 1), 0, 1).astype(jnp.int32)
    element_scale = jnp.clip(jnp.exp(math.log(2.0) - 1.3862944 * jax.random.uniform(streams_of[3], (ELEMS,), jnp.float32) ** block_levels(streams_of[3], (ELEMS,), ((0, 2),), -0.2, 0.2)), 0.5, 2.0)
    dirichlet = place_ends((jax.random.randint(streams_of[4], (2, QUAD, ELEMS), 0, 6) < 1).astype(jnp.int32), jax.random.fold_in(streams_of[4], 1), 0, 1)
    schur_stiffness = draw_schur_stiffness(jax.random.fold_in(streams_of[9], 71), 0)
    schur_mass = draw_schur_mass(jax.random.fold_in(streams_of[9], 71), 0)
    lift = centred(streams_of[7], (2, 4 * QUAD, QUAD * QUAD), (QUAD * QUAD) ** -0.5, 0.625, (), jnp.float32)
    recover = centred(streams_of[8], (2, QUAD * QUAD, 4 * QUAD), (4 * QUAD) ** -0.5, 1.0, (), jnp.float32)
    return {"velocity": velocity, "geometry": geometry, "element_kind": element_kind, "element_scale": element_scale, "dirichlet": dirichlet, "schur_stiffness": schur_stiffness, "schur_mass": schur_mass, "lift": lift, "recover": recover}


HIGHEST = lax.Precision.HIGHEST
SIGMA_COEF = 1.0
BETA_COEF = 0.01
STEP_DT = 0.002


def gauss_derivative(points):
    nodes = -np.cos(np.pi * (2 * np.arange(points) + 1) / (2 * points))
    ident = np.eye(points)
    diffs = nodes[:, None] - nodes[None, :] + ident
    weights = 1.0 / np.prod(diffs, axis=1)
    matrix = (weights[None, :] / weights[:, None]) / diffs
    matrix = matrix * (1.0 - ident)
    return matrix - ident * matrix.sum(axis=1)[:, None]


def kron_tables():
    deriv = gauss_derivative(QUAD)
    identity = np.eye(QUAD)
    return jnp.asarray(np.kron(deriv, identity), jnp.float32), jnp.asarray(np.kron(identity, deriv), jnp.float32)


def synthesize(coef, slope):
    planes = coef.shape[1]
    half = planes // 2
    pairs = coef[:, 1:planes - 1].reshape(coef.shape[0], half - 1, 2, coef.shape[2])
    cosine = pairs[:, :, 0]
    sine = pairs[:, :, 1]
    mean = coef[:, :1]
    top = coef[:, planes - 1:]
    if slope:
        rate = BETA_COEF * jnp.arange(1, half, dtype=jnp.float32)[None, :, None]
        cosine, sine = rate * sine, -rate * cosine
        mean = jnp.zeros_like(mean)
        top = jnp.zeros_like(top)
    real = jnp.concatenate([mean * planes, cosine * (planes / 2), top * planes], axis=1)
    imag = jnp.concatenate([jnp.zeros_like(mean), -sine * (planes / 2), jnp.zeros_like(top)], axis=1)
    return jnp.fft.irfft(lax.complex(real, imag), n=planes, axis=1)


def analyze(field):
    planes = field.shape[1]
    spectrum = jnp.fft.rfft(field, axis=1)
    real = jnp.real(spectrum)
    imag = jnp.imag(spectrum)
    mean = real[:, :1] / planes
    top = real[:, planes // 2:] / planes
    cosine = real[:, 1:planes // 2] * (2.0 / planes)
    sine = -imag[:, 1:planes // 2] * (2.0 / planes)
    pairs = jnp.stack([cosine, sine], axis=2).reshape(field.shape[0], planes - 2, field.shape[2])
    return jnp.concatenate([mean, pairs, top], axis=1)


def advect_block(coef, geo, first, second):
    values = synthesize(coef, False)
    along_z = synthesize(coef, True)
    shaped = values.reshape(3, values.shape[1], -1, QUAD * QUAD)
    along_r = jnp.einsum('cpen,mn->cpem', shaped, first, precision=HIGHEST).reshape(values.shape)
    along_s = jnp.einsum('cpen,mn->cpem', shaped, second, precision=HIGHEST).reshape(values.shape)
    along_x = geo[0] * along_r + geo[1] * along_s
    along_y = geo[2] * along_r + geo[3] * along_s
    advection = values[0] * along_x + values[1] * along_y + values[2] * along_z
    return analyze(advection)


def element_vector(vertical, horizontal):
    right = jnp.concatenate([vertical[:, :, COLUMN_ELEMS:], jnp.zeros_like(vertical[:, :, :COLUMN_ELEMS])], axis=2)
    grid = horizontal.reshape(horizontal.shape[0], horizontal.shape[1], -1, COLUMN_ELEMS)
    top = jnp.concatenate([grid[..., 1:], jnp.zeros_like(grid[..., :1])], axis=3).reshape(horizontal.shape)
    return jnp.concatenate([vertical, right, horizontal, top], axis=0)


def element_apply(vector, lam, second_kind, scale, stiffness, mass):
    flat = vector.reshape(vector.shape[0], -1)
    results = []
    for kind in range(2):
        stiff = jnp.dot(stiffness[kind], flat, precision=HIGHEST).reshape(vector.shape)
        massed = jnp.dot(mass[kind], flat, precision=HIGHEST).reshape(vector.shape)
        results.append(stiff + lam[None, :, None] * massed)
    return scale[None, None, :] * jnp.where(second_kind[None, None, :], results[1], results[0])


def assemble(outputs, free):
    left = outputs[:QUAD]
    right = outputs[QUAD:2 * QUAD]
    bottom = outputs[2 * QUAD:3 * QUAD]
    top = outputs[3 * QUAD:]
    vertical = left + jnp.concatenate([jnp.zeros_like(right[:, :, :COLUMN_ELEMS]), right[:, :, :-COLUMN_ELEMS]], axis=2)
    grid = top.reshape(top.shape[0], top.shape[1], -1, COLUMN_ELEMS)
    shifted = jnp.concatenate([jnp.zeros_like(grid[..., :1]), grid[..., :-1]], axis=3).reshape(bottom.shape)
    horizontal = bottom + shifted
    return vertical * free[0], horizontal * free[1]


def inner(first_pair, second_pair):
    return jnp.sum(first_pair[0] * second_pair[0], axis=(0, 2)) + jnp.sum(first_pair[1] * second_pair[1], axis=(0, 2))


def solve_component(comp, lam, free, second_kind, scale, stiffness, mass, lift, recover):
    planes = comp.shape[0]
    node_values = (SIGMA_COEF * comp).reshape(planes, ELEMS, QUAD * QUAD)
    lifted = jnp.where(second_kind[None, None, :],
                       jnp.einsum('kn,ren->kre', lift[1], node_values, precision=HIGHEST),
                       jnp.einsum('kn,ren->kre', lift[0], node_values, precision=HIGHEST))
    forcing = assemble(lifted, free)
    trace = (jnp.zeros_like(forcing[0]), jnp.zeros_like(forcing[1]))
    residual = forcing
    direction = forcing
    norm_now = inner(residual, residual)
    for sweep in range(CG_STEPS):
        image = assemble(element_apply(element_vector(direction[0], direction[1]), lam, second_kind, scale, stiffness, mass), free)
        alpha = (norm_now / inner(direction, image))[None, :, None]
        trace = (trace[0] + alpha * direction[0], trace[1] + alpha * direction[1])
        residual = (residual[0] - alpha * image[0], residual[1] - alpha * image[1])
        norm_next = inner(residual, residual)
        ratio = (norm_next / norm_now)[None, :, None]
        direction = (residual[0] + ratio * direction[0], residual[1] + ratio * direction[1])
        norm_now = norm_next
    vector = element_vector(trace[0], trace[1])
    recovered = jnp.where(second_kind[None, :, None],
                          jnp.einsum('nl,lre->ren', recover[1], vector, precision=HIGHEST),
                          jnp.einsum('nl,lre->ren', recover[0], vector, precision=HIGHEST))
    weight = SIGMA_COEF / (SIGMA_COEF + lam)
    return comp * weight[:, None] + recovered.reshape(comp.shape)


def reference(velocity, geometry, element_kind, element_scale, dirichlet, schur_stiffness, schur_mass, lift, recover):
    first, second = kron_tables()
    planes = velocity.shape[1]
    columns = ELEMS // COLUMN_ELEMS
    width = COLUMN_ELEMS * QUAD * QUAD
    blocks = velocity.reshape(3, planes, columns, width).transpose(2, 0, 1, 3)
    geo_blocks = geometry.reshape(4, columns, width).transpose(1, 0, 2)
    advected = lax.map(lambda pair: advect_block(pair[0], pair[1], first, second), (blocks, geo_blocks))
    advection_hat = advected.transpose(1, 2, 0, 3).reshape(velocity.shape)
    intermediate = velocity - STEP_DT * advection_hat
    waves = ((jnp.arange(planes, dtype=jnp.int32) + 1) // 2).astype(jnp.float32)
    lam = SIGMA_COEF + (BETA_COEF * waves) ** 2
    free = (1 - dirichlet).astype(jnp.float32)[:, :, None, :]
    second_kind = element_kind == 1
    return lax.map(lambda comp: solve_component(comp, lam, free, second_kind, element_scale,
                                                schur_stiffness, schur_mass, lift, recover), intermediate)
```

```python
import functools
import math

import jax
import jax.numpy as jnp
import numpy as np
from jax import lax
from jax.experimental import pallas as pl
from jax.experimental.pallas import tpu as pltpu
from jax.sharding import PartitionSpec as P

PLANES = 256
QUAD = 9
COLUMN_ELEMS = 32
CG_STEPS = 4


HIGHEST = lax.Precision.HIGHEST
SIGMA_COEF = 1.0
BETA_COEF = 0.01
STEP_DT = 0.002


def passed_along(value, axis, steps):
    count = lax.axis_size(axis)
    leading, last = (max(0, -steps), min(count, count - steps))
    return lax.ppermute(value, axis, [(source, source + steps) for source in range(leading, last)])


def gauss_derivative(points):
    nodes = -np.cos(np.pi * (2 * np.arange(points) + 1) / (2 * points))
    ident = np.eye(points)
    diffs = nodes[:, None] - nodes[None, :] + ident
    weights = 1.0 / np.prod(diffs, axis=1)
    matrix = weights[None, :] / weights[:, None] / diffs
    matrix = matrix * (1.0 - ident)
    return matrix - ident * matrix.sum(axis=1)[:, None]


def kron_tables():
    deriv = gauss_derivative(QUAD)
    identity = np.eye(QUAD)
    return (
        jnp.asarray(np.kron(deriv, identity), jnp.float32),
        jnp.asarray(np.kron(identity, deriv), jnp.float32),
    )


def fourier_tables(planes):
    zeta = jnp.arange(planes, dtype=jnp.int32)
    rows = jnp.arange(planes, dtype=jnp.int32)
    waves = (rows + 1) // 2
    phase = waves[None, :] * zeta[:, None] % planes
    angle = 2.0 * math.pi / planes * phase.astype(jnp.float32)
    cosine = jnp.cos(angle)
    sine = jnp.sin(angle)
    odd = (rows % 2 == 1)[None, :]
    first = (rows == 0)[None, :]
    last = (rows == planes - 1)[None, :]
    synth = jnp.where(first, 1.0, jnp.where(odd, cosine, sine))
    rate = BETA_COEF * waves.astype(jnp.float32)[None, :]
    slope = jnp.where(first | last, 0.0, jnp.where(odd, -rate * sine, rate * cosine))
    weight = jnp.where((rows == 0) | (rows == planes - 1), 1.0 / planes, 2.0 / planes).astype(
        jnp.float32
    )
    analysis = synth.T * weight[:, None]
    return (synth, slope, analysis)


def inner(first_pair, second_pair):
    return jnp.sum(first_pair[0] * second_pair[0], axis=(0, 2)) + jnp.sum(
        first_pair[1] * second_pair[1], axis=(0, 2)
    )


def global_total(first_pair, second_pair):
    return lax.psum(inner(first_pair, second_pair), "elem")


def global_squares(pair):
    return lax.psum(inner(pair, pair), "elem")


def assemble(outputs, incoming, free):
    left = outputs[:QUAD]
    right = outputs[QUAD : 2 * QUAD]
    bottom = outputs[2 * QUAD : 3 * QUAD]
    top = outputs[3 * QUAD :]
    vertical = left + jnp.concatenate([incoming, right[:, :, :-COLUMN_ELEMS]], axis=2)
    grid = top.reshape(top.shape[0], top.shape[1], -1, COLUMN_ELEMS)
    shifted = jnp.concatenate([jnp.zeros_like(grid[..., :1]), grid[..., :-1]], axis=3).reshape(
        bottom.shape
    )
    horizontal = bottom + shifted
    return (vertical * free[0], horizontal * free[1])


def plain_device(
    velocity,
    geometry,
    element_kind,
    element_scale,
    dirichlet,
    schur_stiffness,
    schur_mass,
    lift,
    recover,
):
    first, second = kron_tables()
    synth, slope, analysis = fourier_tables(PLANES)
    local_rows = velocity.shape[1]
    node_count = velocity.shape[2]
    share = node_count // lax.axis_size("planes")
    geo_part = lax.dynamic_slice_in_dim(geometry, lax.axis_index("planes") * share, share, 1)

    def transform(table, field):
        return jnp.einsum("zr,crm->czm", table, field, precision=HIGHEST)

    items = lax.all_to_all(velocity, "planes", split_axis=2, concat_axis=1, tiled=True)
    values = transform(synth, items)
    along_z = transform(slope, items)
    shaped = values.reshape(values.shape[:-1] + (-1, QUAD * QUAD))
    along_r = jnp.einsum("...en,mn->...em", shaped, first, precision=HIGHEST).reshape(values.shape)
    along_s = jnp.einsum("...en,mn->...em", shaped, second, precision=HIGHEST).reshape(values.shape)
    along_x = geo_part[0] * along_r + geo_part[1] * along_s
    along_y = geo_part[2] * along_r + geo_part[3] * along_s
    values, along_x, along_y, along_z = (values, along_x, along_y, along_z)
    advection = values[0] * along_x + values[1] * along_y + values[2] * along_z
    advection_hat = jnp.einsum("rz,czm->crm", analysis, advection, precision=HIGHEST)
    returned = lax.all_to_all(advection_hat, "planes", split_axis=1, concat_axis=2, tiled=True)
    intermediate = velocity - STEP_DT * returned
    elem_count = element_kind.shape[0]
    row_count = 3 * local_rows
    waves = (
        (lax.axis_index("planes") * local_rows + jnp.arange(local_rows, dtype=jnp.int32) + 1) // 2
    ).astype(jnp.float32)
    lam = jnp.tile(SIGMA_COEF + (BETA_COEF * waves) ** 2, 3)
    free = (1 - dirichlet).astype(jnp.float32)[:, :, None, :]
    chooser = (element_kind == 1).astype(jnp.float32)

    def element_apply(vector, kinds, scales):
        flat = vector.reshape(vector.shape[0], -1)
        results = []
        for kind in range(2):
            stiff = jnp.dot(schur_stiffness[kind], flat, precision=HIGHEST).reshape(vector.shape)
            massed = jnp.dot(schur_mass[kind], flat, precision=HIGHEST).reshape(vector.shape)
            results.append(stiff + lam[None, :, None] * massed)
        return scales[None, None, :] * jnp.where(kinds[None, None, :] > 0.5, results[1], results[0])

    def element_vector(vertical, horizontal):
        arriving = passed_along(vertical[:, :, :COLUMN_ELEMS], "elem", -1)
        right = jnp.concatenate([vertical[:, :, COLUMN_ELEMS:], arriving], axis=2)
        grid = horizontal.reshape(horizontal.shape[0], horizontal.shape[1], -1, COLUMN_ELEMS)
        top = jnp.concatenate([grid[..., 1:], jnp.zeros_like(grid[..., :1])], axis=3).reshape(
            horizontal.shape
        )
        return jnp.concatenate([vertical, right, horizontal, top], axis=0)

    node_values = (SIGMA_COEF * intermediate).reshape(row_count, elem_count, QUAD * QUAD)
    lifted = jnp.where(
        chooser[None, None, :] > 0.5,
        jnp.einsum("kn,ren->kre", lift[1], node_values, precision=HIGHEST),
        jnp.einsum("kn,ren->kre", lift[0], node_values, precision=HIGHEST),
    )
    lifted_right = passed_along(lifted[QUAD : 2 * QUAD, :, -COLUMN_ELEMS:], "elem", 1)
    forcing = assemble(lifted, lifted_right, free)
    trace = (jnp.zeros_like(forcing[0]), jnp.zeros_like(forcing[1]))
    residual = forcing
    direction = forcing
    norm_now = global_squares(residual)
    for sweep in range(CG_STEPS):
        outputs = element_apply(element_vector(direction[0], direction[1]), chooser, element_scale)
        operator_arriving = passed_along(outputs[QUAD : 2 * QUAD, :, -COLUMN_ELEMS:], "elem", 1)
        image = assemble(outputs, operator_arriving, free)
        alpha = (norm_now / global_total(direction, image))[None, :, None]
        trace = (trace[0] + alpha * direction[0], trace[1] + alpha * direction[1])
        residual = (residual[0] - alpha * image[0], residual[1] - alpha * image[1])
        norm_next = global_squares(residual)
        ratio = (norm_next / norm_now)[None, :, None]
        direction = (residual[0] + ratio * direction[0], residual[1] + ratio * direction[1])
        norm_now = norm_next
    vector = element_vector(trace[0], trace[1])
    recovered = jnp.where(
        chooser[None, :, None] > 0.5,
        jnp.einsum("nl,lre->ren", recover[1], vector, precision=HIGHEST),
        jnp.einsum("nl,lre->ren", recover[0], vector, precision=HIGHEST),
    )
    weight = SIGMA_COEF / (SIGMA_COEF + lam)
    result = (
        intermediate.reshape(row_count, elem_count, QUAD * QUAD) * weight[:, None, None] + recovered
    )
    return result.reshape(velocity.shape)


LANES = 128
SUB = 16
F32 = jnp.float32
BF16 = jnp.bfloat16


def split(value):
    high = value.astype(BF16)
    return high, (value - high.astype(F32)).astype(BF16)


def np_split(value):
    high = np.asarray(value, np.float32).astype(BF16)
    low = (np.asarray(value, np.float64) - high.astype(np.float64)).astype(np.float32).astype(BF16)
    return high, low


def mm(first, second):
    return jnp.dot(first, second, preferred_element_type=F32)


def stacked_weights(weights):
    high, low = split(weights)
    return jnp.concatenate([high, high, low], axis=1)


def stacked_values(values):
    high, low = split(values)
    return jnp.concatenate([high, low, high], axis=0)


def advect_tables(planes):
    zeta = np.arange(planes)
    rows = np.arange(planes)
    waves = (rows + 1) // 2
    angle = 2.0 * np.pi / planes * ((waves[None, :] * zeta[:, None]) % planes)
    odd = (rows % 2 == 1)[None, :]
    first = (rows == 0)[None, :]
    last = (rows == planes - 1)[None, :]
    synth = np.where(first, 1.0, np.where(odd, np.cos(angle), np.sin(angle)))
    rate = BETA_COEF * waves[None, :]
    slope = np.where(first | last, 0.0, np.where(odd, -rate * np.sin(angle), rate * np.cos(angle)))
    weight = np.where((rows == 0) | (rows == planes - 1), 1.0 / planes, 2.0 / planes)
    analysis = synth.T * weight[:, None]
    high, low = np_split(np.concatenate([synth, slope], axis=0))
    forward = np.concatenate([high, high, low], axis=1)
    high, low = np_split(analysis)
    backward = np.concatenate([high, high, low], axis=1)
    points = QUAD * QUAD
    deriv = gauss_derivative(QUAD)
    both = np.zeros((LANES, 2 * LANES))
    both[:points, :points] = np.kron(deriv, np.eye(QUAD)).T
    both[:points, LANES : LANES + points] = np.kron(np.eye(QUAD), deriv).T
    high, low = np_split(both)
    return jnp.asarray(forward), jnp.asarray(backward), jnp.asarray(np.concatenate([high, high, low], axis=0))


def whole_spec(shape):
    return pl.BlockSpec(shape, lambda *_: (0,) * len(shape))


def params():
    return pltpu.CompilerParams(vmem_limit_bytes=60 * 1024 * 1024)


def element_at(part, slot, group):
    inner = part % group
    return part // group * COLUMN_ELEMS + slot * group + inner % 2 * (group // 2) + inner // 2


def solve_rows(forcing, facts, lam, weights, state, image, traces):
    tiles = forcing.shape[0]
    lane = lax.broadcasted_iota(jnp.int32, (SUB, LANES), 1)
    top_edge = lane >= LANES - 8
    low_edge = lane < 8
    zero = jnp.zeros((SUB, LANES), F32)

    def above(tile_of, at):
        if at % 2 == 0:
            return tile_of(at + 1)
        return jnp.where(top_edge, 0.0, pltpu.roll(tile_of(at - 1), LANES - 8, 1))

    def gather(parts, at):
        left = parts[at][:SUB]
        if at >= 2:
            left = left + parts[at - 2][SUB : 2 * SUB]
        if at % 2 == 1:
            under = parts[at - 1][3 * SUB :]
        else:
            under = jnp.where(low_edge, 0.0, pltpu.roll(parts[at + 1][3 * SUB :], 8, 1))
        fact = facts[at]
        return left * fact[:SUB], (parts[at][2 * SUB : 3 * SUB] + under) * fact[SUB : 2 * SUB]

    def total(acc):
        acc = jnp.sum(acc, axis=0, keepdims=True)
        acc = jnp.broadcast_to(acc, (8, LANES))
        for step in (8, 16, 32, 64):
            acc = acc + pltpu.roll(acc, step, 1)
        return acc[0:1]

    def apply():
        acc = zero
        parts = []

        def halves(which, at):
            return split(state[2, which, at])

        verticals = [halves(0, at) for at in range(2)]
        none = (zero.astype(BF16), zero.astype(BF16))
        for column in range(tiles // 2):
            first = 2 * column
            if first + 2 < tiles:
                verticals = verticals + [halves(0, at) for at in range(first + 2, first + 4)]
            else:
                verticals = verticals + [none, none]
            stacks = []
            for at in (first, first + 1):
                pieces = [
                    verticals[at],
                    verticals[at + 2],
                    halves(1, at),
                    split(above(lambda item: state[2, 1, item], at)),
                ]
                high = [piece[0] for piece in pieces]
                low = [piece[1] for piece in pieces]
                stacks.append(jnp.concatenate(high + low + high, axis=0))
            both = mm(weights[...], jnp.concatenate(stacks, axis=1))
            rows = 4 * SUB
            for at in (first, first + 1):
                lanes = slice((at - first) * LANES, (at - first + 1) * LANES)
                fact = facts[at]
                is_second = fact[2 * SUB : 2 * SUB + 1] > 0.5
                stiff = jnp.where(is_second, both[rows : 2 * rows, lanes], both[:rows, lanes])
                mass = jnp.where(is_second, both[3 * rows :, lanes], both[2 * rows : 3 * rows, lanes])
                parts.append(fact[2 * SUB + 1 : 2 * SUB + 2] * (stiff + lam * mass))
            for at in (first, first + 1):
                im_v, im_h = gather(parts, at)
                image[0, at] = im_v
                image[1, at] = im_h
                acc = acc + (state[2, 0, at] * im_v + state[2, 1, at] * im_h)
        return total(acc)

    acc = zero
    parts = {}
    for at in range(tiles):
        parts[at] = forcing[at]
    for at in range(tiles):
        for which, value in enumerate(gather(parts, at)):
            state[0, which, at] = zero
            state[1, which, at] = value
            state[2, which, at] = value
            acc = acc + value * value
    now = total(acc)

    def sweep(_, now):
        alpha = now / apply()
        acc = zero
        for at in range(tiles):
            for which in range(2):
                state[0, which, at] = state[0, which, at] + alpha * state[2, which, at]
                rest = state[1, which, at] - alpha * image[which, at]
                state[1, which, at] = rest
                acc = acc + rest * rest
        fresh = total(acc)
        ratio = fresh / now
        for at in range(tiles):
            for which in range(2):
                state[2, which, at] = state[1, which, at] + ratio * state[2, which, at]
        return fresh

    now = lax.fori_loop(0, CG_STEPS - 1, sweep, now)
    alpha = now / apply()
    found = [
        [state[0, which, at] + alpha * state[2, which, at] for at in range(tiles)] for which in range(2)
    ]
    for at in range(tiles):
        traces[at, :SUB] = found[0][at]
        traces[at, SUB : 2 * SUB] = found[0][at + 2] if at + 2 < tiles else zero
        traces[at, 2 * SUB : 3 * SUB] = found[1][at]
        traces[at, 3 * SUB :] = above(lambda item: found[1][item], at)


def exact(first, second):
    return jnp.dot(first, second, precision=HIGHEST, preferred_element_type=F32)


def iota(shape, axis):
    return lax.broadcasted_iota(jnp.int32, shape, axis)


def lam_of(row):
    return SIGMA_COEF + (BETA_COEF * ((row + 1) // 2).astype(F32)) ** 2


def advect_and_solve(velocity, geometry, kind, scale, dirichlet, stiffness, mass, lift_maps, recover_maps, count):
    elems = kind.shape[1]
    comps, rows, nodes = velocity.shape
    points = QUAD * QUAD
    per = LANES // rows
    pairs = per // 2
    planes = count * rows
    half = count * LANES // 2
    forward, backward, deriv = advect_tables(planes)

    group = COLUMN_ELEMS // per
    columns = count // group
    tiles = count // 2
    chunk = tiles // columns
    ends = 2

    def kernel(
        vel_ref, geo_ref, kind_ref, scale_ref, fixed_ref, stiff_ref, mass_ref, lift_in, recover_in,
        forward_ref, backward_ref, deriv_ref,
        out,
        mid, kinds, factor, recover_out, sent, recv, hats, ret,
        store, turned, fields, partial, pieces, forcing, traces, found, facts_out, facts,
        state, image, geo, lift_ref, mat_ref, lam_ref, weights, lift_high, lift_low, recover_all,
        send_sem, recv_sem, pair_send, pair_recv,
    ):
        me = lax.axis_index("planes")
        core = lax.axis_index("elem")
        barrier = pltpu.get_barrier_semaphore()

        def peer_at(step):
            bits = count.bit_length() - 1
            peer = 0
            for bit in range(bits):
                weight = count // 2 // 2**bit
                peer = peer + weight * ((me // weight + step // 2**bit) % 2)
            return peer

        def greet(step, carry):
            pl.semaphore_signal(
                barrier, inc=1, device_id={"planes": peer_at(step)}, device_id_type=pl.DeviceIdType.MESH
            )
            return carry

        lax.fori_loop(1, count, greet, 0)
        pl.semaphore_signal(barrier, inc=1, device_id={"elem": 1 - core}, device_id_type=pl.DeviceIdType.MESH)

        def copy_to(source, target, way, comp, peer):
            return pltpu.make_async_remote_copy(
                src_ref=source.at[comp, peer],
                dst_ref=target.at[comp, me],
                send_sem=send_sem.at[way, comp, peer],
                recv_sem=recv_sem.at[way, comp, me],
                device_id={"planes": peer},
                device_id_type=pl.DeviceIdType.MESH,
            )

        def copy_from(source, target, way, comp, peer):
            return pltpu.make_async_remote_copy(
                src_ref=source.at[comp, peer],
                dst_ref=target.at[comp, peer],
                send_sem=send_sem.at[way, comp, peer],
                recv_sem=recv_sem.at[way, comp, peer],
                device_id={"planes": peer},
                device_id_type=pl.DeviceIdType.MESH,
            )

        def start_all(source, target, way, comp):
            def one(step, carry):
                copy_to(source, target, way, comp, peer_at(step)).start()
                return carry

            lax.fori_loop(1, count, one, 0)

        def pair_copy(source, target, at):
            return pltpu.make_async_remote_copy(
                src_ref=source,
                dst_ref=target,
                send_sem=pair_send.at[at],
                recv_sem=pair_recv.at[at],
                device_id={"elem": 1 - core},
                device_id_type=pl.DeviceIdType.MESH,
            )

        def facts_copy():
            return pair_copy(facts_out, facts.at[pl.ds(core * tiles, tiles)], comps * (columns + ends))

        def facts_arrive():
            pair_copy(facts_out, facts.at[pl.ds((1 - core) * tiles, tiles)], comps * (columns + ends)).wait_recv()

        def lifted_copy(comp, column, side):
            return pair_copy(
                pieces.at[comp, 1 - core, pl.ds(column * chunk, chunk)],
                forcing.at[comp, pl.ds(side * tiles + column * chunk, chunk)],
                comp * columns + column,
            )

        def trace_copy(comp, end, side):
            width = tiles // ends
            return pair_copy(
                traces.at[comp, pl.ds((1 - core) * tiles + end * width, width)],
                found.at[comp, side, pl.ds(end * width, width)],
                comps * columns + comp * ends + end,
            )

        def pack(comp):
            for part in range(count):
                rows_of = []
                for local in range(per):
                    at = element_at(part, local, group) * points
                    rows_of.append(vel_ref[comp, :, at : at + points])
                sent[comp, part] = jnp.concatenate(rows_of, axis=0).T

        def arrive(comp, part, block):
            block = jnp.concatenate([block, jnp.zeros((LANES - points, LANES), F32)], axis=0).T
            for local in range(per):
                at = local % 2 * LANES
                store[local // 2, pl.ds(pl.multiple_of(part * rows, rows), rows), at : at + LANES] = block[
                    local * rows : (local + 1) * rows
                ]

        def arrive_all(comp):
            arrive(comp, me, sent[comp, me])

            def one(step, carry):
                part = peer_at(step)
                copy_from(sent, recv, 0, comp, part).wait_recv()
                arrive(comp, part, recv[comp, part])
                return carry

            lax.fori_loop(1, count, one, 0)

        def over_pairs(body):
            def one(pair, carry):
                body(pair)
                return carry

            lax.fori_loop(0, pairs, one, 0)

        def synthesize(comp, pair):
            fields[comp, pair] = mm(forward_ref[...], stacked_values(store[pair]))

        def slope_last(pair):
            fields[comps - 1, pair, planes:] = mm(forward_ref[planes:], stacked_values(store[pair]))

        def derive(comp, pair):
            for which in range(2):
                at = slice(which * LANES, (which + 1) * LANES)
                high, low = split(fields[comp, pair, :planes, at])
                slopes = mm(jnp.concatenate([high, low], axis=1), deriv_ref[: 2 * LANES]) + mm(
                    high, deriv_ref[2 * LANES :]
                )
                part = geo[pair * 2 + which]
                first = fields[0, pair, :planes, at]
                second = fields[1, pair, :planes, at]
                partial[comp, pair, :, at] = slopes[:, :LANES] * (first * part[0:1] + second * part[2:3]) + slopes[
                    :, LANES:
                ] * (first * part[1:2] + second * part[3:4])

        def advect(comp, pair, along):
            result = partial[comp, pair] + along * fields[comp, pair, planes:]
            turned[pair] = mm(backward_ref[...], stacked_values(result))

        def first_advect(pair):
            along = mm(forward_ref[:planes], stacked_values(store[pair]))
            fields[comps - 1, pair, :planes] = along
            advect(0, pair, along)

        def send_back(comp):
            for part in range(count):
                block = jnp.concatenate(
                    [
                        turned[local // 2, part * rows : (part + 1) * rows, local % 2 * LANES : (local % 2 + 1) * LANES]
                        for local in range(per)
                    ],
                    axis=0,
                )
                hats[comp, part] = block.T[:points]
            start_all(hats, ret, 1, comp)

        def lift(comp):
            bit = lax.broadcasted_iota(jnp.int32, (4 * SUB, LANES), 1) // 8 % 2 == 0
            mine = me // group

            def one(step, carry):
                column = (mine // 2 + step // 2) % 2 * 2 + (mine + step) % 2
                fields_of = []
                for inner in range(group):
                    part = column * group + inner

                    @pl.when(part != me)
                    def _():
                        copy_from(hats, ret, 1, comp, part).wait_recv()

                    @pl.when(part == me)
                    def _():
                        ret[comp, part] = hats[comp, part]

                    value = sent[comp, part] - STEP_DT * ret[comp, part]
                    mid[comp, part] = value
                    fields_of.append(value)
                high, low = split(SIGMA_COEF * jnp.concatenate(fields_of, axis=1))
                both = mm(lift_high[...], high) + (mm(lift_high[...], low) + mm(lift_low[...], high))
                lifted = jnp.where(kinds[column, 0:1] > 0.5, both[4 * SUB :], both[: 4 * SUB])
                for local in range(chunk):
                    even = lifted[:, 2 * local * LANES : (2 * local + 1) * LANES]
                    odd = lifted[:, (2 * local + 1) * LANES : (2 * local + 2) * LANES]
                    at = column * chunk + local
                    pieces[comp, 0, at] = jnp.where(bit, even, pltpu.roll(odd, 8, 1))
                    pieces[comp, 1, at] = jnp.where(bit, pltpu.roll(even, LANES - 8, 1), odd)
                lifted_copy(comp, column, core).start()
                for local in range(chunk):
                    at = column * chunk + local
                    forcing[comp, core * tiles + at] = pieces[comp, core, at]
                return carry

            lax.fori_loop(0, columns, one, 0)

        def solve(comp):
            for column in range(columns):
                lifted_copy(comp, column, 1 - core).wait_recv()
            solve_rows(forcing.at[comp], facts, lam_ref[0:1], weights, state, image, traces.at[comp])
            for end in range(ends):
                trace_copy(comp, end, core).start()
            for at in range(tiles):
                found[comp, core, at] = traces[comp, core * tiles + at]

        def recover(comp):
            bit = lax.broadcasted_iota(jnp.int32, (4 * SUB, LANES), 1) // 8 % 2 == 0
            for column in range(columns):
                if column % (columns // ends) == 0:
                    trace_copy(comp, column // (columns // ends), 1 - core).wait_recv()
                edges = []
                for at in range(column * chunk, (column + 1) * chunk):
                    low_rows = found[comp, 0, at]
                    high_rows = found[comp, 1, at]
                    edges.append(jnp.where(bit, low_rows, pltpu.roll(high_rows, 8, 1)))
                    edges.append(jnp.where(bit, pltpu.roll(low_rows, LANES - 8, 1), high_rows))
                both = mm(recover_all[...], stacked_values(jnp.concatenate(edges, axis=1)))
                node = jnp.where(kinds[column, 0:1] > 0.5, both[88 : 88 + points], both[:points])
                for inner in range(group):
                    part = column * group + inner
                    block = mid[comp, part] * factor[0:1] + node[:, inner * LANES : (inner + 1) * LANES]
                    block = jnp.concatenate([block, jnp.zeros((LANES - points, LANES), F32)], axis=0).T
                    for local in range(per):
                        start = element_at(part, local, group) * points
                        out[comp, :, start : start + points] = block[local * rows : (local + 1) * rows, :points]

        def prepare():
            place_of = iota((4 * SUB, 4 * QUAD), 0)
            place = place_of // SUB * QUAD + place_of % SUB
            widen = ((place == iota((4 * SUB, 4 * QUAD), 1)) & (place_of % SUB < QUAD)).astype(F32)
            place_of = iota((4 * QUAD, 4 * SUB), 1)
            place = place_of // SUB * QUAD + place_of % SUB
            widen_cols = ((place == iota((4 * QUAD, 4 * SUB), 0)) & (place_of % SUB < QUAD)).astype(F32)
            recover_out[...] = jnp.zeros_like(recover_out)
            for which in range(2):
                at = which * 4 * SUB
                mat_ref[at : at + 4 * SUB] = exact(exact(widen, stiff_ref[:, which, :]), widen_cols)
                at = at + 8 * SUB
                mat_ref[at : at + 4 * SUB] = exact(exact(widen, mass_ref[:, which, :]), widen_cols)
                lift_ref[which * 4 * SUB : (which + 1) * 4 * SUB] = exact(widen, lift_in[:, which, :])
                recover_out[which * 88 : which * 88 + points] = exact(widen, recover_in[:, which, :]).T
            weights[...] = stacked_weights(mat_ref[...])
            recover_all[...] = stacked_weights(recover_out[...])
            high, low = split(lift_ref[...])
            lift_high[...] = high
            lift_low[...] = low
            is_second = (kind_ref[...] == 1).astype(F32)
            pad = jnp.zeros((SUB - QUAD, elems), F32)
            free_v = (1 - fixed_ref[:, 0, :]).astype(F32)
            free_h = (1 - fixed_ref[:, 1, :]).astype(F32)
            table = jnp.concatenate(
                [free_v, pad, free_h, pad, is_second, scale_ref[...], jnp.zeros((6, elems), F32)], axis=0
            )
            lane = iota((elems, half), 1)
            element = element_at(lane // LANES * 2 + lane // 8 % 2, lane % LANES // 16, group)
            placed = exact(table, (element == iota((elems, half), 0)).astype(F32))
            for at in range(tiles):
                facts_out[at] = placed[:, at * LANES : (at + 1) * LANES]
                facts[core * tiles + at] = placed[:, at * LANES : (at + 1) * LANES]
            lane = iota((elems, 2 * half), 1)
            element = element_at(lane // LANES, lane % LANES // rows, group)
            spread = (element == iota((elems, 2 * half), 0)).astype(F32)
            placed = exact(jnp.broadcast_to(is_second, (8, elems)), spread)
            width = 2 * half // columns
            for column in range(columns):
                kinds[column] = placed[:, column * width : (column + 1) * width]
            lane = iota((8, LANES), 1)
            lam_ref[...] = lam_of(me * rows + core * 8 + lane % 8)
            factor[...] = SIGMA_COEF / (SIGMA_COEF + lam_of(me * rows + lane % rows))
            geo[...] = jnp.zeros_like(geo)
            for part in range(count):

                @pl.when(me == part)
                def _():
                    for local in range(per):
                        at = element_at(part, local, group) * points
                        geo[local, 0:4, 0:points] = geo_ref[:, at : at + points]

        last = comps - 1
        pack(0)
        pl.semaphore_wait(barrier, count)
        start_all(sent, recv, 0, 0)
        for comp in range(1, comps):
            pack(comp)
            start_all(sent, recv, 0, comp)
        prepare()
        facts_copy().start()
        for comp in range(last):
            arrive_all(comp)
            over_pairs(functools.partial(synthesize, comp))
        for comp in range(last):
            over_pairs(functools.partial(derive, comp))
        arrive_all(last)
        for pair in range(pairs):
            first_advect(pair)
        send_back(0)
        for comp in range(1, last):
            over_pairs(lambda pair, comp=comp: advect(comp, pair, fields[last, pair, :planes]))
            send_back(comp)
        over_pairs(slope_last)
        over_pairs(functools.partial(derive, last))
        over_pairs(lambda pair: advect(last, pair, fields[last, pair, :planes]))
        send_back(last)
        facts_arrive()
        for comp in range(comps):
            lift(comp)
            solve(comp)
            recover(comp)
        facts_copy().wait_send()
        for comp in range(comps):
            for column in range(columns):
                lifted_copy(comp, column, core).wait_send()
            for end in range(ends):
                trace_copy(comp, end, core).wait_send()

            def drain(step, carry):
                peer = peer_at(step)
                copy_to(sent, recv, 0, comp, peer).wait_send()
                copy_to(hats, ret, 1, comp, peer).wait_send()
                return carry

            lax.fori_loop(1, count, drain, 0)

    message = (comps, count, points, LANES)
    operands = (velocity, geometry, kind, scale, dirichlet, stiffness, mass, lift_maps, recover_maps)
    operands = operands + (forward, backward, deriv)
    vmem = pl.BlockSpec(memory_space=pltpu.VMEM)
    copies = comps * (columns + ends) + 1
    return pl.pallas_call(
        kernel,
        in_specs=[vmem] * len(operands),
        out_specs=vmem,
        out_shape=jax.ShapeDtypeStruct(velocity.shape, F32),
        scratch_shapes=[
            pltpu.VMEM(message, F32),
            pltpu.VMEM((columns, 8, group * LANES), F32),
            pltpu.VMEM((8, LANES), F32),
            pltpu.VMEM((2 * 88, 4 * SUB), F32),
        ]
        + [pltpu.VMEM(message, F32)] * 4
        + [
            pltpu.VMEM((pairs, planes, 2 * LANES), F32),
            pltpu.VMEM((pairs, planes, 2 * LANES), F32),
            pltpu.VMEM((comps, pairs, 2 * planes, 2 * LANES), F32),
            pltpu.VMEM((comps, pairs, planes, 2 * LANES), F32),
            pltpu.VMEM((comps, 2, tiles, 4 * SUB, LANES), F32),
            pltpu.VMEM((comps, 2 * tiles, 4 * SUB, LANES), F32),
            pltpu.VMEM((comps, 2 * tiles, 4 * SUB, LANES), F32),
            pltpu.VMEM((comps, 2, tiles, 4 * SUB, LANES), F32),
            pltpu.VMEM((tiles, 40, LANES), F32),
            pltpu.VMEM((2 * tiles, 40, LANES), F32),
            pltpu.VMEM((3, 2, 2 * tiles, SUB, LANES), F32),
            pltpu.VMEM((2, 2 * tiles, SUB, LANES), F32),
            pltpu.VMEM((per, 8, LANES), F32),
            pltpu.VMEM((8 * SUB, points), F32),
            pltpu.VMEM((16 * SUB, 4 * SUB), F32),
            pltpu.VMEM((8, LANES), F32),
            pltpu.VMEM((16 * SUB, 12 * SUB), BF16),
            pltpu.VMEM((8 * SUB, points), BF16),
            pltpu.VMEM((8 * SUB, points), BF16),
            pltpu.VMEM((2 * 88, 12 * SUB), BF16),
        ]
        + [
            pltpu.SemaphoreType.DMA((2, comps, count)),
            pltpu.SemaphoreType.DMA((2, comps, count)),
            pltpu.SemaphoreType.DMA((copies,)),
            pltpu.SemaphoreType.DMA((copies,)),
        ],
        compiler_params=pltpu.CompilerParams(
            vmem_limit_bytes=60 * 1024 * 1024, collective_id=0, has_side_effects=True
        ),
        name="advect_and_solve",
    )(*operands)


def fast_device(
    velocity,
    geometry,
    element_kind,
    element_scale,
    dirichlet,
    schur_stiffness,
    schur_mass,
    lift,
    recover,
):
    count = lax.axis_size("planes")
    return advect_and_solve(
        velocity,
        geometry,
        element_kind[None],
        element_scale[None],
        dirichlet.swapaxes(0, 1),
        schur_stiffness.swapaxes(0, 1),
        schur_mass.swapaxes(0, 1),
        lift.swapaxes(0, 1),
        recover.transpose(2, 0, 1),
        count,
    )


def per_device(velocity, geometry, element_kind, *rest):
    count = lax.axis_size("planes")
    rows = velocity.shape[1]
    elems = element_kind.shape[0]
    fits = count & (count - 1) == 0 and rows == 16 and elems == LANES and elems * rows == count * LANES and lax.axis_size("elem") == 2
    body = fast_device if fits else plain_device
    return body(velocity, geometry, element_kind, *rest)


def solution(mesh):
    in_specs = (
        P(None, "planes", "elem"),
        P(None, "elem"),
        P("elem"),
        P("elem"),
        P(None, None, "elem"),
        P(),
        P(),
        P(),
        P(),
    )
    out_specs = P(None, "planes", "elem")
    return jax.shard_map(
        per_device, mesh=mesh, in_specs=in_specs, out_specs=out_specs, check_vma=False
    )
```

```python
import functools
import math

import jax
import jax.numpy as jnp
import numpy as np
from jax import lax
from jax.experimental import pallas as pl
from jax.experimental.pallas import tpu as pltpu
from jax.sharding import PartitionSpec as P

PLANES = 256
QUAD = 9
COLUMN_ELEMS = 32
CG_STEPS = 4


HIGHEST = lax.Precision.HIGHEST
SIGMA_COEF = 1.0
BETA_COEF = 0.01
STEP_DT = 0.002


def passed_along(value, axis, steps):
    count = lax.axis_size(axis)
    leading, last = (max(0, -steps), min(count, count - steps))
    return lax.ppermute(value, axis, [(source, source + steps) for source in range(leading, last)])


def gauss_derivative(points):
    nodes = -np.cos(np.pi * (2 * np.arange(points) + 1) / (2 * points))
    ident = np.eye(points)
    diffs = nodes[:, None] - nodes[None, :] + ident
    weights = 1.0 / np.prod(diffs, axis=1)
    matrix = weights[None, :] / weights[:, None] / diffs
    matrix = matrix * (1.0 - ident)
    return matrix - ident * matrix.sum(axis=1)[:, None]


def kron_tables():
    deriv = gauss_derivative(QUAD)
    identity = np.eye(QUAD)
    return (
        jnp.asarray(np.kron(deriv, identity), jnp.float32),
        jnp.asarray(np.kron(identity, deriv), jnp.float32),
    )


def fourier_tables(planes):
    zeta = jnp.arange(planes, dtype=jnp.int32)
    rows = jnp.arange(planes, dtype=jnp.int32)
    waves = (rows + 1) // 2
    phase = waves[None, :] * zeta[:, None] % planes
    angle = 2.0 * math.pi / planes * phase.astype(jnp.float32)
    cosine = jnp.cos(angle)
    sine = jnp.sin(angle)
    odd = (rows % 2 == 1)[None, :]
    first = (rows == 0)[None, :]
    last = (rows == planes - 1)[None, :]
    synth = jnp.where(first, 1.0, jnp.where(odd, cosine, sine))
    rate = BETA_COEF * waves.astype(jnp.float32)[None, :]
    slope = jnp.where(first | last, 0.0, jnp.where(odd, -rate * sine, rate * cosine))
    weight = jnp.where((rows == 0) | (rows == planes - 1), 1.0 / planes, 2.0 / planes).astype(
        jnp.float32
    )
    analysis = synth.T * weight[:, None]
    return (synth, slope, analysis)


def inner(first_pair, second_pair):
    return jnp.sum(first_pair[0] * second_pair[0], axis=(0, 2)) + jnp.sum(
        first_pair[1] * second_pair[1], axis=(0, 2)
    )


def global_total(first_pair, second_pair):
    return lax.psum(inner(first_pair, second_pair), "elem")


def global_squares(pair):
    return lax.psum(inner(pair, pair), "elem")


def assemble(outputs, incoming, free):
    left = outputs[:QUAD]
    right = outputs[QUAD : 2 * QUAD]
    bottom = outputs[2 * QUAD : 3 * QUAD]
    top = outputs[3 * QUAD :]
    vertical = left + jnp.concatenate([incoming, right[:, :, :-COLUMN_ELEMS]], axis=2)
    grid = top.reshape(top.shape[0], top.shape[1], -1, COLUMN_ELEMS)
    shifted = jnp.concatenate([jnp.zeros_like(grid[..., :1]), grid[..., :-1]], axis=3).reshape(
        bottom.shape
    )
    horizontal = bottom + shifted
    return (vertical * free[0], horizontal * free[1])


def plain_device(
    velocity,
    geometry,
    element_kind,
    element_scale,
    dirichlet,
    schur_stiffness,
    schur_mass,
    lift,
    recover,
):
    first, second = kron_tables()
    synth, slope, analysis = fourier_tables(PLANES)
    local_rows = velocity.shape[1]
    node_count = velocity.shape[2]
    share = node_count // lax.axis_size("planes")
    geo_part = lax.dynamic_slice_in_dim(geometry, lax.axis_index("planes") * share, share, 1)

    def transform(table, field):
        return jnp.einsum("zr,crm->czm", table, field, precision=HIGHEST)

    items = lax.all_to_all(velocity, "planes", split_axis=2, concat_axis=1, tiled=True)
    values = transform(synth, items)
    along_z = transform(slope, items)
    shaped = values.reshape(values.shape[:-1] + (-1, QUAD * QUAD))
    along_r = jnp.einsum("...en,mn->...em", shaped, first, precision=HIGHEST).reshape(values.shape)
    along_s = jnp.einsum("...en,mn->...em", shaped, second, precision=HIGHEST).reshape(values.shape)
    along_x = geo_part[0] * along_r + geo_part[1] * along_s
    along_y = geo_part[2] * along_r + geo_part[3] * along_s
    values, along_x, along_y, along_z = (values, along_x, along_y, along_z)
    advection = values[0] * along_x + values[1] * along_y + values[2] * along_z
    advection_hat = jnp.einsum("rz,czm->crm", analysis, advection, precision=HIGHEST)
    returned = lax.all_to_all(advection_hat, "planes", split_axis=1, concat_axis=2, tiled=True)
    intermediate = velocity - STEP_DT * returned
    elem_count = element_kind.shape[0]
    row_count = 3 * local_rows
    waves = (
        (lax.axis_index("planes") * local_rows + jnp.arange(local_rows, dtype=jnp.int32) + 1) // 2
    ).astype(jnp.float32)
    lam = jnp.tile(SIGMA_COEF + (BETA_COEF * waves) ** 2, 3)
    free = (1 - dirichlet).astype(jnp.float32)[:, :, None, :]
    chooser = (element_kind == 1).astype(jnp.float32)

    def element_apply(vector, kinds, scales):
        flat = vector.reshape(vector.shape[0], -1)
        results = []
        for kind in range(2):
            stiff = jnp.dot(schur_stiffness[kind], flat, precision=HIGHEST).reshape(vector.shape)
            massed = jnp.dot(schur_mass[kind], flat, precision=HIGHEST).reshape(vector.shape)
            results.append(stiff + lam[None, :, None] * massed)
        return scales[None, None, :] * jnp.where(kinds[None, None, :] > 0.5, results[1], results[0])

    def element_vector(vertical, horizontal):
        arriving = passed_along(vertical[:, :, :COLUMN_ELEMS], "elem", -1)
        right = jnp.concatenate([vertical[:, :, COLUMN_ELEMS:], arriving], axis=2)
        grid = horizontal.reshape(horizontal.shape[0], horizontal.shape[1], -1, COLUMN_ELEMS)
        top = jnp.concatenate([grid[..., 1:], jnp.zeros_like(grid[..., :1])], axis=3).reshape(
            horizontal.shape
        )
        return jnp.concatenate([vertical, right, horizontal, top], axis=0)

    node_values = (SIGMA_COEF * intermediate).reshape(row_count, elem_count, QUAD * QUAD)
    lifted = jnp.where(
        chooser[None, None, :] > 0.5,
        jnp.einsum("kn,ren->kre", lift[1], node_values, precision=HIGHEST),
        jnp.einsum("kn,ren->kre", lift[0], node_values, precision=HIGHEST),
    )
    lifted_right = passed_along(lifted[QUAD : 2 * QUAD, :, -COLUMN_ELEMS:], "elem", 1)
    forcing = assemble(lifted, lifted_right, free)
    trace = (jnp.zeros_like(forcing[0]), jnp.zeros_like(forcing[1]))
    residual = forcing
    direction = forcing
    norm_now = global_squares(residual)
    for sweep in range(CG_STEPS):
        outputs = element_apply(element_vector(direction[0], direction[1]), chooser, element_scale)
        operator_arriving = passed_along(outputs[QUAD : 2 * QUAD, :, -COLUMN_ELEMS:], "elem", 1)
        image = assemble(outputs, operator_arriving, free)
        alpha = (norm_now / global_total(direction, image))[None, :, None]
        trace = (trace[0] + alpha * direction[0], trace[1] + alpha * direction[1])
        residual = (residual[0] - alpha * image[0], residual[1] - alpha * image[1])
        norm_next = global_squares(residual)
        ratio = (norm_next / norm_now)[None, :, None]
        direction = (residual[0] + ratio * direction[0], residual[1] + ratio * direction[1])
        norm_now = norm_next
    vector = element_vector(trace[0], trace[1])
    recovered = jnp.where(
        chooser[None, :, None] > 0.5,
        jnp.einsum("nl,lre->ren", recover[1], vector, precision=HIGHEST),
        jnp.einsum("nl,lre->ren", recover[0], vector, precision=HIGHEST),
    )
    weight = SIGMA_COEF / (SIGMA_COEF + lam)
    result = (
        intermediate.reshape(row_count, elem_count, QUAD * QUAD) * weight[:, None, None] + recovered
    )
    return result.reshape(velocity.shape)


LANES = 128
EDGE = 40
F32 = jnp.float32
BF16 = jnp.bfloat16


def split(value):
    high = value.astype(BF16)
    return high, (value - high.astype(F32)).astype(BF16)


def np_split(value):
    high = np.asarray(value, np.float32).astype(BF16)
    low = (np.asarray(value, np.float64) - high.astype(np.float64)).astype(np.float32).astype(BF16)
    return high, low


def mm(first, second):
    return jnp.dot(first, second, preferred_element_type=F32)


def stacked_values(values):
    high, low = split(values)
    return jnp.concatenate([high, low, high], axis=0)


def advect_tables(planes):
    zeta = np.arange(planes)
    rows = np.arange(planes)
    waves = (rows + 1) // 2
    angle = 2.0 * np.pi / planes * ((waves[None, :] * zeta[:, None]) % planes)
    odd = (rows % 2 == 1)[None, :]
    first = (rows == 0)[None, :]
    last = (rows == planes - 1)[None, :]
    synth = np.where(first, 1.0, np.where(odd, np.cos(angle), np.sin(angle)))
    rate = BETA_COEF * waves[None, :]
    slope = np.where(first | last, 0.0, np.where(odd, -rate * np.sin(angle), rate * np.cos(angle)))
    weight = np.where((rows == 0) | (rows == planes - 1), 1.0 / planes, 2.0 / planes)
    analysis = synth.T * weight[:, None]
    high, low = np_split(np.concatenate([synth, slope], axis=0))
    forward = np.concatenate([high, high, low], axis=1)
    high, low = np_split(analysis)
    backward = np.concatenate([high, high, low], axis=1)
    points = QUAD * QUAD
    deriv = gauss_derivative(QUAD)
    both = np.zeros((LANES, 2 * LANES))
    both[:points, :points] = np.kron(deriv, np.eye(QUAD)).T
    both[:points, LANES : LANES + points] = np.kron(np.eye(QUAD), deriv).T
    high, low = np_split(both)
    return jnp.asarray(forward), jnp.asarray(backward), jnp.asarray(np.concatenate([high, high, low], axis=0))


def whole_spec(shape):
    return pl.BlockSpec(shape, lambda *_: (0,) * len(shape))


def params():
    return pltpu.CompilerParams(vmem_limit_bytes=60 * 1024 * 1024)


def element_at(part, slot, group):
    inner = part % group
    return part // group * COLUMN_ELEMS + slot * group + inner % 2 * (group // 2) + inner // 2


def stacked_weights(weights):
    high, low = split(weights)
    pad = jnp.zeros((weights.shape[0], LANES - 3 * EDGE), BF16)
    return jnp.concatenate([high, high, low, pad], axis=1)


def stacked_edges(value):
    high = value.astype(BF16).astype(F32)
    pad = jnp.zeros((LANES - 3 * EDGE, value.shape[1]), F32)
    return jnp.concatenate([high, value - high, high, pad], axis=0).astype(BF16)


def tree(terms):
    while len(terms) > 1:
        terms = [terms[at] + terms[at + 1] for at in range(0, len(terms), 2)]
    return terms[0]


def solve_rows(forcing, facts, lam, weights, state, image, traces):
    tiles = forcing.shape[0]
    lane = lax.broadcasted_iota(jnp.int32, (8, LANES), 1)
    sub = lax.broadcasted_iota(jnp.int32, (8, LANES), 0)
    top_edge = lane >= LANES - 8
    low_edge = lane < 8
    zero = jnp.zeros((8, LANES), F32)
    lam = jnp.concatenate([lam] * (EDGE // 8), axis=0)

    def above(tile_of, at):
        if at % 2 == 0:
            return tile_of(at + 1)
        return jnp.where(top_edge, 0.0, pltpu.roll(tile_of(at - 1), LANES - 8, 1))

    def below(tile_of, at):
        if at % 2 == 1:
            return tile_of(at - 1)
        return jnp.where(low_edge, 0.0, pltpu.roll(tile_of(at + 1), 8, 1))

    def edges(tile_of, at):
        beside = at + 2 < tiles
        right = tile_of(0, at + 2) if beside else zero
        right_rest = tile_of(2, at + 2) if beside else zero
        top = above(lambda item: tile_of(1, item), at)
        top_rest = above(lambda item: tile_of(2, item), at)
        rest = jnp.where(sub == 0, right_rest, jnp.where(sub == 2, top_rest, 0.0))
        rest = tile_of(2, at) + pltpu.roll(rest, 1, 0)
        return jnp.concatenate([tile_of(0, at), right, tile_of(1, at), top, rest], axis=0)

    def gather(parts, at):
        part = parts[at]
        fact = facts[at]
        left = part[:8]
        rest = below(lambda item: parts[item][32:40], at)
        if at >= 2:
            left = left + parts[at - 2][8:16]
            rest = jnp.where(sub == 1, parts[at - 2][32:40], jnp.where(sub == 3, rest, 0.0))
        else:
            rest = jnp.where(sub == 3, rest, 0.0)
        rest = part[32:40] + pltpu.roll(rest, 7, 0)
        bottom = part[16:24] + below(lambda item: parts[item][24:32], at)
        return left * fact[:8], bottom * fact[8:16], rest * fact[16:24]

    def total(acc):
        acc = tree([acc] + [pltpu.roll(acc, 8 * step, 1) for step in range(1, LANES // 8)])
        return tree([acc] + [pltpu.roll(acc, step, 0) for step in range(1, 8)])

    def apply():
        sums = [zero, zero, zero]
        parts = []
        for first in range(0, tiles, 2):
            both = jnp.concatenate([edges(lambda which, item: state[2, which, item], at) for at in (first, first + 1)], axis=1)
            both = mm(weights[...], stacked_edges(both))
            for at in (first, first + 1):
                lanes = slice((at - first) * LANES, (at - first + 1) * LANES)
                fact = facts[at]
                is_second = jnp.concatenate([fact[24:32]] * (EDGE // 8), axis=0) > 0.5
                scale = jnp.concatenate([fact[32:40]] * (EDGE // 8), axis=0)
                stiff = jnp.where(is_second, both[EDGE : 2 * EDGE, lanes], both[:EDGE, lanes])
                mass = jnp.where(is_second, both[3 * EDGE :, lanes], both[2 * EDGE : 3 * EDGE, lanes])
                parts.append(scale * (stiff + lam * mass))
            for at in (first, first + 1):
                for which, value in enumerate(gather(parts, at)):
                    image[which, at] = value
                    sums[which] = sums[which] + state[2, which, at] * value
        return total(sums[0] + sums[1] + sums[2])

    sums = [zero, zero, zero]
    parts = {}
    for at in range(tiles):
        parts[at] = forcing[at]
    for at in range(tiles):
        for which, value in enumerate(gather(parts, at)):
            state[0, which, at] = zero
            state[1, which, at] = value
            state[2, which, at] = value
            sums[which] = sums[which] + value * value
    now = total(sums[0] + sums[1] + sums[2])

    def sweep(_, now):
        alpha = now / apply()
        sums = [zero, zero, zero]
        for at in range(tiles):
            for which in range(3):
                state[0, which, at] = state[0, which, at] + alpha * state[2, which, at]
                rest = state[1, which, at] - alpha * image[which, at]
                state[1, which, at] = rest
                sums[which] = sums[which] + rest * rest
        fresh = total(sums[0] + sums[1] + sums[2])
        ratio = fresh / now
        for at in range(tiles):
            for which in range(3):
                state[2, which, at] = state[1, which, at] + ratio * state[2, which, at]
        return fresh

    now = lax.fori_loop(0, CG_STEPS - 1, sweep, now)
    alpha = now / apply()
    found = [[state[0, which, at] + alpha * state[2, which, at] for at in range(tiles)] for which in range(3)]
    for at in range(tiles):
        traces[at] = edges(lambda which, item: found[which][item], at)


def exact(first, second):
    return jnp.dot(first, second, precision=HIGHEST, preferred_element_type=F32)


def iota(shape, axis):
    return lax.broadcasted_iota(jnp.int32, shape, axis)


def lam_of(row):
    return SIGMA_COEF + (BETA_COEF * ((row + 1) // 2).astype(F32)) ** 2


def advect_and_solve(velocity, geometry, kind, scale, dirichlet, stiffness, mass, lift_maps, recover_maps, count):
    elems = kind.shape[1]
    comps, rows, nodes = velocity.shape
    points = QUAD * QUAD
    per = LANES // rows
    pairs = per // 2
    planes = count * rows
    half = count * LANES // 2
    forward, backward, deriv = advect_tables(planes)

    group = COLUMN_ELEMS // per
    columns = count // group
    tiles = count // 2
    chunk = tiles // columns
    ends = 2

    def kernel(
        vel_ref, geo_ref, kind_ref, scale_ref, fixed_ref, stiff_ref, mass_ref, lift_in, recover_in,
        forward_ref, backward_ref, deriv_ref,
        out,
        mid, kinds, factor, recover_out, sent, recv, hats, ret,
        store, turned, fields, partial, pieces, forcing, traces, found, facts_out, facts,
        state, image, geo, lift_ref, mat_ref, lam_ref, weights, lift_high, lift_low, recover_all,
        send_sem, recv_sem, pair_send, pair_recv,
    ):
        me = lax.axis_index("planes")
        core = lax.axis_index("elem")
        barrier = pltpu.get_barrier_semaphore()

        def peer_at(step):
            bits = count.bit_length() - 1
            peer = 0
            for bit in range(bits):
                weight = count // 2 // 2**bit
                peer = peer + weight * ((me // weight + step // 2**bit) % 2)
            return peer

        def greet(step, carry):
            pl.semaphore_signal(
                barrier, inc=1, device_id={"planes": peer_at(step)}, device_id_type=pl.DeviceIdType.MESH
            )
            return carry

        lax.fori_loop(1, count, greet, 0)
        pl.semaphore_signal(barrier, inc=1, device_id={"elem": 1 - core}, device_id_type=pl.DeviceIdType.MESH)

        def copy_to(source, target, way, comp, peer):
            return pltpu.make_async_remote_copy(
                src_ref=source.at[comp, peer],
                dst_ref=target.at[comp, me],
                send_sem=send_sem.at[way, comp, peer],
                recv_sem=recv_sem.at[way, comp, me],
                device_id={"planes": peer},
                device_id_type=pl.DeviceIdType.MESH,
            )

        def copy_from(source, target, way, comp, peer):
            return pltpu.make_async_remote_copy(
                src_ref=source.at[comp, peer],
                dst_ref=target.at[comp, peer],
                send_sem=send_sem.at[way, comp, peer],
                recv_sem=recv_sem.at[way, comp, peer],
                device_id={"planes": peer},
                device_id_type=pl.DeviceIdType.MESH,
            )

        def start_all(source, target, way, comp):
            def one(step, carry):
                copy_to(source, target, way, comp, peer_at(step)).start()
                return carry

            lax.fori_loop(1, count, one, 0)

        def follow_all(source, target, way, comp, before):
            def one(step, carry):
                peer = peer_at(step)
                copy_to(source, target, way, before, peer).wait_send()
                copy_to(source, target, way, comp, peer).start()
                return carry

            lax.fori_loop(1, count, one, 0)

        def pair_copy(source, target, at):
            return pltpu.make_async_remote_copy(
                src_ref=source,
                dst_ref=target,
                send_sem=pair_send.at[at],
                recv_sem=pair_recv.at[at],
                device_id={"elem": 1 - core},
                device_id_type=pl.DeviceIdType.MESH,
            )

        def facts_copy():
            return pair_copy(facts_out, facts.at[pl.ds(core * tiles, tiles)], comps * (columns + ends))

        def facts_arrive():
            pair_copy(facts_out, facts.at[pl.ds((1 - core) * tiles, tiles)], comps * (columns + ends)).wait_recv()

        def lifted_copy(comp, column, side):
            return pair_copy(
                pieces.at[comp, 1 - core, pl.ds(column * chunk, chunk)],
                forcing.at[comp, pl.ds(side * tiles + column * chunk, chunk)],
                comp * columns + column,
            )

        def trace_copy(comp, end, side):
            width = tiles // ends
            return pair_copy(
                traces.at[comp, pl.ds((1 - core) * tiles + end * width, width)],
                found.at[comp, side, pl.ds(end * width, width)],
                comps * columns + comp * ends + end,
            )

        def pack(comp):
            for part in range(count):
                rows_of = []
                for local in range(per):
                    at = element_at(part, local, group) * points
                    rows_of.append(vel_ref[comp, :, at : at + points])
                sent[comp, part] = jnp.concatenate(rows_of, axis=0).T

        def arrive(comp, part, block):
            block = jnp.concatenate([block, jnp.zeros((LANES - points, LANES), F32)], axis=0).T
            for local in range(per):
                at = local % 2 * LANES
                store[local // 2, pl.ds(pl.multiple_of(part * rows, rows), rows), at : at + LANES] = block[
                    local * rows : (local + 1) * rows
                ]

        def arrive_all(comp):
            arrive(comp, me, sent[comp, me])

            def one(step, carry):
                part = peer_at(step)
                copy_from(sent, recv, 0, comp, part).wait_recv()
                arrive(comp, part, recv[comp, part])
                return carry

            lax.fori_loop(1, count, one, 0)

        def over_pairs(body):
            def one(pair, carry):
                body(pair)
                return carry

            lax.fori_loop(0, pairs, one, 0)

        def synthesize(comp, pair):
            fields[comp, pair] = mm(forward_ref[...], stacked_values(store[pair]))

        def slope_last(pair):
            fields[comps - 1, pair, planes:] = mm(forward_ref[planes:], stacked_values(store[pair]))

        def derive(comp, pair):
            for which in range(2):
                at = slice(which * LANES, (which + 1) * LANES)
                high, low = split(fields[comp, pair, :planes, at])
                slopes = mm(jnp.concatenate([high, low], axis=1), deriv_ref[: 2 * LANES]) + mm(
                    high, deriv_ref[2 * LANES :]
                )
                part = geo[pair * 2 + which]
                first = fields[0, pair, :planes, at]
                second = fields[1, pair, :planes, at]
                partial[comp, pair, :, at] = slopes[:, :LANES] * (first * part[0:1] + second * part[2:3]) + slopes[
                    :, LANES:
                ] * (first * part[1:2] + second * part[3:4])

        def advect(comp, pair, along):
            result = partial[comp, pair] + along * fields[comp, pair, planes:]
            turned[pair] = mm(backward_ref[...], stacked_values(result))

        def first_advect(pair):
            along = mm(forward_ref[:planes], stacked_values(store[pair]))
            fields[comps - 1, pair, :planes] = along
            advect(0, pair, along)

        def turn_back(comp):
            for part in range(count):
                block = jnp.concatenate(
                    [
                        turned[local // 2, part * rows : (part + 1) * rows, local % 2 * LANES : (local % 2 + 1) * LANES]
                        for local in range(per)
                    ],
                    axis=0,
                )
                hats[comp, part] = block.T[:points]

        def lift(comp):
            bit = lax.broadcasted_iota(jnp.int32, (EDGE, LANES), 1) // 8 % 2 == 0
            mine = me // group

            def one(step, carry):
                column = (mine // 2 + step // 2) % 2 * 2 + (mine + step) % 2
                fields_of = []
                for inner in range(group):
                    part = column * group + inner

                    @pl.when(part != me)
                    def _():
                        copy_from(hats, ret, 1, comp, part).wait_recv()

                    @pl.when(part == me)
                    def _():
                        ret[comp, part] = hats[comp, part]

                    value = sent[comp, part] - STEP_DT * ret[comp, part]
                    mid[comp, part] = value
                    fields_of.append(value)
                high, low = split(SIGMA_COEF * jnp.concatenate(fields_of, axis=1))
                both = mm(lift_high[...], high) + (mm(lift_high[...], low) + mm(lift_low[...], high))
                lifted = jnp.where(kinds[column, 0:1] > 0.5, both[EDGE:], both[:EDGE])
                for local in range(chunk):
                    even = lifted[:, 2 * local * LANES : (2 * local + 1) * LANES]
                    odd = lifted[:, (2 * local + 1) * LANES : (2 * local + 2) * LANES]
                    at = column * chunk + local
                    pieces[comp, 0, at] = jnp.where(bit, even, pltpu.roll(odd, 8, 1))
                    pieces[comp, 1, at] = jnp.where(bit, pltpu.roll(even, LANES - 8, 1), odd)
                lifted_copy(comp, column, core).start()
                for local in range(chunk):
                    at = column * chunk + local
                    forcing[comp, core * tiles + at] = pieces[comp, core, at]
                return carry

            lax.fori_loop(0, columns, one, 0)

        def solve(comp):
            for column in range(columns):
                lifted_copy(comp, column, 1 - core).wait_recv()
            solve_rows(forcing.at[comp], facts, lam_ref[...], weights, state, image, traces.at[comp])
            for end in range(ends):
                trace_copy(comp, end, core).start()
            for at in range(tiles):
                found[comp, core, at] = traces[comp, core * tiles + at]

        def recover(comp):
            bit = lax.broadcasted_iota(jnp.int32, (EDGE, LANES), 1) // 8 % 2 == 0
            for column in range(columns):
                if column % (columns // ends) == 0:
                    trace_copy(comp, column // (columns // ends), 1 - core).wait_recv()
                edges = []
                for at in range(column * chunk, (column + 1) * chunk):
                    low_rows = found[comp, 0, at]
                    high_rows = found[comp, 1, at]
                    edges.append(jnp.where(bit, low_rows, pltpu.roll(high_rows, 8, 1)))
                    edges.append(jnp.where(bit, pltpu.roll(low_rows, LANES - 8, 1), high_rows))
                both = mm(recover_all[...], stacked_edges(jnp.concatenate(edges, axis=1)))
                node = jnp.where(kinds[column, 0:1] > 0.5, both[88 : 88 + points], both[:points])
                for inner in range(group):
                    part = column * group + inner
                    block = mid[comp, part] * factor[0:1] + node[:, inner * LANES : (inner + 1) * LANES]
                    block = jnp.concatenate([block, jnp.zeros((LANES - points, LANES), F32)], axis=0).T
                    for local in range(per):
                        start = element_at(part, local, group) * points
                        out[comp, :, start : start + points] = block[local * rows : (local + 1) * rows, :points]

        def prepare():
            def place(row):
                return jnp.where(row < 32, row // 8 * QUAD + row % 8, (row - 32) * QUAD + 8)

            widen = (place(iota((EDGE, 4 * QUAD), 0)) == iota((EDGE, 4 * QUAD), 1)).astype(F32)
            widen_cols = (place(iota((4 * QUAD, EDGE), 1)) == iota((4 * QUAD, EDGE), 0)).astype(F32)
            recover_out[...] = jnp.zeros_like(recover_out)
            for which in range(2):
                at = which * EDGE
                mat_ref[at : at + EDGE] = exact(exact(widen, stiff_ref[:, which, :]), widen_cols)
                at = at + 2 * EDGE
                mat_ref[at : at + EDGE] = exact(exact(widen, mass_ref[:, which, :]), widen_cols)
                lift_ref[which * EDGE : (which + 1) * EDGE] = exact(widen, lift_in[:, which, :])
                recover_out[which * 88 : which * 88 + points] = exact(widen, recover_in[:, which, :]).T
            weights[...] = stacked_weights(mat_ref[...])
            recover_all[...] = stacked_weights(recover_out[...])
            high, low = split(lift_ref[...])
            lift_high[...] = high
            lift_low[...] = low
            is_second = (kind_ref[...] == 1).astype(F32)
            free_v = (1 - fixed_ref[:, 0, :]).astype(F32)
            free_h = (1 - fixed_ref[:, 1, :]).astype(F32)
            none = jnp.zeros((5, elems), F32)
            rest = [free_v[8:9], none[:1], free_h[8:9], none]
            table = jnp.concatenate([free_v[:8], free_h[:8]] + rest + [is_second] * 8 + [scale_ref[...]] * 8, axis=0)
            lane = iota((elems, half), 1)
            element = element_at(lane // LANES * 2 + lane // 8 % 2, lane % LANES // 16, group)
            placed = exact(table, (element == iota((elems, half), 0)).astype(F32))
            for at in range(tiles):
                facts_out[at] = placed[:, at * LANES : (at + 1) * LANES]
                facts[core * tiles + at] = placed[:, at * LANES : (at + 1) * LANES]
            lane = iota((elems, 2 * half), 1)
            element = element_at(lane // LANES, lane % LANES // rows, group)
            spread = (element == iota((elems, 2 * half), 0)).astype(F32)
            placed = exact(jnp.broadcast_to(is_second, (8, elems)), spread)
            width = 2 * half // columns
            for column in range(columns):
                kinds[column] = placed[:, column * width : (column + 1) * width]
            lane = iota((8, LANES), 1)
            lam_ref[...] = lam_of(me * rows + core * 8 + lane % 8)
            factor[...] = SIGMA_COEF / (SIGMA_COEF + lam_of(me * rows + lane % rows))
            geo[...] = jnp.zeros_like(geo)
            for part in range(count):

                @pl.when(me == part)
                def _():
                    for local in range(per):
                        at = element_at(part, local, group) * points
                        geo[local, 0:4, 0:points] = geo_ref[:, at : at + points]

        last = comps - 1
        pack(0)
        pl.semaphore_wait(barrier, count)
        start_all(sent, recv, 0, 0)
        for comp in range(1, comps):
            pack(comp)
        prepare()
        facts_copy().start()
        for comp in range(last):
            follow_all(sent, recv, 0, comp + 1, comp)
            arrive_all(comp)
            over_pairs(functools.partial(synthesize, comp))
        for comp in range(last):
            over_pairs(functools.partial(derive, comp))
        arrive_all(last)
        for pair in range(pairs):
            first_advect(pair)
        turn_back(0)
        start_all(hats, ret, 1, 0)
        for comp in range(1, last):
            over_pairs(lambda pair, comp=comp: advect(comp, pair, fields[last, pair, :planes]))
            turn_back(comp)
            start_all(hats, ret, 1, comp)
        over_pairs(slope_last)
        over_pairs(functools.partial(derive, last))
        over_pairs(lambda pair: advect(last, pair, fields[last, pair, :planes]))
        turn_back(last)
        follow_all(hats, ret, 1, last, 0)
        facts_arrive()
        for comp in range(comps):
            lift(comp)
            solve(comp)
            recover(comp)
        facts_copy().wait_send()
        for comp in range(comps):
            for column in range(columns):
                lifted_copy(comp, column, core).wait_send()
            for end in range(ends):
                trace_copy(comp, end, core).wait_send()

        def drain(step, carry):
            peer = peer_at(step)
            copy_to(sent, recv, 0, last, peer).wait_send()
            for comp in range(1, comps):
                copy_to(hats, ret, 1, comp, peer).wait_send()
            return carry

        lax.fori_loop(1, count, drain, 0)

    message = (comps, count, points, LANES)
    operands = (velocity, geometry, kind, scale, dirichlet, stiffness, mass, lift_maps, recover_maps)
    operands = operands + (forward, backward, deriv)
    vmem = pl.BlockSpec(memory_space=pltpu.VMEM)
    copies = comps * (columns + ends) + 1
    return pl.pallas_call(
        kernel,
        in_specs=[vmem] * len(operands),
        out_specs=vmem,
        out_shape=jax.ShapeDtypeStruct(velocity.shape, F32),
        scratch_shapes=[
            pltpu.VMEM(message, F32),
            pltpu.VMEM((columns, 8, group * LANES), F32),
            pltpu.VMEM((8, LANES), F32),
            pltpu.VMEM((2 * 88, EDGE), F32),
        ]
        + [pltpu.VMEM(message, F32)] * 4
        + [
            pltpu.VMEM((pairs, planes, 2 * LANES), F32),
            pltpu.VMEM((pairs, planes, 2 * LANES), F32),
            pltpu.VMEM((comps, pairs, 2 * planes, 2 * LANES), F32),
            pltpu.VMEM((comps, pairs, planes, 2 * LANES), F32),
            pltpu.VMEM((comps, 2, tiles, EDGE, LANES), F32),
            pltpu.VMEM((comps, 2 * tiles, EDGE, LANES), F32),
            pltpu.VMEM((comps, 2 * tiles, EDGE, LANES), F32),
            pltpu.VMEM((comps, 2, tiles, EDGE, LANES), F32),
            pltpu.VMEM((tiles, 40, LANES), F32),
            pltpu.VMEM((2 * tiles, 40, LANES), F32),
            pltpu.VMEM((3, 3, 2 * tiles, 8, LANES), F32),
            pltpu.VMEM((3, 2 * tiles, 8, LANES), F32),
            pltpu.VMEM((per, 8, LANES), F32),
            pltpu.VMEM((2 * EDGE, points), F32),
            pltpu.VMEM((4 * EDGE, EDGE), F32),
            pltpu.VMEM((8, LANES), F32),
            pltpu.VMEM((4 * EDGE, LANES), BF16),
            pltpu.VMEM((2 * EDGE, points), BF16),
            pltpu.VMEM((2 * EDGE, points), BF16),
            pltpu.VMEM((2 * 88, LANES), BF16),
        ]
        + [
            pltpu.SemaphoreType.DMA((2, comps, count)),
            pltpu.SemaphoreType.DMA((2, comps, count)),
            pltpu.SemaphoreType.DMA((copies,)),
            pltpu.SemaphoreType.DMA((copies,)),
        ],
        compiler_params=pltpu.CompilerParams(
            vmem_limit_bytes=60 * 1024 * 1024, collective_id=0, has_side_effects=True
        ),
        name="advect_and_solve",
    )(*operands)


def fast_device(
    velocity,
    geometry,
    element_kind,
    element_scale,
    dirichlet,
    schur_stiffness,
    schur_mass,
    lift,
    recover,
):
    count = lax.axis_size("planes")
    return advect_and_solve(
        velocity,
        geometry,
        element_kind[None],
        element_scale[None],
        dirichlet.swapaxes(0, 1),
        schur_stiffness.swapaxes(0, 1),
        schur_mass.swapaxes(0, 1),
        lift.swapaxes(0, 1),
        recover.transpose(2, 0, 1),
        count,
    )


def per_device(velocity, geometry, element_kind, *rest):
    count = lax.axis_size("planes")
    rows = velocity.shape[1]
    elems = element_kind.shape[0]
    fits = count & (count - 1) == 0 and rows == 16 and elems == LANES and elems * rows == count * LANES and lax.axis_size("elem") == 2
    body = fast_device if fits else plain_device
    return body(velocity, geometry, element_kind, *rest)


def solution(mesh):
    in_specs = (
        P(None, "planes", "elem"),
        P(None, "elem"),
        P("elem"),
        P("elem"),
        P(None, None, "elem"),
        P(),
        P(),
        P(),
        P(),
    )
    out_specs = P(None, "planes", "elem")
    return jax.shard_map(
        per_device, mesh=mesh, in_specs=in_specs, out_specs=out_specs, check_vma=False
    )
```

```python
import functools
import math

import jax
import jax.numpy as jnp
import numpy as np
from jax import lax
from jax.experimental import pallas as pl
from jax.experimental.pallas import tpu as pltpu
from jax.sharding import PartitionSpec as P

PLANES = 256
QUAD = 9
COLUMN_ELEMS = 32
CG_STEPS = 4


HIGHEST = lax.Precision.HIGHEST
SIGMA_COEF = 1.0
BETA_COEF = 0.01
STEP_DT = 0.002


def passed_along(value, axis, steps):
    count = lax.axis_size(axis)
    leading, last = (max(0, -steps), min(count, count - steps))
    return lax.ppermute(value, axis, [(source, source + steps) for source in range(leading, last)])


def gauss_derivative(points):
    nodes = -np.cos(np.pi * (2 * np.arange(points) + 1) / (2 * points))
    ident = np.eye(points)
    diffs = nodes[:, None] - nodes[None, :] + ident
    weights = 1.0 / np.prod(diffs, axis=1)
    matrix = weights[None, :] / weights[:, None] / diffs
    matrix = matrix * (1.0 - ident)
    return matrix - ident * matrix.sum(axis=1)[:, None]


def kron_tables():
    deriv = gauss_derivative(QUAD)
    identity = np.eye(QUAD)
    return (
        jnp.asarray(np.kron(deriv, identity), jnp.float32),
        jnp.asarray(np.kron(identity, deriv), jnp.float32),
    )


def fourier_tables(planes):
    zeta = jnp.arange(planes, dtype=jnp.int32)
    rows = jnp.arange(planes, dtype=jnp.int32)
    waves = (rows + 1) // 2
    phase = waves[None, :] * zeta[:, None] % planes
    angle = 2.0 * math.pi / planes * phase.astype(jnp.float32)
    cosine = jnp.cos(angle)
    sine = jnp.sin(angle)
    odd = (rows % 2 == 1)[None, :]
    first = (rows == 0)[None, :]
    last = (rows == planes - 1)[None, :]
    synth = jnp.where(first, 1.0, jnp.where(odd, cosine, sine))
    rate = BETA_COEF * waves.astype(jnp.float32)[None, :]
    slope = jnp.where(first | last, 0.0, jnp.where(odd, -rate * sine, rate * cosine))
    weight = jnp.where((rows == 0) | (rows == planes - 1), 1.0 / planes, 2.0 / planes).astype(
        jnp.float32
    )
    analysis = synth.T * weight[:, None]
    return (synth, slope, analysis)


def inner(first_pair, second_pair):
    return jnp.sum(first_pair[0] * second_pair[0], axis=(0, 2)) + jnp.sum(
        first_pair[1] * second_pair[1], axis=(0, 2)
    )


def global_total(first_pair, second_pair):
    return lax.psum(inner(first_pair, second_pair), "elem")


def global_squares(pair):
    return lax.psum(inner(pair, pair), "elem")


def assemble(outputs, incoming, free):
    left = outputs[:QUAD]
    right = outputs[QUAD : 2 * QUAD]
    bottom = outputs[2 * QUAD : 3 * QUAD]
    top = outputs[3 * QUAD :]
    vertical = left + jnp.concatenate([incoming, right[:, :, :-COLUMN_ELEMS]], axis=2)
    grid = top.reshape(top.shape[0], top.shape[1], -1, COLUMN_ELEMS)
    shifted = jnp.concatenate([jnp.zeros_like(grid[..., :1]), grid[..., :-1]], axis=3).reshape(
        bottom.shape
    )
    horizontal = bottom + shifted
    return (vertical * free[0], horizontal * free[1])


def plain_device(
    velocity,
    geometry,
    element_kind,
    element_scale,
    dirichlet,
    schur_stiffness,
    schur_mass,
    lift,
    recover,
):
    first, second = kron_tables()
    synth, slope, analysis = fourier_tables(PLANES)
    local_rows = velocity.shape[1]
    node_count = velocity.shape[2]
    share = node_count // lax.axis_size("planes")
    geo_part = lax.dynamic_slice_in_dim(geometry, lax.axis_index("planes") * share, share, 1)

    def transform(table, field):
        return jnp.einsum("zr,crm->czm", table, field, precision=HIGHEST)

    items = lax.all_to_all(velocity, "planes", split_axis=2, concat_axis=1, tiled=True)
    values = transform(synth, items)
    along_z = transform(slope, items)
    shaped = values.reshape(values.shape[:-1] + (-1, QUAD * QUAD))
    along_r = jnp.einsum("...en,mn->...em", shaped, first, precision=HIGHEST).reshape(values.shape)
    along_s = jnp.einsum("...en,mn->...em", shaped, second, precision=HIGHEST).reshape(values.shape)
    along_x = geo_part[0] * along_r + geo_part[1] * along_s
    along_y = geo_part[2] * along_r + geo_part[3] * along_s
    values, along_x, along_y, along_z = (values, along_x, along_y, along_z)
    advection = values[0] * along_x + values[1] * along_y + values[2] * along_z
    advection_hat = jnp.einsum("rz,czm->crm", analysis, advection, precision=HIGHEST)
    returned = lax.all_to_all(advection_hat, "planes", split_axis=1, concat_axis=2, tiled=True)
    intermediate = velocity - STEP_DT * returned
    elem_count = element_kind.shape[0]
    row_count = 3 * local_rows
    waves = (
        (lax.axis_index("planes") * local_rows + jnp.arange(local_rows, dtype=jnp.int32) + 1) // 2
    ).astype(jnp.float32)
    lam = jnp.tile(SIGMA_COEF + (BETA_COEF * waves) ** 2, 3)
    free = (1 - dirichlet).astype(jnp.float32)[:, :, None, :]
    chooser = (element_kind == 1).astype(jnp.float32)

    def element_apply(vector, kinds, scales):
        flat = vector.reshape(vector.shape[0], -1)
        results = []
        for kind in range(2):
            stiff = jnp.dot(schur_stiffness[kind], flat, precision=HIGHEST).reshape(vector.shape)
            massed = jnp.dot(schur_mass[kind], flat, precision=HIGHEST).reshape(vector.shape)
            results.append(stiff + lam[None, :, None] * massed)
        return scales[None, None, :] * jnp.where(kinds[None, None, :] > 0.5, results[1], results[0])

    def element_vector(vertical, horizontal):
        arriving = passed_along(vertical[:, :, :COLUMN_ELEMS], "elem", -1)
        right = jnp.concatenate([vertical[:, :, COLUMN_ELEMS:], arriving], axis=2)
        grid = horizontal.reshape(horizontal.shape[0], horizontal.shape[1], -1, COLUMN_ELEMS)
        top = jnp.concatenate([grid[..., 1:], jnp.zeros_like(grid[..., :1])], axis=3).reshape(
            horizontal.shape
        )
        return jnp.concatenate([vertical, right, horizontal, top], axis=0)

    node_values = (SIGMA_COEF * intermediate).reshape(row_count, elem_count, QUAD * QUAD)
    lifted = jnp.where(
        chooser[None, None, :] > 0.5,
        jnp.einsum("kn,ren->kre", lift[1], node_values, precision=HIGHEST),
        jnp.einsum("kn,ren->kre", lift[0], node_values, precision=HIGHEST),
    )
    lifted_right = passed_along(lifted[QUAD : 2 * QUAD, :, -COLUMN_ELEMS:], "elem", 1)
    forcing = assemble(lifted, lifted_right, free)
    trace = (jnp.zeros_like(forcing[0]), jnp.zeros_like(forcing[1]))
    residual = forcing
    direction = forcing
    norm_now = global_squares(residual)
    for sweep in range(CG_STEPS):
        outputs = element_apply(element_vector(direction[0], direction[1]), chooser, element_scale)
        operator_arriving = passed_along(outputs[QUAD : 2 * QUAD, :, -COLUMN_ELEMS:], "elem", 1)
        image = assemble(outputs, operator_arriving, free)
        alpha = (norm_now / global_total(direction, image))[None, :, None]
        trace = (trace[0] + alpha * direction[0], trace[1] + alpha * direction[1])
        residual = (residual[0] - alpha * image[0], residual[1] - alpha * image[1])
        norm_next = global_squares(residual)
        ratio = (norm_next / norm_now)[None, :, None]
        direction = (residual[0] + ratio * direction[0], residual[1] + ratio * direction[1])
        norm_now = norm_next
    vector = element_vector(trace[0], trace[1])
    recovered = jnp.where(
        chooser[None, :, None] > 0.5,
        jnp.einsum("nl,lre->ren", recover[1], vector, precision=HIGHEST),
        jnp.einsum("nl,lre->ren", recover[0], vector, precision=HIGHEST),
    )
    weight = SIGMA_COEF / (SIGMA_COEF + lam)
    result = (
        intermediate.reshape(row_count, elem_count, QUAD * QUAD) * weight[:, None, None] + recovered
    )
    return result.reshape(velocity.shape)


LANES = 128
EDGE = 40
F32 = jnp.float32
BF16 = jnp.bfloat16


def split(value):
    high = value.astype(BF16)
    return high, (value - high.astype(F32)).astype(BF16)


def np_split(value):
    high = np.asarray(value, np.float32).astype(BF16)
    low = (np.asarray(value, np.float64) - high.astype(np.float64)).astype(np.float32).astype(BF16)
    return high, low


def mm(first, second):
    return jnp.dot(first, second, preferred_element_type=F32)


def stacked_values(values):
    high, low = split(values)
    return jnp.concatenate([high, low, high], axis=0)


def advect_tables(planes):
    zeta = np.arange(planes)
    rows = np.arange(planes)
    waves = (rows + 1) // 2
    angle = 2.0 * np.pi / planes * ((waves[None, :] * zeta[:, None]) % planes)
    odd = (rows % 2 == 1)[None, :]
    first = (rows == 0)[None, :]
    last = (rows == planes - 1)[None, :]
    synth = np.where(first, 1.0, np.where(odd, np.cos(angle), np.sin(angle)))
    rate = BETA_COEF * waves[None, :]
    slope = np.where(first | last, 0.0, np.where(odd, -rate * np.sin(angle), rate * np.cos(angle)))
    weight = np.where((rows == 0) | (rows == planes - 1), 1.0 / planes, 2.0 / planes)
    analysis = synth.T * weight[:, None]
    high, low = np_split(np.concatenate([synth, slope], axis=0))
    forward = np.concatenate([high, high, low], axis=1)
    high, low = np_split(analysis)
    backward = np.concatenate([high, high, low], axis=1)
    points = QUAD * QUAD
    deriv = gauss_derivative(QUAD)
    both = np.zeros((LANES, 2 * LANES))
    both[:points, :points] = np.kron(deriv, np.eye(QUAD)).T
    both[:points, LANES : LANES + points] = np.kron(np.eye(QUAD), deriv).T
    high, low = np_split(both)
    return jnp.asarray(forward), jnp.asarray(backward), jnp.asarray(np.concatenate([high, high, low], axis=0))


def whole_spec(shape):
    return pl.BlockSpec(shape, lambda *_: (0,) * len(shape))


def params():
    return pltpu.CompilerParams(vmem_limit_bytes=60 * 1024 * 1024)


def element_at(part, slot, group):
    inner = part % group
    return part // group * COLUMN_ELEMS + slot * group + inner % 2 * (group // 2) + inner // 2


def stacked_weights(weights):
    high, low = split(weights)
    pad = jnp.zeros((weights.shape[0], LANES - 3 * EDGE), BF16)
    return jnp.concatenate([high, high, low, pad], axis=1)


def stacked_edges(value):
    high = value.astype(BF16).astype(F32)
    pad = jnp.zeros((LANES - 3 * EDGE, value.shape[1]), F32)
    return jnp.concatenate([high, value - high, high, pad], axis=0).astype(BF16)


def tree(terms):
    while len(terms) > 1:
        terms = [terms[at] + terms[at + 1] for at in range(0, len(terms), 2)]
    return terms[0]


def solve_rows(forcing, facts, lam, weights, state, image, traces):
    tiles = forcing.shape[0]
    lane = lax.broadcasted_iota(jnp.int32, (8, LANES), 1)
    sub = lax.broadcasted_iota(jnp.int32, (8, LANES), 0)
    top_edge = lane >= LANES - 8
    low_edge = lane < 8
    zero = jnp.zeros((8, LANES), F32)
    lam = jnp.concatenate([lam] * (EDGE // 8), axis=0)

    def above(tile_of, at):
        if at % 2 == 0:
            return tile_of(at + 1)
        return jnp.where(top_edge, 0.0, pltpu.roll(tile_of(at - 1), LANES - 8, 1))

    def below(tile_of, at):
        if at % 2 == 1:
            return tile_of(at - 1)
        return jnp.where(low_edge, 0.0, pltpu.roll(tile_of(at + 1), 8, 1))

    def edges(tile_of, at):
        beside = at + 2 < tiles
        right = tile_of(0, at + 2) if beside else zero
        right_rest = tile_of(2, at + 2) if beside else zero
        top = above(lambda item: tile_of(1, item), at)
        top_rest = above(lambda item: tile_of(2, item), at)
        rest = jnp.where(sub == 0, right_rest, jnp.where(sub == 2, top_rest, 0.0))
        rest = tile_of(2, at) + pltpu.roll(rest, 1, 0)
        return jnp.concatenate([tile_of(0, at), right, tile_of(1, at), top, rest], axis=0)

    def gather(parts, at):
        part = parts[at]
        fact = facts[at]
        left = part[:8]
        rest = below(lambda item: parts[item][32:40], at)
        if at >= 2:
            left = left + parts[at - 2][8:16]
            rest = jnp.where(sub == 1, parts[at - 2][32:40], jnp.where(sub == 3, rest, 0.0))
        else:
            rest = jnp.where(sub == 3, rest, 0.0)
        rest = part[32:40] + pltpu.roll(rest, 7, 0)
        bottom = part[16:24] + below(lambda item: parts[item][24:32], at)
        return left * fact[:8], bottom * fact[8:16], rest * fact[16:24]

    def total(acc):
        acc = tree([acc] + [pltpu.roll(acc, 8 * step, 1) for step in range(1, LANES // 8)])
        return tree([acc] + [pltpu.roll(acc, step, 0) for step in range(1, 8)])

    def apply():
        sums = [zero, zero, zero]
        parts = []
        for first in range(0, tiles, 2):
            both = jnp.concatenate([edges(lambda which, item: state[2, which, item], at) for at in (first, first + 1)], axis=1)
            both = mm(weights[...], stacked_edges(both))
            for at in (first, first + 1):
                lanes = slice((at - first) * LANES, (at - first + 1) * LANES)
                fact = facts[at]
                is_second = jnp.concatenate([fact[24:32]] * (EDGE // 8), axis=0) > 0.5
                scale = jnp.concatenate([fact[32:40]] * (EDGE // 8), axis=0)
                stiff = jnp.where(is_second, both[EDGE : 2 * EDGE, lanes], both[:EDGE, lanes])
                mass = jnp.where(is_second, both[3 * EDGE :, lanes], both[2 * EDGE : 3 * EDGE, lanes])
                parts.append(scale * (stiff + lam * mass))
            for at in (first, first + 1):
                for which, value in enumerate(gather(parts, at)):
                    image[which, at] = value
                    sums[which] = sums[which] + state[2, which, at] * value
        return total(sums[0] + sums[1] + sums[2])

    sums = [zero, zero, zero]
    parts = {}
    for at in range(tiles):
        parts[at] = forcing[at]
    for at in range(tiles):
        for which, value in enumerate(gather(parts, at)):
            state[0, which, at] = zero
            state[1, which, at] = value
            state[2, which, at] = value
            sums[which] = sums[which] + value * value
    now = total(sums[0] + sums[1] + sums[2])

    def sweep(_, now):
        alpha = now / apply()
        sums = [zero, zero, zero]
        for at in range(tiles):
            for which in range(3):
                state[0, which, at] = state[0, which, at] + alpha * state[2, which, at]
                rest = state[1, which, at] - alpha * image[which, at]
                state[1, which, at] = rest
                sums[which] = sums[which] + rest * rest
        fresh = total(sums[0] + sums[1] + sums[2])
        ratio = fresh / now
        for at in range(tiles):
            for which in range(3):
                state[2, which, at] = state[1, which, at] + ratio * state[2, which, at]
        return fresh

    now = lax.fori_loop(0, CG_STEPS - 1, sweep, now)
    alpha = now / apply()
    found = [[state[0, which, at] + alpha * state[2, which, at] for at in range(tiles)] for which in range(3)]
    for at in range(tiles):
        traces[at] = edges(lambda which, item: found[which][item], at)


def exact(first, second):
    return jnp.dot(first, second, precision=HIGHEST, preferred_element_type=F32)


def iota(shape, axis):
    return lax.broadcasted_iota(jnp.int32, shape, axis)


def lam_of(row):
    return SIGMA_COEF + (BETA_COEF * ((row + 1) // 2).astype(F32)) ** 2


def advect_and_solve(velocity, geometry, kind, scale, dirichlet, stiffness, mass, lift_maps, recover_maps, count):
    elems = kind.shape[1]
    comps, rows, nodes = velocity.shape
    points = QUAD * QUAD
    per = LANES // rows
    pairs = per // 2
    planes = count * rows
    half = count * LANES // 2
    forward, backward, deriv = advect_tables(planes)

    group = COLUMN_ELEMS // per
    columns = count // group
    tiles = count // 2
    chunk = tiles // columns
    ends = 2

    def kernel(
        vel_in, geo_ref, kind_ref, scale_ref, fixed_ref, stiff_ref, mass_ref, lift_in, recover_in,
        forward_in, backward_in, deriv_in,
        out,
        vel_ref, forward_ref, backward_ref, deriv_ref, result,
        mid, kinds, factor, recover_out, sent, recv, hats, ret,
        store, turned, fields, partial, pieces, forcing, traces, found, facts_out, facts,
        state, image, geo, lift_ref, mat_ref, lam_ref, weights, lift_high, lift_low, recover_all,
        send_sem, recv_sem, pair_send, pair_recv, load_sem, out_sem,
    ):
        loads = [pltpu.make_async_copy(vel_in.at[comp], vel_ref.at[comp], load_sem.at[comp]) for comp in range(comps)]
        tables = ((forward_in, forward_ref), (deriv_in, deriv_ref), (backward_in, backward_ref))
        for at, (source, target) in enumerate(tables):
            loads.append(pltpu.make_async_copy(source, target, load_sem.at[comps + at]))
        for load in loads:
            load.start()
        me = lax.axis_index("planes")
        core = lax.axis_index("elem")
        barrier = pltpu.get_barrier_semaphore()

        def peer_at(step):
            bits = count.bit_length() - 1
            peer = 0
            for bit in range(bits):
                weight = count // 2 // 2**bit
                peer = peer + weight * ((me // weight + step // 2**bit) % 2)
            return peer

        def greet(step, carry):
            pl.semaphore_signal(
                barrier, inc=1, device_id={"planes": peer_at(step)}, device_id_type=pl.DeviceIdType.MESH
            )
            return carry

        lax.fori_loop(1, count, greet, 0)
        pl.semaphore_signal(barrier, inc=1, device_id={"elem": 1 - core}, device_id_type=pl.DeviceIdType.MESH)

        def copy_to(source, target, way, comp, peer):
            return pltpu.make_async_remote_copy(
                src_ref=source.at[comp, peer],
                dst_ref=target.at[comp, me],
                send_sem=send_sem.at[way, comp, peer],
                recv_sem=recv_sem.at[way, comp, me],
                device_id={"planes": peer},
                device_id_type=pl.DeviceIdType.MESH,
            )

        def copy_from(source, target, way, comp, peer):
            return pltpu.make_async_remote_copy(
                src_ref=source.at[comp, peer],
                dst_ref=target.at[comp, peer],
                send_sem=send_sem.at[way, comp, peer],
                recv_sem=recv_sem.at[way, comp, peer],
                device_id={"planes": peer},
                device_id_type=pl.DeviceIdType.MESH,
            )

        def start_all(source, target, way, comp):
            def one(step, carry):
                copy_to(source, target, way, comp, peer_at(step)).start()
                return carry

            lax.fori_loop(1, count, one, 0)

        def follow_all(source, target, way, comp, before):
            def one(step, carry):
                peer = peer_at(step)
                copy_to(source, target, way, before, peer).wait_send()
                copy_to(source, target, way, comp, peer).start()
                return carry

            lax.fori_loop(1, count, one, 0)

        def pair_copy(source, target, at):
            return pltpu.make_async_remote_copy(
                src_ref=source,
                dst_ref=target,
                send_sem=pair_send.at[at],
                recv_sem=pair_recv.at[at],
                device_id={"elem": 1 - core},
                device_id_type=pl.DeviceIdType.MESH,
            )

        def facts_copy():
            return pair_copy(facts_out, facts.at[pl.ds(core * tiles, tiles)], comps * (columns + ends))

        def facts_arrive():
            pair_copy(facts_out, facts.at[pl.ds((1 - core) * tiles, tiles)], comps * (columns + ends)).wait_recv()

        def lifted_copy(comp, column, side):
            return pair_copy(
                pieces.at[comp, 1 - core, pl.ds(column * chunk, chunk)],
                forcing.at[comp, pl.ds(side * tiles + column * chunk, chunk)],
                comp * columns + column,
            )

        def trace_copy(comp, end, side):
            width = tiles // ends
            return pair_copy(
                traces.at[comp, pl.ds((1 - core) * tiles + end * width, width)],
                found.at[comp, side, pl.ds(end * width, width)],
                comps * columns + comp * ends + end,
            )

        def pack(comp):
            for part in range(count):
                rows_of = []
                for local in range(per):
                    at = element_at(part, local, group) * points
                    rows_of.append(vel_ref[comp, :, at : at + points])
                sent[comp, part] = jnp.concatenate(rows_of, axis=0).T

        def arrive(comp, part, block):
            block = jnp.concatenate([block, jnp.zeros((LANES - points, LANES), F32)], axis=0).T
            for local in range(per):
                at = local % 2 * LANES
                store[local // 2, pl.ds(pl.multiple_of(part * rows, rows), rows), at : at + LANES] = block[
                    local * rows : (local + 1) * rows
                ]

        def arrive_all(comp):
            arrive(comp, me, sent[comp, me])

            def one(step, carry):
                part = peer_at(step)
                copy_from(sent, recv, 0, comp, part).wait_recv()
                arrive(comp, part, recv[comp, part])
                return carry

            lax.fori_loop(1, count, one, 0)

        def over_pairs(body):
            def one(pair, carry):
                body(pair)
                return carry

            lax.fori_loop(0, pairs, one, 0)

        def synthesize(comp, pair):
            fields[comp, pair] = mm(forward_ref[...], stacked_values(store[pair]))

        def slope_last(pair):
            fields[comps - 1, pair, planes:] = mm(forward_ref[planes:], stacked_values(store[pair]))

        def derive(comp, pair):
            for which in range(2):
                at = slice(which * LANES, (which + 1) * LANES)
                high, low = split(fields[comp, pair, :planes, at])
                slopes = mm(jnp.concatenate([high, low], axis=1), deriv_ref[: 2 * LANES]) + mm(
                    high, deriv_ref[2 * LANES :]
                )
                part = geo[pair * 2 + which]
                first = fields[0, pair, :planes, at]
                second = fields[1, pair, :planes, at]
                partial[comp, pair, :, at] = slopes[:, :LANES] * (first * part[0:1] + second * part[2:3]) + slopes[
                    :, LANES:
                ] * (first * part[1:2] + second * part[3:4])

        def advect(comp, pair, along):
            result = partial[comp, pair] + along * fields[comp, pair, planes:]
            turned[pair] = mm(backward_ref[...], stacked_values(result))

        def first_advect(pair):
            along = mm(forward_ref[:planes], stacked_values(store[pair]))
            fields[comps - 1, pair, :planes] = along
            advect(0, pair, along)

        def turn_back(comp):
            for part in range(count):
                block = jnp.concatenate(
                    [
                        turned[local // 2, part * rows : (part + 1) * rows, local % 2 * LANES : (local % 2 + 1) * LANES]
                        for local in range(per)
                    ],
                    axis=0,
                )
                hats[comp, part] = block.T[:points]

        def lift(comp):
            bit = lax.broadcasted_iota(jnp.int32, (EDGE, LANES), 1) // 8 % 2 == 0
            mine = me // group

            def one(step, carry):
                column = (mine // 2 + step // 2) % 2 * 2 + (mine + step) % 2
                fields_of = []
                for inner in range(group):
                    part = column * group + inner

                    @pl.when(part != me)
                    def _():
                        copy_from(hats, ret, 1, comp, part).wait_recv()

                    @pl.when(part == me)
                    def _():
                        ret[comp, part] = hats[comp, part]

                    value = sent[comp, part] - STEP_DT * ret[comp, part]
                    mid[comp, part] = value
                    fields_of.append(value)
                high, low = split(SIGMA_COEF * jnp.concatenate(fields_of, axis=1))
                both = mm(lift_high[...], high) + (mm(lift_high[...], low) + mm(lift_low[...], high))
                lifted = jnp.where(kinds[column, 0:1] > 0.5, both[EDGE:], both[:EDGE])
                for local in range(chunk):
                    even = lifted[:, 2 * local * LANES : (2 * local + 1) * LANES]
                    odd = lifted[:, (2 * local + 1) * LANES : (2 * local + 2) * LANES]
                    at = column * chunk + local
                    pieces[comp, 0, at] = jnp.where(bit, even, pltpu.roll(odd, 8, 1))
                    pieces[comp, 1, at] = jnp.where(bit, pltpu.roll(even, LANES - 8, 1), odd)
                lifted_copy(comp, column, core).start()
                for local in range(chunk):
                    at = column * chunk + local
                    forcing[comp, core * tiles + at] = pieces[comp, core, at]
                return carry

            lax.fori_loop(0, columns, one, 0)

        def solve(comp):
            for column in range(columns):
                lifted_copy(comp, column, 1 - core).wait_recv()
            solve_rows(forcing.at[comp], facts, lam_ref[...], weights, state, image, traces.at[comp])
            for end in range(ends):
                trace_copy(comp, end, core).start()
            for at in range(tiles):
                found[comp, core, at] = traces[comp, core * tiles + at]

        def leave(comp, end):
            cut = nodes // 2 // LANES * LANES
            lanes = pl.ds(end * cut, (cut, nodes - cut)[end])
            return pltpu.make_async_copy(result.at[comp, :, lanes], out.at[comp, :, lanes], out_sem.at[comp, end])

        def recover(comp):
            bit = lax.broadcasted_iota(jnp.int32, (EDGE, LANES), 1) // 8 % 2 == 0
            for column in range(columns):
                if column == columns // 2:
                    leave(comp, 0).start()
                if column % (columns // ends) == 0:
                    trace_copy(comp, column // (columns // ends), 1 - core).wait_recv()
                edges = []
                for at in range(column * chunk, (column + 1) * chunk):
                    low_rows = found[comp, 0, at]
                    high_rows = found[comp, 1, at]
                    edges.append(jnp.where(bit, low_rows, pltpu.roll(high_rows, 8, 1)))
                    edges.append(jnp.where(bit, pltpu.roll(low_rows, LANES - 8, 1), high_rows))
                both = mm(recover_all[...], stacked_edges(jnp.concatenate(edges, axis=1)))
                node = jnp.where(kinds[column, 0:1] > 0.5, both[88 : 88 + points], both[:points])
                for inner in range(group):
                    part = column * group + inner
                    block = mid[comp, part] * factor[0:1] + node[:, inner * LANES : (inner + 1) * LANES]
                    block = jnp.concatenate([block, jnp.zeros((LANES - points, LANES), F32)], axis=0).T
                    for local in range(per):
                        start = element_at(part, local, group) * points
                        result[comp, :, start : start + points] = block[local * rows : (local + 1) * rows, :points]
            leave(comp, 1).start()

        def prepare():
            def place(row):
                return jnp.where(row < 32, row // 8 * QUAD + row % 8, (row - 32) * QUAD + 8)

            widen = (place(iota((EDGE, 4 * QUAD), 0)) == iota((EDGE, 4 * QUAD), 1)).astype(F32)
            widen_cols = (place(iota((4 * QUAD, EDGE), 1)) == iota((4 * QUAD, EDGE), 0)).astype(F32)
            recover_out[...] = jnp.zeros_like(recover_out)
            for which in range(2):
                at = which * EDGE
                mat_ref[at : at + EDGE] = exact(exact(widen, stiff_ref[:, which, :]), widen_cols)
                at = at + 2 * EDGE
                mat_ref[at : at + EDGE] = exact(exact(widen, mass_ref[:, which, :]), widen_cols)
                lift_ref[which * EDGE : (which + 1) * EDGE] = exact(widen, lift_in[:, which, :])
                recover_out[which * 88 : which * 88 + points] = exact(widen, recover_in[:, which, :]).T
            weights[...] = stacked_weights(mat_ref[...])
            recover_all[...] = stacked_weights(recover_out[...])
            high, low = split(lift_ref[...])
            lift_high[...] = high
            lift_low[...] = low
            is_second = (kind_ref[...] == 1).astype(F32)
            free_v = (1 - fixed_ref[:, 0, :]).astype(F32)
            free_h = (1 - fixed_ref[:, 1, :]).astype(F32)
            none = jnp.zeros((5, elems), F32)
            rest = [free_v[8:9], none[:1], free_h[8:9], none]
            table = jnp.concatenate([free_v[:8], free_h[:8]] + rest + [is_second] * 8 + [scale_ref[...]] * 8, axis=0)
            lane = iota((elems, half), 1)
            element = element_at(lane // LANES * 2 + lane // 8 % 2, lane % LANES // 16, group)
            placed = exact(table, (element == iota((elems, half), 0)).astype(F32))
            for at in range(tiles):
                facts_out[at] = placed[:, at * LANES : (at + 1) * LANES]
                facts[core * tiles + at] = placed[:, at * LANES : (at + 1) * LANES]
            lane = iota((elems, 2 * half), 1)
            element = element_at(lane // LANES, lane % LANES // rows, group)
            spread = (element == iota((elems, 2 * half), 0)).astype(F32)
            placed = exact(jnp.broadcast_to(is_second, (8, elems)), spread)
            width = 2 * half // columns
            for column in range(columns):
                kinds[column] = placed[:, column * width : (column + 1) * width]
            lane = iota((8, LANES), 1)
            lam_ref[...] = lam_of(me * rows + core * 8 + lane % 8)
            factor[...] = SIGMA_COEF / (SIGMA_COEF + lam_of(me * rows + lane % rows))
            geo[...] = jnp.zeros_like(geo)
            for part in range(count):

                @pl.when(me == part)
                def _():
                    for local in range(per):
                        at = element_at(part, local, group) * points
                        geo[local, 0:4, 0:points] = geo_ref[:, at : at + points]

        last = comps - 1
        loads[0].wait()
        pack(0)
        pl.semaphore_wait(barrier, count)
        start_all(sent, recv, 0, 0)
        for comp in range(1, comps):
            loads[comp].wait()
            pack(comp)
        prepare()
        facts_copy().start()
        for load in loads[comps:]:
            load.wait()
        for comp in range(last):
            follow_all(sent, recv, 0, comp + 1, comp)
            arrive_all(comp)
            over_pairs(functools.partial(synthesize, comp))
        for comp in range(last):
            over_pairs(functools.partial(derive, comp))
        arrive_all(last)
        for pair in range(pairs):
            first_advect(pair)
        turn_back(0)
        start_all(hats, ret, 1, 0)
        for comp in range(1, last):
            over_pairs(lambda pair, comp=comp: advect(comp, pair, fields[last, pair, :planes]))
            turn_back(comp)
            start_all(hats, ret, 1, comp)
        over_pairs(slope_last)
        over_pairs(functools.partial(derive, last))
        over_pairs(lambda pair: advect(last, pair, fields[last, pair, :planes]))
        turn_back(last)
        follow_all(hats, ret, 1, last, 0)
        facts_arrive()
        for comp in range(comps):
            lift(comp)
            solve(comp)
            recover(comp)
        facts_copy().wait_send()
        for comp in range(comps):
            for column in range(columns):
                lifted_copy(comp, column, core).wait_send()
            for end in range(ends):
                trace_copy(comp, end, core).wait_send()

        def drain(step, carry):
            peer = peer_at(step)
            copy_to(sent, recv, 0, last, peer).wait_send()
            for comp in range(1, comps):
                copy_to(hats, ret, 1, comp, peer).wait_send()
            return carry

        lax.fori_loop(1, count, drain, 0)
        for comp in range(comps):
            for end in range(2):
                leave(comp, end).wait()

    message = (comps, count, points, LANES)
    operands = (velocity, geometry, kind, scale, dirichlet, stiffness, mass, lift_maps, recover_maps)
    operands = operands + (forward, backward, deriv)
    vmem = pl.BlockSpec(memory_space=pltpu.VMEM)
    anywhere = pl.BlockSpec(memory_space=pl.ANY)
    copies = comps * (columns + ends) + 1
    return pl.pallas_call(
        kernel,
        in_specs=[anywhere] + [vmem] * 8 + [anywhere] * 3,
        out_specs=anywhere,
        out_shape=jax.ShapeDtypeStruct(velocity.shape, F32),
        scratch_shapes=[
            pltpu.VMEM(velocity.shape, F32),
            pltpu.VMEM(forward.shape, BF16),
            pltpu.VMEM(backward.shape, BF16),
            pltpu.VMEM(deriv.shape, BF16),
            pltpu.VMEM(velocity.shape, F32),
            pltpu.VMEM(message, F32),
            pltpu.VMEM((columns, 8, group * LANES), F32),
            pltpu.VMEM((8, LANES), F32),
            pltpu.VMEM((2 * 88, EDGE), F32),
        ]
        + [pltpu.VMEM(message, F32)] * 4
        + [
            pltpu.VMEM((pairs, planes, 2 * LANES), F32),
            pltpu.VMEM((pairs, planes, 2 * LANES), F32),
            pltpu.VMEM((comps, pairs, 2 * planes, 2 * LANES), F32),
            pltpu.VMEM((comps, pairs, planes, 2 * LANES), F32),
            pltpu.VMEM((comps, 2, tiles, EDGE, LANES), F32),
            pltpu.VMEM((comps, 2 * tiles, EDGE, LANES), F32),
            pltpu.VMEM((comps, 2 * tiles, EDGE, LANES), F32),
            pltpu.VMEM((comps, 2, tiles, EDGE, LANES), F32),
            pltpu.VMEM((tiles, 40, LANES), F32),
            pltpu.VMEM((2 * tiles, 40, LANES), F32),
            pltpu.VMEM((3, 3, 2 * tiles, 8, LANES), F32),
            pltpu.VMEM((3, 2 * tiles, 8, LANES), F32),
            pltpu.VMEM((per, 8, LANES), F32),
            pltpu.VMEM((2 * EDGE, points), F32),
            pltpu.VMEM((4 * EDGE, EDGE), F32),
            pltpu.VMEM((8, LANES), F32),
            pltpu.VMEM((4 * EDGE, LANES), BF16),
            pltpu.VMEM((2 * EDGE, points), BF16),
            pltpu.VMEM((2 * EDGE, points), BF16),
            pltpu.VMEM((2 * 88, LANES), BF16),
        ]
        + [
            pltpu.SemaphoreType.DMA((2, comps, count)),
            pltpu.SemaphoreType.DMA((2, comps, count)),
            pltpu.SemaphoreType.DMA((copies,)),
            pltpu.SemaphoreType.DMA((copies,)),
            pltpu.SemaphoreType.DMA((comps + 3,)),
            pltpu.SemaphoreType.DMA((comps, 2)),
        ],
        compiler_params=pltpu.CompilerParams(
            vmem_limit_bytes=60 * 1024 * 1024, collective_id=0, has_side_effects=True
        ),
        name="advect_and_solve",
    )(*operands)


def fast_device(
    velocity,
    geometry,
    element_kind,
    element_scale,
    dirichlet,
    schur_stiffness,
    schur_mass,
    lift,
    recover,
):
    count = lax.axis_size("planes")
    return advect_and_solve(
        velocity,
        geometry,
        element_kind[None],
        element_scale[None],
        dirichlet.swapaxes(0, 1),
        schur_stiffness.swapaxes(0, 1),
        schur_mass.swapaxes(0, 1),
        lift.swapaxes(0, 1),
        recover.transpose(2, 0, 1),
        count,
    )


def per_device(velocity, geometry, element_kind, *rest):
    count = lax.axis_size("planes")
    rows = velocity.shape[1]
    elems = element_kind.shape[0]
    fits = count & (count - 1) == 0 and rows == 16 and elems == LANES and elems * rows == count * LANES and lax.axis_size("elem") == 2
    body = fast_device if fits else plain_device
    return body(velocity, geometry, element_kind, *rest)


def solution(mesh):
    in_specs = (
        P(None, "planes", "elem"),
        P(None, "elem"),
        P("elem"),
        P("elem"),
        P(None, None, "elem"),
        P(),
        P(),
        P(),
        P(),
    )
    out_specs = P(None, "planes", "elem")
    return jax.shard_map(
        per_device, mesh=mesh, in_specs=in_specs, out_specs=out_specs, check_vma=False
    )
```

```python
import functools
import math

import jax
import jax.numpy as jnp
import numpy as np
from jax import lax
from jax.experimental import pallas as pl
from jax.experimental.pallas import tpu as pltpu
from jax.sharding import PartitionSpec as P

PLANES = 256
QUAD = 9
COLUMN_ELEMS = 32
CG_STEPS = 4


HIGHEST = lax.Precision.HIGHEST
SIGMA_COEF = 1.0
BETA_COEF = 0.01
STEP_DT = 0.002


def passed_along(value, axis, steps):
    count = lax.axis_size(axis)
    leading, last = (max(0, -steps), min(count, count - steps))
    return lax.ppermute(value, axis, [(source, source + steps) for source in range(leading, last)])


def gauss_derivative(points):
    nodes = -np.cos(np.pi * (2 * np.arange(points) + 1) / (2 * points))
    ident = np.eye(points)
    diffs = nodes[:, None] - nodes[None, :] + ident
    weights = 1.0 / np.prod(diffs, axis=1)
    matrix = weights[None, :] / weights[:, None] / diffs
    matrix = matrix * (1.0 - ident)
    return matrix - ident * matrix.sum(axis=1)[:, None]


def kron_tables():
    deriv = gauss_derivative(QUAD)
    identity = np.eye(QUAD)
    return (
        jnp.asarray(np.kron(deriv, identity), jnp.float32),
        jnp.asarray(np.kron(identity, deriv), jnp.float32),
    )


def fourier_tables(planes):
    zeta = jnp.arange(planes, dtype=jnp.int32)
    rows = jnp.arange(planes, dtype=jnp.int32)
    waves = (rows + 1) // 2
    phase = waves[None, :] * zeta[:, None] % planes
    angle = 2.0 * math.pi / planes * phase.astype(jnp.float32)
    cosine = jnp.cos(angle)
    sine = jnp.sin(angle)
    odd = (rows % 2 == 1)[None, :]
    first = (rows == 0)[None, :]
    last = (rows == planes - 1)[None, :]
    synth = jnp.where(first, 1.0, jnp.where(odd, cosine, sine))
    rate = BETA_COEF * waves.astype(jnp.float32)[None, :]
    slope = jnp.where(first | last, 0.0, jnp.where(odd, -rate * sine, rate * cosine))
    weight = jnp.where((rows == 0) | (rows == planes - 1), 1.0 / planes, 2.0 / planes).astype(
        jnp.float32
    )
    analysis = synth.T * weight[:, None]
    return (synth, slope, analysis)


def inner(first_pair, second_pair):
    return jnp.sum(first_pair[0] * second_pair[0], axis=(0, 2)) + jnp.sum(
        first_pair[1] * second_pair[1], axis=(0, 2)
    )


def global_total(first_pair, second_pair):
    return lax.psum(inner(first_pair, second_pair), "elem")


def global_squares(pair):
    return lax.psum(inner(pair, pair), "elem")


def assemble(outputs, incoming, free):
    left = outputs[:QUAD]
    right = outputs[QUAD : 2 * QUAD]
    bottom = outputs[2 * QUAD : 3 * QUAD]
    top = outputs[3 * QUAD :]
    vertical = left + jnp.concatenate([incoming, right[:, :, :-COLUMN_ELEMS]], axis=2)
    grid = top.reshape(top.shape[0], top.shape[1], -1, COLUMN_ELEMS)
    shifted = jnp.concatenate([jnp.zeros_like(grid[..., :1]), grid[..., :-1]], axis=3).reshape(
        bottom.shape
    )
    horizontal = bottom + shifted
    return (vertical * free[0], horizontal * free[1])


def plain_device(
    velocity,
    geometry,
    element_kind,
    element_scale,
    dirichlet,
    schur_stiffness,
    schur_mass,
    lift,
    recover,
):
    first, second = kron_tables()
    synth, slope, analysis = fourier_tables(PLANES)
    local_rows = velocity.shape[1]
    node_count = velocity.shape[2]
    share = node_count // lax.axis_size("planes")
    geo_part = lax.dynamic_slice_in_dim(geometry, lax.axis_index("planes") * share, share, 1)

    def transform(table, field):
        return jnp.einsum("zr,crm->czm", table, field, precision=HIGHEST)

    items = lax.all_to_all(velocity, "planes", split_axis=2, concat_axis=1, tiled=True)
    values = transform(synth, items)
    along_z = transform(slope, items)
    shaped = values.reshape(values.shape[:-1] + (-1, QUAD * QUAD))
    along_r = jnp.einsum("...en,mn->...em", shaped, first, precision=HIGHEST).reshape(values.shape)
    along_s = jnp.einsum("...en,mn->...em", shaped, second, precision=HIGHEST).reshape(values.shape)
    along_x = geo_part[0] * along_r + geo_part[1] * along_s
    along_y = geo_part[2] * along_r + geo_part[3] * along_s
    values, along_x, along_y, along_z = (values, along_x, along_y, along_z)
    advection = values[0] * along_x + values[1] * along_y + values[2] * along_z
    advection_hat = jnp.einsum("rz,czm->crm", analysis, advection, precision=HIGHEST)
    returned = lax.all_to_all(advection_hat, "planes", split_axis=1, concat_axis=2, tiled=True)
    intermediate = velocity - STEP_DT * returned
    elem_count = element_kind.shape[0]
    row_count = 3 * local_rows
    waves = (
        (lax.axis_index("planes") * local_rows + jnp.arange(local_rows, dtype=jnp.int32) + 1) // 2
    ).astype(jnp.float32)
    lam = jnp.tile(SIGMA_COEF + (BETA_COEF * waves) ** 2, 3)
    free = (1 - dirichlet).astype(jnp.float32)[:, :, None, :]
    chooser = (element_kind == 1).astype(jnp.float32)

    def element_apply(vector, kinds, scales):
        flat = vector.reshape(vector.shape[0], -1)
        results = []
        for kind in range(2):
            stiff = jnp.dot(schur_stiffness[kind], flat, precision=HIGHEST).reshape(vector.shape)
            massed = jnp.dot(schur_mass[kind], flat, precision=HIGHEST).reshape(vector.shape)
            results.append(stiff + lam[None, :, None] * massed)
        return scales[None, None, :] * jnp.where(kinds[None, None, :] > 0.5, results[1], results[0])

    def element_vector(vertical, horizontal):
        arriving = passed_along(vertical[:, :, :COLUMN_ELEMS], "elem", -1)
        right = jnp.concatenate([vertical[:, :, COLUMN_ELEMS:], arriving], axis=2)
        grid = horizontal.reshape(horizontal.shape[0], horizontal.shape[1], -1, COLUMN_ELEMS)
        top = jnp.concatenate([grid[..., 1:], jnp.zeros_like(grid[..., :1])], axis=3).reshape(
            horizontal.shape
        )
        return jnp.concatenate([vertical, right, horizontal, top], axis=0)

    node_values = (SIGMA_COEF * intermediate).reshape(row_count, elem_count, QUAD * QUAD)
    lifted = jnp.where(
        chooser[None, None, :] > 0.5,
        jnp.einsum("kn,ren->kre", lift[1], node_values, precision=HIGHEST),
        jnp.einsum("kn,ren->kre", lift[0], node_values, precision=HIGHEST),
    )
    lifted_right = passed_along(lifted[QUAD : 2 * QUAD, :, -COLUMN_ELEMS:], "elem", 1)
    forcing = assemble(lifted, lifted_right, free)
    trace = (jnp.zeros_like(forcing[0]), jnp.zeros_like(forcing[1]))
    residual = forcing
    direction = forcing
    norm_now = global_squares(residual)
    for sweep in range(CG_STEPS):
        outputs = element_apply(element_vector(direction[0], direction[1]), chooser, element_scale)
        operator_arriving = passed_along(outputs[QUAD : 2 * QUAD, :, -COLUMN_ELEMS:], "elem", 1)
        image = assemble(outputs, operator_arriving, free)
        alpha = (norm_now / global_total(direction, image))[None, :, None]
        trace = (trace[0] + alpha * direction[0], trace[1] + alpha * direction[1])
        residual = (residual[0] - alpha * image[0], residual[1] - alpha * image[1])
        norm_next = global_squares(residual)
        ratio = (norm_next / norm_now)[None, :, None]
        direction = (residual[0] + ratio * direction[0], residual[1] + ratio * direction[1])
        norm_now = norm_next
    vector = element_vector(trace[0], trace[1])
    recovered = jnp.where(
        chooser[None, :, None] > 0.5,
        jnp.einsum("nl,lre->ren", recover[1], vector, precision=HIGHEST),
        jnp.einsum("nl,lre->ren", recover[0], vector, precision=HIGHEST),
    )
    weight = SIGMA_COEF / (SIGMA_COEF + lam)
    result = (
        intermediate.reshape(row_count, elem_count, QUAD * QUAD) * weight[:, None, None] + recovered
    )
    return result.reshape(velocity.shape)


LANES = 128
EDGE = 40
F32 = jnp.float32
BF16 = jnp.bfloat16


def split(value):
    high = value.astype(BF16)
    return high, (value - high.astype(F32)).astype(BF16)


def np_split(value):
    high = np.asarray(value, np.float32).astype(BF16)
    low = (np.asarray(value, np.float64) - high.astype(np.float64)).astype(np.float32).astype(BF16)
    return high, low


def mm(first, second):
    return jnp.dot(first, second, preferred_element_type=F32)


def stacked_values(values):
    high, low = split(values)
    return jnp.concatenate([high, low, high], axis=0)


def advect_tables(planes):
    zeta = np.arange(planes)
    rows = np.arange(planes)
    waves = (rows + 1) // 2
    angle = 2.0 * np.pi / planes * ((waves[None, :] * zeta[:, None]) % planes)
    odd = (rows % 2 == 1)[None, :]
    first = (rows == 0)[None, :]
    last = (rows == planes - 1)[None, :]
    synth = np.where(first, 1.0, np.where(odd, np.cos(angle), np.sin(angle)))
    rate = BETA_COEF * waves[None, :]
    slope = np.where(first | last, 0.0, np.where(odd, -rate * np.sin(angle), rate * np.cos(angle)))
    weight = np.where((rows == 0) | (rows == planes - 1), 1.0 / planes, 2.0 / planes)
    analysis = synth.T * weight[:, None]
    high, low = np_split(np.concatenate([synth, slope], axis=0))
    forward = np.concatenate([high, high, low], axis=1)
    high, low = np_split(analysis)
    backward = np.concatenate([high, high, low], axis=1)
    points = QUAD * QUAD
    deriv = gauss_derivative(QUAD)
    both = np.zeros((LANES, 2 * LANES))
    both[:points, :points] = np.kron(deriv, np.eye(QUAD)).T
    both[:points, LANES : LANES + points] = np.kron(np.eye(QUAD), deriv).T
    high, low = np_split(both)
    return jnp.asarray(forward), jnp.asarray(backward), jnp.asarray(np.concatenate([high, high, low], axis=0))


def whole_spec(shape):
    return pl.BlockSpec(shape, lambda *_: (0,) * len(shape))


def params():
    return pltpu.CompilerParams(vmem_limit_bytes=60 * 1024 * 1024)


def element_at(part, slot, group):
    inner = part % group
    return part // group * COLUMN_ELEMS + slot * group + inner % 2 * (group // 2) + inner // 2


def stacked_weights(weights):
    high, low = split(weights)
    pad = jnp.zeros((weights.shape[0], LANES - 3 * EDGE), BF16)
    return jnp.concatenate([high, high, low, pad], axis=1)


def stacked_edges(value):
    high = value.astype(BF16).astype(F32)
    pad = jnp.zeros((LANES - 3 * EDGE, value.shape[1]), F32)
    return jnp.concatenate([high, value - high, high, pad], axis=0).astype(BF16)


def tree(terms):
    while len(terms) > 1:
        terms = [terms[at] + terms[at + 1] for at in range(0, len(terms), 2)]
    return terms[0]


def solve_rows(forcing, facts, lam, weights, state, image, traces):
    tiles = forcing.shape[0]
    lane = lax.broadcasted_iota(jnp.int32, (8, LANES), 1)
    sub = lax.broadcasted_iota(jnp.int32, (8, LANES), 0)
    top_edge = lane >= LANES - 8
    low_edge = lane < 8
    zero = jnp.zeros((8, LANES), F32)
    lam = jnp.concatenate([lam] * (EDGE // 8), axis=0)

    def above(tile_of, at):
        if at % 2 == 0:
            return tile_of(at + 1)
        return jnp.where(top_edge, 0.0, pltpu.roll(tile_of(at - 1), LANES - 8, 1))

    def below(tile_of, at):
        if at % 2 == 1:
            return tile_of(at - 1)
        return jnp.where(low_edge, 0.0, pltpu.roll(tile_of(at + 1), 8, 1))

    def edges(tile_of, at):
        beside = at + 2 < tiles
        right = tile_of(0, at + 2) if beside else zero
        right_rest = tile_of(2, at + 2) if beside else zero
        top = above(lambda item: tile_of(1, item), at)
        top_rest = above(lambda item: tile_of(2, item), at)
        rest = jnp.where(sub == 0, right_rest, jnp.where(sub == 2, top_rest, 0.0))
        rest = tile_of(2, at) + pltpu.roll(rest, 1, 0)
        return jnp.concatenate([tile_of(0, at), right, tile_of(1, at), top, rest], axis=0)

    def gather(parts, at):
        part = parts[at]
        fact = facts[at]
        left = part[:8]
        rest = below(lambda item: parts[item][32:40], at)
        if at >= 2:
            left = left + parts[at - 2][8:16]
            rest = jnp.where(sub == 1, parts[at - 2][32:40], jnp.where(sub == 3, rest, 0.0))
        else:
            rest = jnp.where(sub == 3, rest, 0.0)
        rest = part[32:40] + pltpu.roll(rest, 7, 0)
        bottom = part[16:24] + below(lambda item: parts[item][24:32], at)
        return left * fact[:8], bottom * fact[8:16], rest * fact[16:24]

    def total(acc):
        acc = tree([acc] + [pltpu.roll(acc, 8 * step, 1) for step in range(1, LANES // 8)])
        return tree([acc] + [pltpu.roll(acc, step, 0) for step in range(1, 8)])

    def apply():
        sums = [zero, zero, zero]
        parts = []
        for first in range(0, tiles, 2):
            both = jnp.concatenate([edges(lambda which, item: state[2, which, item], at) for at in (first, first + 1)], axis=1)
            both = mm(weights[...], stacked_edges(both))
            for at in (first, first + 1):
                lanes = slice((at - first) * LANES, (at - first + 1) * LANES)
                fact = facts[at]
                is_second = jnp.concatenate([fact[24:32]] * (EDGE // 8), axis=0) > 0.5
                scale = jnp.concatenate([fact[32:40]] * (EDGE // 8), axis=0)
                stiff = jnp.where(is_second, both[EDGE : 2 * EDGE, lanes], both[:EDGE, lanes])
                mass = jnp.where(is_second, both[3 * EDGE :, lanes], both[2 * EDGE : 3 * EDGE, lanes])
                parts.append(scale * (stiff + lam * mass))
            for at in (first, first + 1):
                for which, value in enumerate(gather(parts, at)):
                    image[which, at] = value
                    sums[which] = sums[which] + state[2, which, at] * value
        return total(sums[0] + sums[1] + sums[2])

    sums = [zero, zero, zero]
    parts = {}
    for at in range(tiles):
        parts[at] = forcing[at]
    for at in range(tiles):
        for which, value in enumerate(gather(parts, at)):
            state[0, which, at] = zero
            state[1, which, at] = value
            state[2, which, at] = value
            sums[which] = sums[which] + value * value
    now = total(sums[0] + sums[1] + sums[2])

    def sweep(_, now):
        alpha = now / apply()
        sums = [zero, zero, zero]
        for at in range(tiles):
            for which in range(3):
                state[0, which, at] = state[0, which, at] + alpha * state[2, which, at]
                rest = state[1, which, at] - alpha * image[which, at]
                state[1, which, at] = rest
                sums[which] = sums[which] + rest * rest
        fresh = total(sums[0] + sums[1] + sums[2])
        ratio = fresh / now
        for at in range(tiles):
            for which in range(3):
                state[2, which, at] = state[1, which, at] + ratio * state[2, which, at]
        return fresh

    now = lax.fori_loop(0, CG_STEPS - 1, sweep, now)
    alpha = now / apply()
    found = [[state[0, which, at] + alpha * state[2, which, at] for at in range(tiles)] for which in range(3)]
    for at in range(tiles):
        traces[at] = edges(lambda which, item: found[which][item], at)


def exact(first, second):
    return jnp.dot(first, second, precision=HIGHEST, preferred_element_type=F32)


def iota(shape, axis):
    return lax.broadcasted_iota(jnp.int32, shape, axis)


def lam_of(row):
    return SIGMA_COEF + (BETA_COEF * ((row + 1) // 2).astype(F32)) ** 2


def advect_and_solve(velocity, geometry, kind, scale, dirichlet, stiffness, mass, lift_maps, recover_maps, count):
    elems = kind.shape[1]
    comps, rows, nodes = velocity.shape
    points = QUAD * QUAD
    per = LANES // rows
    pairs = per // 2
    planes = count * rows
    half = count * LANES // 2
    forward, backward, deriv = advect_tables(planes)

    group = COLUMN_ELEMS // per
    columns = count // group
    tiles = count // 2
    chunk = tiles // columns
    ends = 2

    def kernel(
        vel_in, geo_ref, kind_ref, scale_ref, fixed_ref, stiff_ref, mass_ref, lift_in, recover_in,
        forward_in, backward_in, deriv_in,
        out,
        vel_ref, forward_ref, backward_ref, deriv_ref, result,
        mid, kinds, factor, recover_out, sent, recv, hats, ret,
        store, turned, fields, partial, pieces, forcing, traces, found, facts_out, facts,
        state, image, geo, lift_ref, mat_ref, lam_ref, weights, lift_high, lift_low, recover_all,
        send_sem, recv_sem, pair_send, pair_recv, load_sem, out_sem,
    ):
        loads = [pltpu.make_async_copy(vel_in.at[comp], vel_ref.at[comp], load_sem.at[comp]) for comp in range(comps)]
        tables = ((forward_in, forward_ref), (deriv_in, deriv_ref), (backward_in, backward_ref))
        for at, (source, target) in enumerate(tables):
            loads.append(pltpu.make_async_copy(source, target, load_sem.at[comps + at]))
        for load in loads:
            load.start()
        me = lax.axis_index("planes")
        core = lax.axis_index("elem")
        barrier = pltpu.get_barrier_semaphore()

        def peer_at(step):
            return (me + step) % count

        def source_at(step):
            return (me + count - step) % count

        def greet(step, carry):
            pl.semaphore_signal(
                barrier, inc=1, device_id={"planes": peer_at(step)}, device_id_type=pl.DeviceIdType.MESH
            )
            return carry

        lax.fori_loop(1, count, greet, 0)
        pl.semaphore_signal(barrier, inc=1, device_id={"elem": 1 - core}, device_id_type=pl.DeviceIdType.MESH)

        def copy_to(source, target, way, comp, peer):
            return pltpu.make_async_remote_copy(
                src_ref=source.at[comp, peer],
                dst_ref=target.at[comp, me],
                send_sem=send_sem.at[way, comp, peer],
                recv_sem=recv_sem.at[way, comp, me],
                device_id={"planes": peer},
                device_id_type=pl.DeviceIdType.MESH,
            )

        def copy_from(source, target, way, comp, peer):
            return pltpu.make_async_remote_copy(
                src_ref=source.at[comp, peer],
                dst_ref=target.at[comp, peer],
                send_sem=send_sem.at[way, comp, peer],
                recv_sem=recv_sem.at[way, comp, peer],
                device_id={"planes": peer},
                device_id_type=pl.DeviceIdType.MESH,
            )

        def start_all(source, target, way, comp):
            def one(step, carry):
                copy_to(source, target, way, comp, peer_at(step)).start()
                return carry

            lax.fori_loop(1, count, one, 0)

        def follow_all(source, target, way, comp, before):
            def one(step, carry):
                peer = peer_at(step)
                copy_to(source, target, way, before, peer).wait_send()
                copy_to(source, target, way, comp, peer).start()
                return carry

            lax.fori_loop(1, count, one, 0)

        def pair_copy(source, target, at):
            return pltpu.make_async_remote_copy(
                src_ref=source,
                dst_ref=target,
                send_sem=pair_send.at[at],
                recv_sem=pair_recv.at[at],
                device_id={"elem": 1 - core},
                device_id_type=pl.DeviceIdType.MESH,
            )

        def facts_copy():
            return pair_copy(facts_out, facts.at[pl.ds(core * tiles, tiles)], comps * (columns + ends))

        def facts_arrive():
            pair_copy(facts_out, facts.at[pl.ds((1 - core) * tiles, tiles)], comps * (columns + ends)).wait_recv()

        def lifted_copy(comp, column, side):
            return pair_copy(
                pieces.at[comp, 1 - core, pl.ds(column * chunk, chunk)],
                forcing.at[comp, pl.ds(side * tiles + column * chunk, chunk)],
                comp * columns + column,
            )

        def trace_copy(comp, end, side):
            width = tiles // ends
            return pair_copy(
                traces.at[comp, pl.ds((1 - core) * tiles + end * width, width)],
                found.at[comp, side, pl.ds(end * width, width)],
                comps * columns + comp * ends + end,
            )

        def pack(comp):
            for part in range(count):
                rows_of = []
                for local in range(per):
                    at = element_at(part, local, group) * points
                    rows_of.append(vel_ref[comp, :, at : at + points])
                sent[comp, part] = jnp.concatenate(rows_of, axis=0).T

        def arrive(comp, part, block):
            block = jnp.concatenate([block, jnp.zeros((LANES - points, LANES), F32)], axis=0).T
            for local in range(per):
                at = local % 2 * LANES
                store[local // 2, pl.ds(pl.multiple_of(part * rows, rows), rows), at : at + LANES] = block[
                    local * rows : (local + 1) * rows
                ]

        def arrive_all(comp):
            arrive(comp, me, sent[comp, me])

            def one(step, carry):
                part = source_at(step)
                copy_from(sent, recv, 0, comp, part).wait_recv()
                arrive(comp, part, recv[comp, part])
                return carry

            lax.fori_loop(1, count, one, 0)

        def over_pairs(body):
            def one(pair, carry):
                body(pair)
                return carry

            lax.fori_loop(0, pairs, one, 0)

        def synthesize(comp, pair):
            fields[comp, pair] = mm(forward_ref[...], stacked_values(store[pair]))

        def slope_last(pair):
            fields[comps - 1, pair, planes:] = mm(forward_ref[planes:], stacked_values(store[pair]))

        def derive(comp, pair):
            for which in range(2):
                at = slice(which * LANES, (which + 1) * LANES)
                high, low = split(fields[comp, pair, :planes, at])
                slopes = mm(jnp.concatenate([high, low], axis=1), deriv_ref[: 2 * LANES]) + mm(
                    high, deriv_ref[2 * LANES :]
                )
                part = geo[pair * 2 + which]
                first = fields[0, pair, :planes, at]
                second = fields[1, pair, :planes, at]
                partial[comp, pair, :, at] = slopes[:, :LANES] * (first * part[0:1] + second * part[2:3]) + slopes[
                    :, LANES:
                ] * (first * part[1:2] + second * part[3:4])

        def advect(comp, pair, along):
            result = partial[comp, pair] + along * fields[comp, pair, planes:]
            turned[pair] = mm(backward_ref[...], stacked_values(result))

        def first_advect(pair):
            along = mm(forward_ref[:planes], stacked_values(store[pair]))
            fields[comps - 1, pair, :planes] = along
            advect(0, pair, along)

        def turn_back(comp):
            for part in range(count):
                block = jnp.concatenate(
                    [
                        turned[local // 2, part * rows : (part + 1) * rows, local % 2 * LANES : (local % 2 + 1) * LANES]
                        for local in range(per)
                    ],
                    axis=0,
                )
                hats[comp, part] = block.T[:points]

        def lift(comp):
            bit = lax.broadcasted_iota(jnp.int32, (EDGE, LANES), 1) // 8 % 2 == 0
            mine = me // group

            def one(step, carry):
                column = (mine // 2 + step // 2) % 2 * 2 + (mine + step) % 2
                fields_of = []
                for inner in range(group):
                    part = column * group + inner

                    @pl.when(part != me)
                    def _():
                        copy_from(hats, ret, 1, comp, part).wait_recv()

                    @pl.when(part == me)
                    def _():
                        ret[comp, part] = hats[comp, part]

                    value = sent[comp, part] - STEP_DT * ret[comp, part]
                    mid[comp, part] = value
                    fields_of.append(value)
                high, low = split(SIGMA_COEF * jnp.concatenate(fields_of, axis=1))
                both = mm(lift_high[...], high) + (mm(lift_high[...], low) + mm(lift_low[...], high))
                lifted = jnp.where(kinds[column, 0:1] > 0.5, both[EDGE:], both[:EDGE])
                for local in range(chunk):
                    even = lifted[:, 2 * local * LANES : (2 * local + 1) * LANES]
                    odd = lifted[:, (2 * local + 1) * LANES : (2 * local + 2) * LANES]
                    at = column * chunk + local
                    pieces[comp, 0, at] = jnp.where(bit, even, pltpu.roll(odd, 8, 1))
                    pieces[comp, 1, at] = jnp.where(bit, pltpu.roll(even, LANES - 8, 1), odd)
                lifted_copy(comp, column, core).start()
                for local in range(chunk):
                    at = column * chunk + local
                    forcing[comp, core * tiles + at] = pieces[comp, core, at]
                return carry

            lax.fori_loop(0, columns, one, 0)

        def solve(comp):
            for column in range(columns):
                lifted_copy(comp, column, 1 - core).wait_recv()
            solve_rows(forcing.at[comp], facts, lam_ref[...], weights, state, image, traces.at[comp])
            for end in range(ends):
                trace_copy(comp, end, core).start()
            for at in range(tiles):
                found[comp, core, at] = traces[comp, core * tiles + at]

        def leave(comp, end):
            cut = nodes // 2 // LANES * LANES
            lanes = pl.ds(end * cut, (cut, nodes - cut)[end])
            return pltpu.make_async_copy(result.at[comp, :, lanes], out.at[comp, :, lanes], out_sem.at[comp, end])

        def recover(comp):
            bit = lax.broadcasted_iota(jnp.int32, (EDGE, LANES), 1) // 8 % 2 == 0
            for column in range(columns):
                if column == columns // 2:
                    leave(comp, 0).start()
                if column % (columns // ends) == 0:
                    trace_copy(comp, column // (columns // ends), 1 - core).wait_recv()
                edges = []
                for at in range(column * chunk, (column + 1) * chunk):
                    low_rows = found[comp, 0, at]
                    high_rows = found[comp, 1, at]
                    edges.append(jnp.where(bit, low_rows, pltpu.roll(high_rows, 8, 1)))
                    edges.append(jnp.where(bit, pltpu.roll(low_rows, LANES - 8, 1), high_rows))
                both = mm(recover_all[...], stacked_edges(jnp.concatenate(edges, axis=1)))
                node = jnp.where(kinds[column, 0:1] > 0.5, both[88 : 88 + points], both[:points])
                for inner in range(group):
                    part = column * group + inner
                    block = mid[comp, part] * factor[0:1] + node[:, inner * LANES : (inner + 1) * LANES]
                    block = jnp.concatenate([block, jnp.zeros((LANES - points, LANES), F32)], axis=0).T
                    for local in range(per):
                        start = element_at(part, local, group) * points
                        result[comp, :, start : start + points] = block[local * rows : (local + 1) * rows, :points]
            leave(comp, 1).start()

        def prepare():
            def place(row):
                return jnp.where(row < 32, row // 8 * QUAD + row % 8, (row - 32) * QUAD + 8)

            widen = (place(iota((EDGE, 4 * QUAD), 0)) == iota((EDGE, 4 * QUAD), 1)).astype(F32)
            widen_cols = (place(iota((4 * QUAD, EDGE), 1)) == iota((4 * QUAD, EDGE), 0)).astype(F32)
            recover_out[...] = jnp.zeros_like(recover_out)
            for which in range(2):
                at = which * EDGE
                mat_ref[at : at + EDGE] = exact(exact(widen, stiff_ref[:, which, :]), widen_cols)
                at = at + 2 * EDGE
                mat_ref[at : at + EDGE] = exact(exact(widen, mass_ref[:, which, :]), widen_cols)
                lift_ref[which * EDGE : (which + 1) * EDGE] = exact(widen, lift_in[:, which, :])
                recover_out[which * 88 : which * 88 + points] = exact(widen, recover_in[:, which, :]).T
            weights[...] = stacked_weights(mat_ref[...])
            recover_all[...] = stacked_weights(recover_out[...])
            high, low = split(lift_ref[...])
            lift_high[...] = high
            lift_low[...] = low
            is_second = (kind_ref[...] == 1).astype(F32)
            free_v = (1 - fixed_ref[:, 0, :]).astype(F32)
            free_h = (1 - fixed_ref[:, 1, :]).astype(F32)
            none = jnp.zeros((5, elems), F32)
            rest = [free_v[8:9], none[:1], free_h[8:9], none]
            table = jnp.concatenate([free_v[:8], free_h[:8]] + rest + [is_second] * 8 + [scale_ref[...]] * 8, axis=0)
            lane = iota((elems, half), 1)
            element = element_at(lane // LANES * 2 + lane // 8 % 2, lane % LANES // 16, group)
            placed = exact(table, (element == iota((elems, half), 0)).astype(F32))
            for at in range(tiles):
                facts_out[at] = placed[:, at * LANES : (at + 1) * LANES]
                facts[core * tiles + at] = placed[:, at * LANES : (at + 1) * LANES]
            lane = iota((elems, 2 * half), 1)
            element = element_at(lane // LANES, lane % LANES // rows, group)
            spread = (element == iota((elems, 2 * half), 0)).astype(F32)
            placed = exact(jnp.broadcast_to(is_second, (8, elems)), spread)
            width = 2 * half // columns
            for column in range(columns):
                kinds[column] = placed[:, column * width : (column + 1) * width]
            lane = iota((8, LANES), 1)
            lam_ref[...] = lam_of(me * rows + core * 8 + lane % 8)
            factor[...] = SIGMA_COEF / (SIGMA_COEF + lam_of(me * rows + lane % rows))
            geo[...] = jnp.zeros_like(geo)
            for part in range(count):

                @pl.when(me == part)
                def _():
                    for local in range(per):
                        at = element_at(part, local, group) * points
                        geo[local, 0:4, 0:points] = geo_ref[:, at : at + points]

        last = comps - 1
        loads[0].wait()
        pack(0)
        pl.semaphore_wait(barrier, count)
        start_all(sent, recv, 0, 0)
        for comp in range(1, comps):
            loads[comp].wait()
            pack(comp)
        prepare()
        facts_copy().start()
        for load in loads[comps:]:
            load.wait()
        for comp in range(last):
            follow_all(sent, recv, 0, comp + 1, comp)
            arrive_all(comp)
            over_pairs(functools.partial(synthesize, comp))
        for comp in range(last):
            over_pairs(functools.partial(derive, comp))
        arrive_all(last)
        for pair in range(pairs):
            first_advect(pair)
        turn_back(0)
        start_all(hats, ret, 1, 0)
        for comp in range(1, last):
            over_pairs(lambda pair, comp=comp: advect(comp, pair, fields[last, pair, :planes]))
            turn_back(comp)
            start_all(hats, ret, 1, comp)
        over_pairs(slope_last)
        over_pairs(functools.partial(derive, last))
        over_pairs(lambda pair: advect(last, pair, fields[last, pair, :planes]))
        turn_back(last)
        follow_all(hats, ret, 1, last, 0)
        facts_arrive()
        for comp in range(comps):
            lift(comp)
            solve(comp)
            recover(comp)
        facts_copy().wait_send()
        for comp in range(comps):
            for column in range(columns):
                lifted_copy(comp, column, core).wait_send()
            for end in range(ends):
                trace_copy(comp, end, core).wait_send()

        def drain(step, carry):
            peer = peer_at(step)
            copy_to(sent, recv, 0, last, peer).wait_send()
            for comp in range(1, comps):
                copy_to(hats, ret, 1, comp, peer).wait_send()
            return carry

        lax.fori_loop(1, count, drain, 0)
        for comp in range(comps):
            for end in range(2):
                leave(comp, end).wait()

    message = (comps, count, points, LANES)
    operands = (velocity, geometry, kind, scale, dirichlet, stiffness, mass, lift_maps, recover_maps)
    operands = operands + (forward, backward, deriv)
    vmem = pl.BlockSpec(memory_space=pltpu.VMEM)
    anywhere = pl.BlockSpec(memory_space=pl.ANY)
    copies = comps * (columns + ends) + 1
    return pl.pallas_call(
        kernel,
        in_specs=[anywhere] + [vmem] * 8 + [anywhere] * 3,
        out_specs=anywhere,
        out_shape=jax.ShapeDtypeStruct(velocity.shape, F32),
        scratch_shapes=[
            pltpu.VMEM(velocity.shape, F32),
            pltpu.VMEM(forward.shape, BF16),
            pltpu.VMEM(backward.shape, BF16),
            pltpu.VMEM(deriv.shape, BF16),
            pltpu.VMEM(velocity.shape, F32),
            pltpu.VMEM(message, F32),
            pltpu.VMEM((columns, 8, group * LANES), F32),
            pltpu.VMEM((8, LANES), F32),
            pltpu.VMEM((2 * 88, EDGE), F32),
        ]
        + [pltpu.VMEM(message, F32)] * 4
        + [
            pltpu.VMEM((pairs, planes, 2 * LANES), F32),
            pltpu.VMEM((pairs, planes, 2 * LANES), F32),
            pltpu.VMEM((comps, pairs, 2 * planes, 2 * LANES), F32),
            pltpu.VMEM((comps, pairs, planes, 2 * LANES), F32),
            pltpu.VMEM((comps, 2, tiles, EDGE, LANES), F32),
            pltpu.VMEM((comps, 2 * tiles, EDGE, LANES), F32),
            pltpu.VMEM((comps, 2 * tiles, EDGE, LANES), F32),
            pltpu.VMEM((comps, 2, tiles, EDGE, LANES), F32),
            pltpu.VMEM((tiles, 40, LANES), F32),
            pltpu.VMEM((2 * tiles, 40, LANES), F32),
            pltpu.VMEM((3, 3, 2 * tiles, 8, LANES), F32),
            pltpu.VMEM((3, 2 * tiles, 8, LANES), F32),
            pltpu.VMEM((per, 8, LANES), F32),
            pltpu.VMEM((2 * EDGE, points), F32),
            pltpu.VMEM((4 * EDGE, EDGE), F32),
            pltpu.VMEM((8, LANES), F32),
            pltpu.VMEM((4 * EDGE, LANES), BF16),
            pltpu.VMEM((2 * EDGE, points), BF16),
            pltpu.VMEM((2 * EDGE, points), BF16),
            pltpu.VMEM((2 * 88, LANES), BF16),
        ]
        + [
            pltpu.SemaphoreType.DMA((2, comps, count)),
            pltpu.SemaphoreType.DMA((2, comps, count)),
            pltpu.SemaphoreType.DMA((copies,)),
            pltpu.SemaphoreType.DMA((copies,)),
            pltpu.SemaphoreType.DMA((comps + 3,)),
            pltpu.SemaphoreType.DMA((comps, 2)),
        ],
        compiler_params=pltpu.CompilerParams(
            vmem_limit_bytes=60 * 1024 * 1024, collective_id=0, has_side_effects=True
        ),
        name="advect_and_solve",
    )(*operands)


def fast_device(
    velocity,
    geometry,
    element_kind,
    element_scale,
    dirichlet,
    schur_stiffness,
    schur_mass,
    lift,
    recover,
):
    count = lax.axis_size("planes")
    return advect_and_solve(
        velocity,
        geometry,
        element_kind[None],
        element_scale[None],
        dirichlet.swapaxes(0, 1),
        schur_stiffness.swapaxes(0, 1),
        schur_mass.swapaxes(0, 1),
        lift.swapaxes(0, 1),
        recover.transpose(2, 0, 1),
        count,
    )


def per_device(velocity, geometry, element_kind, *rest):
    count = lax.axis_size("planes")
    rows = velocity.shape[1]
    elems = element_kind.shape[0]
    fits = count & (count - 1) == 0 and rows == 16 and elems == LANES and elems * rows == count * LANES and lax.axis_size("elem") == 2
    body = fast_device if fits else plain_device
    return body(velocity, geometry, element_kind, *rest)


def solution(mesh):
    in_specs = (
        P(None, "planes", "elem"),
        P(None, "elem"),
        P("elem"),
        P("elem"),
        P(None, None, "elem"),
        P(),
        P(),
        P(),
        P(),
    )
    out_specs = P(None, "planes", "elem")
    return jax.shard_map(
        per_device, mesh=mesh, in_specs=in_specs, out_specs=out_specs, check_vma=False
    )
```

```python
import functools
import math

import jax
import jax.numpy as jnp
import numpy as np
from jax import lax
from jax.experimental import pallas as pl
from jax.experimental.pallas import tpu as pltpu
from jax.sharding import PartitionSpec as P

PLANES = 256
QUAD = 9
COLUMN_ELEMS = 32
CG_STEPS = 4


HIGHEST = lax.Precision.HIGHEST
SIGMA_COEF = 1.0
BETA_COEF = 0.01
STEP_DT = 0.002


def passed_along(value, axis, steps):
    count = lax.axis_size(axis)
    leading, last = (max(0, -steps), min(count, count - steps))
    return lax.ppermute(value, axis, [(source, source + steps) for source in range(leading, last)])


def gauss_derivative(points):
    nodes = -np.cos(np.pi * (2 * np.arange(points) + 1) / (2 * points))
    ident = np.eye(points)
    diffs = nodes[:, None] - nodes[None, :] + ident
    weights = 1.0 / np.prod(diffs, axis=1)
    matrix = weights[None, :] / weights[:, None] / diffs
    matrix = matrix * (1.0 - ident)
    return matrix - ident * matrix.sum(axis=1)[:, None]


def kron_tables():
    deriv = gauss_derivative(QUAD)
    identity = np.eye(QUAD)
    return (
        jnp.asarray(np.kron(deriv, identity), jnp.float32),
        jnp.asarray(np.kron(identity, deriv), jnp.float32),
    )


def fourier_tables(planes):
    zeta = jnp.arange(planes, dtype=jnp.int32)
    rows = jnp.arange(planes, dtype=jnp.int32)
    waves = (rows + 1) // 2
    phase = waves[None, :] * zeta[:, None] % planes
    angle = 2.0 * math.pi / planes * phase.astype(jnp.float32)
    cosine = jnp.cos(angle)
    sine = jnp.sin(angle)
    odd = (rows % 2 == 1)[None, :]
    first = (rows == 0)[None, :]
    last = (rows == planes - 1)[None, :]
    synth = jnp.where(first, 1.0, jnp.where(odd, cosine, sine))
    rate = BETA_COEF * waves.astype(jnp.float32)[None, :]
    slope = jnp.where(first | last, 0.0, jnp.where(odd, -rate * sine, rate * cosine))
    weight = jnp.where((rows == 0) | (rows == planes - 1), 1.0 / planes, 2.0 / planes).astype(
        jnp.float32
    )
    analysis = synth.T * weight[:, None]
    return (synth, slope, analysis)


def inner(first_pair, second_pair):
    return jnp.sum(first_pair[0] * second_pair[0], axis=(0, 2)) + jnp.sum(
        first_pair[1] * second_pair[1], axis=(0, 2)
    )


def global_total(first_pair, second_pair):
    return lax.psum(inner(first_pair, second_pair), "elem")


def global_squares(pair):
    return lax.psum(inner(pair, pair), "elem")


def assemble(outputs, incoming, free):
    left = outputs[:QUAD]
    right = outputs[QUAD : 2 * QUAD]
    bottom = outputs[2 * QUAD : 3 * QUAD]
    top = outputs[3 * QUAD :]
    vertical = left + jnp.concatenate([incoming, right[:, :, :-COLUMN_ELEMS]], axis=2)
    grid = top.reshape(top.shape[0], top.shape[1], -1, COLUMN_ELEMS)
    shifted = jnp.concatenate([jnp.zeros_like(grid[..., :1]), grid[..., :-1]], axis=3).reshape(
        bottom.shape
    )
    horizontal = bottom + shifted
    return (vertical * free[0], horizontal * free[1])


def plain_device(
    velocity,
    geometry,
    element_kind,
    element_scale,
    dirichlet,
    schur_stiffness,
    schur_mass,
    lift,
    recover,
):
    first, second = kron_tables()
    synth, slope, analysis = fourier_tables(PLANES)
    local_rows = velocity.shape[1]
    node_count = velocity.shape[2]
    share = node_count // lax.axis_size("planes")
    geo_part = lax.dynamic_slice_in_dim(geometry, lax.axis_index("planes") * share, share, 1)

    def transform(table, field):
        return jnp.einsum("zr,crm->czm", table, field, precision=HIGHEST)

    items = lax.all_to_all(velocity, "planes", split_axis=2, concat_axis=1, tiled=True)
    values = transform(synth, items)
    along_z = transform(slope, items)
    shaped = values.reshape(values.shape[:-1] + (-1, QUAD * QUAD))
    along_r = jnp.einsum("...en,mn->...em", shaped, first, precision=HIGHEST).reshape(values.shape)
    along_s = jnp.einsum("...en,mn->...em", shaped, second, precision=HIGHEST).reshape(values.shape)
    along_x = geo_part[0] * along_r + geo_part[1] * along_s
    along_y = geo_part[2] * along_r + geo_part[3] * along_s
    values, along_x, along_y, along_z = (values, along_x, along_y, along_z)
    advection = values[0] * along_x + values[1] * along_y + values[2] * along_z
    advection_hat = jnp.einsum("rz,czm->crm", analysis, advection, precision=HIGHEST)
    returned = lax.all_to_all(advection_hat, "planes", split_axis=1, concat_axis=2, tiled=True)
    intermediate = velocity - STEP_DT * returned
    elem_count = element_kind.shape[0]
    row_count = 3 * local_rows
    waves = (
        (lax.axis_index("planes") * local_rows + jnp.arange(local_rows, dtype=jnp.int32) + 1) // 2
    ).astype(jnp.float32)
    lam = jnp.tile(SIGMA_COEF + (BETA_COEF * waves) ** 2, 3)
    free = (1 - dirichlet).astype(jnp.float32)[:, :, None, :]
    chooser = (element_kind == 1).astype(jnp.float32)

    def element_apply(vector, kinds, scales):
        flat = vector.reshape(vector.shape[0], -1)
        results = []
        for kind in range(2):
            stiff = jnp.dot(schur_stiffness[kind], flat, precision=HIGHEST).reshape(vector.shape)
            massed = jnp.dot(schur_mass[kind], flat, precision=HIGHEST).reshape(vector.shape)
            results.append(stiff + lam[None, :, None] * massed)
        return scales[None, None, :] * jnp.where(kinds[None, None, :] > 0.5, results[1], results[0])

    def element_vector(vertical, horizontal):
        arriving = passed_along(vertical[:, :, :COLUMN_ELEMS], "elem", -1)
        right = jnp.concatenate([vertical[:, :, COLUMN_ELEMS:], arriving], axis=2)
        grid = horizontal.reshape(horizontal.shape[0], horizontal.shape[1], -1, COLUMN_ELEMS)
        top = jnp.concatenate([grid[..., 1:], jnp.zeros_like(grid[..., :1])], axis=3).reshape(
            horizontal.shape
        )
        return jnp.concatenate([vertical, right, horizontal, top], axis=0)

    node_values = (SIGMA_COEF * intermediate).reshape(row_count, elem_count, QUAD * QUAD)
    lifted = jnp.where(
        chooser[None, None, :] > 0.5,
        jnp.einsum("kn,ren->kre", lift[1], node_values, precision=HIGHEST),
        jnp.einsum("kn,ren->kre", lift[0], node_values, precision=HIGHEST),
    )
    lifted_right = passed_along(lifted[QUAD : 2 * QUAD, :, -COLUMN_ELEMS:], "elem", 1)
    forcing = assemble(lifted, lifted_right, free)
    trace = (jnp.zeros_like(forcing[0]), jnp.zeros_like(forcing[1]))
    residual = forcing
    direction = forcing
    norm_now = global_squares(residual)
    for sweep in range(CG_STEPS):
        outputs = element_apply(element_vector(direction[0], direction[1]), chooser, element_scale)
        operator_arriving = passed_along(outputs[QUAD : 2 * QUAD, :, -COLUMN_ELEMS:], "elem", 1)
        image = assemble(outputs, operator_arriving, free)
        alpha = (norm_now / global_total(direction, image))[None, :, None]
        trace = (trace[0] + alpha * direction[0], trace[1] + alpha * direction[1])
        residual = (residual[0] - alpha * image[0], residual[1] - alpha * image[1])
        norm_next = global_squares(residual)
        ratio = (norm_next / norm_now)[None, :, None]
        direction = (residual[0] + ratio * direction[0], residual[1] + ratio * direction[1])
        norm_now = norm_next
    vector = element_vector(trace[0], trace[1])
    recovered = jnp.where(
        chooser[None, :, None] > 0.5,
        jnp.einsum("nl,lre->ren", recover[1], vector, precision=HIGHEST),
        jnp.einsum("nl,lre->ren", recover[0], vector, precision=HIGHEST),
    )
    weight = SIGMA_COEF / (SIGMA_COEF + lam)
    result = (
        intermediate.reshape(row_count, elem_count, QUAD * QUAD) * weight[:, None, None] + recovered
    )
    return result.reshape(velocity.shape)


LANES = 128
EDGE = 40
F32 = jnp.float32
BF16 = jnp.bfloat16


def split(value):
    high = value.astype(BF16)
    return high, (value - high.astype(F32)).astype(BF16)


def np_split(value):
    high = np.asarray(value, np.float32).astype(BF16)
    low = (np.asarray(value, np.float64) - high.astype(np.float64)).astype(np.float32).astype(BF16)
    return high, low


def mm(first, second):
    return jnp.dot(first, second, preferred_element_type=F32)


def stacked_values(values):
    high, low = split(values)
    return jnp.concatenate([high, low, high], axis=0)


def advect_tables(planes):
    zeta = np.arange(planes)
    rows = np.arange(planes)
    waves = (rows + 1) // 2
    angle = 2.0 * np.pi / planes * ((waves[None, :] * zeta[:, None]) % planes)
    odd = (rows % 2 == 1)[None, :]
    first = (rows == 0)[None, :]
    last = (rows == planes - 1)[None, :]
    synth = np.where(first, 1.0, np.where(odd, np.cos(angle), np.sin(angle)))
    rate = BETA_COEF * waves[None, :]
    slope = np.where(first | last, 0.0, np.where(odd, -rate * np.sin(angle), rate * np.cos(angle)))
    weight = np.where((rows == 0) | (rows == planes - 1), 1.0 / planes, 2.0 / planes)
    analysis = synth.T * weight[:, None]
    high, low = np_split(np.concatenate([synth, slope], axis=0))
    forward = np.concatenate([high, high, low], axis=1)
    high, low = np_split(analysis)
    backward = np.concatenate([high, high, low], axis=1)
    points = QUAD * QUAD
    deriv = gauss_derivative(QUAD)
    both = np.zeros((LANES, 2 * LANES))
    both[:points, :points] = np.kron(deriv, np.eye(QUAD)).T
    both[:points, LANES : LANES + points] = np.kron(np.eye(QUAD), deriv).T
    high, low = np_split(both)
    return jnp.asarray(forward), jnp.asarray(backward), jnp.asarray(np.concatenate([high, high, low], axis=0))


def whole_spec(shape):
    return pl.BlockSpec(shape, lambda *_: (0,) * len(shape))


def params():
    return pltpu.CompilerParams(vmem_limit_bytes=60 * 1024 * 1024)


def element_at(part, slot, group):
    inner = part % group
    return part // group * COLUMN_ELEMS + slot * group + inner % 2 * (group // 2) + inner // 2


def stacked_weights(weights):
    high, low = split(weights)
    pad = jnp.zeros((weights.shape[0], LANES - 3 * EDGE), BF16)
    return jnp.concatenate([high, high, low, pad], axis=1)


def stacked_edges(value):
    high = value.astype(BF16).astype(F32)
    pad = jnp.zeros((LANES - 3 * EDGE, value.shape[1]), F32)
    return jnp.concatenate([high, value - high, high, pad], axis=0).astype(BF16)


def tree(terms):
    while len(terms) > 1:
        terms = [terms[at] + terms[at + 1] for at in range(0, len(terms), 2)]
    return terms[0]


def solve_rows(forcing, facts, lam, weights, state, image, traces):
    tiles = forcing.shape[0]
    lane = lax.broadcasted_iota(jnp.int32, (8, LANES), 1)
    sub = lax.broadcasted_iota(jnp.int32, (8, LANES), 0)
    top_edge = lane >= LANES - 8
    low_edge = lane < 8
    zero = jnp.zeros((8, LANES), F32)
    lam = jnp.concatenate([lam] * (EDGE // 8), axis=0)

    def above(tile_of, at):
        if at % 2 == 0:
            return tile_of(at + 1)
        return jnp.where(top_edge, 0.0, pltpu.roll(tile_of(at - 1), LANES - 8, 1))

    def below(tile_of, at):
        if at % 2 == 1:
            return tile_of(at - 1)
        return jnp.where(low_edge, 0.0, pltpu.roll(tile_of(at + 1), 8, 1))

    def edges(tile_of, at):
        beside = at + 2 < tiles
        right = tile_of(0, at + 2) if beside else zero
        right_rest = tile_of(2, at + 2) if beside else zero
        top = above(lambda item: tile_of(1, item), at)
        top_rest = above(lambda item: tile_of(2, item), at)
        rest = jnp.where(sub == 0, right_rest, jnp.where(sub == 2, top_rest, 0.0))
        rest = tile_of(2, at) + pltpu.roll(rest, 1, 0)
        return jnp.concatenate([tile_of(0, at), right, tile_of(1, at), top, rest], axis=0)

    def gather(parts, at):
        part = parts[at]
        fact = facts[at]
        left = part[:8]
        rest = below(lambda item: parts[item][32:40], at)
        if at >= 2:
            left = left + parts[at - 2][8:16]
            rest = jnp.where(sub == 1, parts[at - 2][32:40], jnp.where(sub == 3, rest, 0.0))
        else:
            rest = jnp.where(sub == 3, rest, 0.0)
        rest = part[32:40] + pltpu.roll(rest, 7, 0)
        bottom = part[16:24] + below(lambda item: parts[item][24:32], at)
        return left * fact[:8], bottom * fact[8:16], rest * fact[16:24]

    def total(acc):
        acc = tree([acc] + [pltpu.roll(acc, 8 * step, 1) for step in range(1, LANES // 8)])
        return tree([acc] + [pltpu.roll(acc, step, 0) for step in range(1, 8)])

    def apply():
        sums = [zero, zero, zero]
        parts = []
        for first in range(0, tiles, 2):
            both = jnp.concatenate([edges(lambda which, item: state[2, which, item], at) for at in (first, first + 1)], axis=1)
            both = mm(weights[...], stacked_edges(both))
            for at in (first, first + 1):
                lanes = slice((at - first) * LANES, (at - first + 1) * LANES)
                fact = facts[at]
                is_second = jnp.concatenate([fact[24:32]] * (EDGE // 8), axis=0) > 0.5
                scale = jnp.concatenate([fact[32:40]] * (EDGE // 8), axis=0)
                stiff = jnp.where(is_second, both[EDGE : 2 * EDGE, lanes], both[:EDGE, lanes])
                mass = jnp.where(is_second, both[3 * EDGE :, lanes], both[2 * EDGE : 3 * EDGE, lanes])
                parts.append(scale * (stiff + lam * mass))
            for at in (first, first + 1):
                for which, value in enumerate(gather(parts, at)):
                    image[which, at] = value
                    sums[which] = sums[which] + state[2, which, at] * value
        return total(sums[0] + sums[1] + sums[2])

    sums = [zero, zero, zero]
    parts = {}
    for at in range(tiles):
        parts[at] = forcing[at]
    for at in range(tiles):
        for which, value in enumerate(gather(parts, at)):
            state[0, which, at] = zero
            state[1, which, at] = value
            state[2, which, at] = value
            sums[which] = sums[which] + value * value
    now = total(sums[0] + sums[1] + sums[2])

    def sweep(_, now):
        alpha = now / apply()
        sums = [zero, zero, zero]
        for at in range(tiles):
            for which in range(3):
                state[0, which, at] = state[0, which, at] + alpha * state[2, which, at]
                rest = state[1, which, at] - alpha * image[which, at]
                state[1, which, at] = rest
                sums[which] = sums[which] + rest * rest
        fresh = total(sums[0] + sums[1] + sums[2])
        ratio = fresh / now
        for at in range(tiles):
            for which in range(3):
                state[2, which, at] = state[1, which, at] + ratio * state[2, which, at]
        return fresh

    now = lax.fori_loop(0, CG_STEPS - 1, sweep, now)
    alpha = now / apply()
    found = [[state[0, which, at] + alpha * state[2, which, at] for at in range(tiles)] for which in range(3)]
    for at in range(tiles):
        traces[at] = edges(lambda which, item: found[which][item], at)


def exact(first, second):
    return jnp.dot(first, second, precision=HIGHEST, preferred_element_type=F32)


def iota(shape, axis):
    return lax.broadcasted_iota(jnp.int32, shape, axis)


def lam_of(row):
    return SIGMA_COEF + (BETA_COEF * ((row + 1) // 2).astype(F32)) ** 2


def advect_and_solve(velocity, geometry, kind, scale, dirichlet, stiffness, mass, lift_maps, recover_maps, count):
    elems = kind.shape[1]
    comps, rows, nodes = velocity.shape
    points = QUAD * QUAD
    per = LANES // rows
    pairs = per // 2
    planes = count * rows
    half = count * LANES // 2
    forward, backward, deriv = advect_tables(planes)

    group = COLUMN_ELEMS // per
    columns = count // group
    tiles = count // 2
    chunk = tiles // columns
    ends = 2

    def kernel(
        vel_in, geo_ref, kind_ref, scale_ref, fixed_ref, stiff_ref, mass_ref, lift_in, recover_in,
        forward_in, backward_in, deriv_in,
        out,
        vel_ref, forward_ref, backward_ref, deriv_ref, result,
        mid, kinds, factor, recover_out, sent, recv, hats, ret,
        store, turned, fields, partial, pieces, forcing, traces, found, facts_out, facts,
        state, image, geo, lift_ref, mat_ref, lam_ref, weights, lift_high, lift_low, recover_all,
        send_sem, recv_sem, pair_send, pair_recv, load_sem, out_sem,
    ):
        loads = [pltpu.make_async_copy(vel_in.at[comp], vel_ref.at[comp], load_sem.at[comp]) for comp in range(comps)]
        tables = ((forward_in, forward_ref), (deriv_in, deriv_ref), (backward_in, backward_ref))
        for at, (source, target) in enumerate(tables):
            loads.append(pltpu.make_async_copy(source, target, load_sem.at[comps + at]))
        for load in loads:
            load.start()
        me = lax.axis_index("planes")
        core = lax.axis_index("elem")
        barrier = pltpu.get_barrier_semaphore()

        def peer_at(step):
            return (me + step) % count

        def source_at(step):
            return (me + count - step) % count

        def greet(step, carry):
            pl.semaphore_signal(
                barrier, inc=1, device_id={"planes": peer_at(step)}, device_id_type=pl.DeviceIdType.MESH
            )
            return carry

        lax.fori_loop(1, count, greet, 0)
        pl.semaphore_signal(barrier, inc=1, device_id={"elem": 1 - core}, device_id_type=pl.DeviceIdType.MESH)

        def copy_to(source, target, way, comp, peer):
            return pltpu.make_async_remote_copy(
                src_ref=source.at[comp, peer],
                dst_ref=target.at[comp, me],
                send_sem=send_sem.at[way, comp, peer],
                recv_sem=recv_sem.at[way, comp, me],
                device_id={"planes": peer},
                device_id_type=pl.DeviceIdType.MESH,
            )

        def copy_from(source, target, way, comp, peer):
            return pltpu.make_async_remote_copy(
                src_ref=source.at[comp, peer],
                dst_ref=target.at[comp, peer],
                send_sem=send_sem.at[way, comp, peer],
                recv_sem=recv_sem.at[way, comp, peer],
                device_id={"planes": peer},
                device_id_type=pl.DeviceIdType.MESH,
            )

        def start_all(source, target, way, comp):
            def one(step, carry):
                copy_to(source, target, way, comp, peer_at(step)).start()
                return carry

            lax.fori_loop(1, count, one, 0)

        def follow_all(source, target, way, comp, before):
            def one(step, carry):
                peer = peer_at(step)
                copy_to(source, target, way, before, peer).wait_send()
                copy_to(source, target, way, comp, peer).start()
                return carry

            lax.fori_loop(1, count, one, 0)

        def pair_copy(source, target, at):
            return pltpu.make_async_remote_copy(
                src_ref=source,
                dst_ref=target,
                send_sem=pair_send.at[at],
                recv_sem=pair_recv.at[at],
                device_id={"elem": 1 - core},
                device_id_type=pl.DeviceIdType.MESH,
            )

        def facts_copy():
            return pair_copy(facts_out, facts.at[pl.ds(core * tiles, tiles)], comps * (columns + ends))

        def facts_arrive():
            pair_copy(facts_out, facts.at[pl.ds((1 - core) * tiles, tiles)], comps * (columns + ends)).wait_recv()

        def lifted_copy(comp, column, side):
            return pair_copy(
                pieces.at[comp, 1 - core, pl.ds(column * chunk, chunk)],
                forcing.at[comp, pl.ds(side * tiles + column * chunk, chunk)],
                comp * columns + column,
            )

        def trace_copy(comp, end, side):
            width = tiles // ends
            return pair_copy(
                traces.at[comp, pl.ds((1 - core) * tiles + end * width, width)],
                found.at[comp, side, pl.ds(end * width, width)],
                comps * columns + comp * ends + end,
            )

        def pack(comp):
            for part in range(count):
                rows_of = []
                for local in range(per):
                    at = element_at(part, local, group) * points
                    rows_of.append(vel_ref[comp, :, at : at + points])
                sent[comp, part] = jnp.concatenate(rows_of, axis=0).T

        def arrive(comp, part, block):
            block = jnp.concatenate([block, jnp.zeros((LANES - points, LANES), F32)], axis=0).T
            for local in range(per):
                at = local % 2 * LANES
                store[local // 2, pl.ds(pl.multiple_of(part * rows, rows), rows), at : at + LANES] = block[
                    local * rows : (local + 1) * rows
                ]

        def arrive_all(comp):
            arrive(comp, me, sent[comp, me])

            def one(step, carry):
                part = source_at(step)
                copy_from(sent, recv, 0, comp, part).wait_recv()
                arrive(comp, part, recv[comp, part])
                return carry

            lax.fori_loop(1, count, one, 0)

        def over_pairs(body):
            def one(pair, carry):
                body(pair)
                return carry

            lax.fori_loop(0, pairs, one, 0)

        def synthesize(comp, pair):
            fields[comp, pair] = mm(forward_ref[...], stacked_values(store[pair]))

        def slope_last(pair):
            fields[comps - 1, pair, planes:] = mm(forward_ref[planes:], stacked_values(store[pair]))

        def derive(comp, pair):
            for which in range(2):
                at = slice(which * LANES, (which + 1) * LANES)
                high, low = split(fields[comp, pair, :planes, at])
                slopes = mm(jnp.concatenate([high, low], axis=1), deriv_ref[: 2 * LANES]) + mm(
                    high, deriv_ref[2 * LANES :]
                )
                part = geo[pair * 2 + which]
                first = fields[0, pair, :planes, at]
                second = fields[1, pair, :planes, at]
                partial[comp, pair, :, at] = slopes[:, :LANES] * (first * part[0:1] + second * part[2:3]) + slopes[
                    :, LANES:
                ] * (first * part[1:2] + second * part[3:4])

        def advect(comp, pair, along):
            result = partial[comp, pair] + along * fields[comp, pair, planes:]
            turned[pair] = mm(backward_ref[...], stacked_values(result))

        def first_advect(pair):
            along = mm(forward_ref[:planes], stacked_values(store[pair]))
            fields[comps - 1, pair, :planes] = along
            advect(0, pair, along)

        def turn_back(comp):
            for part in range(count):
                block = jnp.concatenate(
                    [
                        turned[local // 2, part * rows : (part + 1) * rows, local % 2 * LANES : (local % 2 + 1) * LANES]
                        for local in range(per)
                    ],
                    axis=0,
                )
                hats[comp, part] = block.T[:points]

        def lift(comp):
            bit = lax.broadcasted_iota(jnp.int32, (EDGE, LANES), 1) // 8 % 2 == 0
            mine = me // group

            def one(step, carry):
                column = (mine // 2 + step // 2) % 2 * 2 + (mine + step) % 2
                fields_of = []
                for inner in range(group):
                    part = column * group + inner

                    @pl.when(part != me)
                    def _():
                        copy_from(hats, ret, 1, comp, part).wait_recv()

                    @pl.when(part == me)
                    def _():
                        ret[comp, part] = hats[comp, part]

                    value = sent[comp, part] - STEP_DT * ret[comp, part]
                    mid[comp, part] = value
                    fields_of.append(value)
                high, low = split(SIGMA_COEF * jnp.concatenate(fields_of, axis=1))
                both = mm(lift_high[...], high) + (mm(lift_high[...], low) + mm(lift_low[...], high))
                lifted = jnp.where(kinds[column, 0:1] > 0.5, both[EDGE:], both[:EDGE])
                for local in range(chunk):
                    even = lifted[:, 2 * local * LANES : (2 * local + 1) * LANES]
                    odd = lifted[:, (2 * local + 1) * LANES : (2 * local + 2) * LANES]
                    at = column * chunk + local
                    pieces[comp, 0, at] = jnp.where(bit, even, pltpu.roll(odd, 8, 1))
                    pieces[comp, 1, at] = jnp.where(bit, pltpu.roll(even, LANES - 8, 1), odd)
                lifted_copy(comp, column, core).start()
                for local in range(chunk):
                    at = column * chunk + local
                    forcing[comp, core * tiles + at] = pieces[comp, core, at]
                return carry

            lax.fori_loop(0, columns, one, 0)

        def solve(comp):
            for column in range(columns):
                lifted_copy(comp, column, 1 - core).wait_recv()
            solve_rows(forcing.at[comp], facts, lam_ref[...], weights, state, image, traces.at[comp])
            for end in range(ends):
                trace_copy(comp, end, core).start()
            for at in range(tiles):
                found[comp, core, at] = traces[comp, core * tiles + at]

        def leave(comp, end):
            cut = nodes // 2 // LANES * LANES
            lanes = pl.ds(end * cut, (cut, nodes - cut)[end])
            return pltpu.make_async_copy(result.at[comp, :, lanes], out.at[comp, :, lanes], out_sem.at[comp, end])

        def recover(comp):
            bit = lax.broadcasted_iota(jnp.int32, (EDGE, LANES), 1) // 8 % 2 == 0
            for column in range(columns):
                if column == columns // 2:
                    leave(comp, 0).start()
                if column % (columns // ends) == 0:
                    trace_copy(comp, column // (columns // ends), 1 - core).wait_recv()
                edges = []
                for at in range(column * chunk, (column + 1) * chunk):
                    low_rows = found[comp, 0, at]
                    high_rows = found[comp, 1, at]
                    edges.append(jnp.where(bit, low_rows, pltpu.roll(high_rows, 8, 1)))
                    edges.append(jnp.where(bit, pltpu.roll(low_rows, LANES - 8, 1), high_rows))
                both = mm(recover_all[...], stacked_edges(jnp.concatenate(edges, axis=1)))
                node = jnp.where(kinds[column, 0:1] > 0.5, both[88 : 88 + points], both[:points])
                for inner in range(group):
                    part = column * group + inner
                    block = mid[comp, part] * factor[0:1] + node[:, inner * LANES : (inner + 1) * LANES]
                    block = jnp.concatenate([block, jnp.zeros((LANES - points, LANES), F32)], axis=0).T
                    for local in range(per):
                        start = element_at(part, local, group) * points
                        result[comp, :, start : start + points] = block[local * rows : (local + 1) * rows, :points]
            leave(comp, 1).start()

        def prepare():
            def place(row):
                return jnp.where(row < 32, row // 8 * QUAD + row % 8, (row - 32) * QUAD + 8)

            widen = (place(iota((EDGE, 4 * QUAD), 0)) == iota((EDGE, 4 * QUAD), 1)).astype(F32)
            widen_cols = (place(iota((4 * QUAD, EDGE), 1)) == iota((4 * QUAD, EDGE), 0)).astype(F32)
            recover_out[...] = jnp.zeros_like(recover_out)
            for which in range(2):
                at = which * EDGE
                mat_ref[at : at + EDGE] = exact(exact(widen, stiff_ref[:, which, :]), widen_cols)
                at = at + 2 * EDGE
                mat_ref[at : at + EDGE] = exact(exact(widen, mass_ref[:, which, :]), widen_cols)
                lift_ref[which * EDGE : (which + 1) * EDGE] = exact(widen, lift_in[:, which, :])
                recover_out[which * 88 : which * 88 + points] = exact(widen, recover_in[:, which, :]).T
            weights[...] = stacked_weights(mat_ref[...])
            recover_all[...] = stacked_weights(recover_out[...])
            high, low = split(lift_ref[...])
            lift_high[...] = high
            lift_low[...] = low
            is_second = (kind_ref[...] == 1).astype(F32)
            free_v = (1 - fixed_ref[:, 0, :]).astype(F32)
            free_h = (1 - fixed_ref[:, 1, :]).astype(F32)
            none = jnp.zeros((5, elems), F32)
            rest = [free_v[8:9], none[:1], free_h[8:9], none]
            table = jnp.concatenate([free_v[:8], free_h[:8]] + rest + [is_second] * 8 + [scale_ref[...]] * 8, axis=0)
            lane = iota((elems, half), 1)
            element = element_at(lane // LANES * 2 + lane // 8 % 2, lane % LANES // 16, group)
            placed = exact(table, (element == iota((elems, half), 0)).astype(F32))
            for at in range(tiles):
                facts_out[at] = placed[:, at * LANES : (at + 1) * LANES]
                facts[core * tiles + at] = placed[:, at * LANES : (at + 1) * LANES]
            lane = iota((elems, 2 * half), 1)
            element = element_at(lane // LANES, lane % LANES // rows, group)
            spread = (element == iota((elems, 2 * half), 0)).astype(F32)
            placed = exact(jnp.broadcast_to(is_second, (8, elems)), spread)
            width = 2 * half // columns
            for column in range(columns):
                kinds[column] = placed[:, column * width : (column + 1) * width]
            lane = iota((8, LANES), 1)
            lam_ref[...] = lam_of(me * rows + core * 8 + lane % 8)
            factor[...] = SIGMA_COEF / (SIGMA_COEF + lam_of(me * rows + lane % rows))
            geo[...] = jnp.zeros_like(geo)
            for part in range(count):

                @pl.when(me == part)
                def _():
                    for local in range(per):
                        at = element_at(part, local, group) * points
                        geo[local, 0:4, 0:points] = geo_ref[:, at : at + points]

        last = comps - 1
        loads[0].wait()
        pack(0)
        pl.semaphore_wait(barrier, count)
        start_all(sent, recv, 0, 0)
        for comp in range(1, comps):
            loads[comp].wait()
            pack(comp)
        prepare()
        facts_copy().start()
        for load in loads[comps:]:
            load.wait()
        for comp in range(last):
            follow_all(sent, recv, 0, comp + 1, comp)
            arrive_all(comp)
            over_pairs(functools.partial(synthesize, comp))
        for comp in range(last):
            over_pairs(functools.partial(derive, comp))
        arrive_all(last)
        for pair in range(pairs):
            first_advect(pair)
        turn_back(0)
        start_all(hats, ret, 1, 0)
        for comp in range(1, last):
            over_pairs(lambda pair, comp=comp: advect(comp, pair, fields[last, pair, :planes]))
            turn_back(comp)
            start_all(hats, ret, 1, comp)
        over_pairs(slope_last)
        over_pairs(functools.partial(derive, last))
        over_pairs(lambda pair: advect(last, pair, fields[last, pair, :planes]))
        turn_back(last)
        follow_all(hats, ret, 1, last, 0)
        facts_arrive()
        for comp in range(comps):
            lift(comp)
            if comp > 0:
                recover(comp - 1)
            solve(comp)
        recover(last)
        facts_copy().wait_send()
        for comp in range(comps):
            for column in range(columns):
                lifted_copy(comp, column, core).wait_send()
            for end in range(ends):
                trace_copy(comp, end, core).wait_send()

        def drain(step, carry):
            peer = peer_at(step)
            copy_to(sent, recv, 0, last, peer).wait_send()
            for comp in range(1, comps):
                copy_to(hats, ret, 1, comp, peer).wait_send()
            return carry

        lax.fori_loop(1, count, drain, 0)
        for comp in range(comps):
            for end in range(2):
                leave(comp, end).wait()

    message = (comps, count, points, LANES)
    operands = (velocity, geometry, kind, scale, dirichlet, stiffness, mass, lift_maps, recover_maps)
    operands = operands + (forward, backward, deriv)
    vmem = pl.BlockSpec(memory_space=pltpu.VMEM)
    anywhere = pl.BlockSpec(memory_space=pl.ANY)
    copies = comps * (columns + ends) + 1
    done = pl.pallas_call(
        kernel,
        in_specs=[anywhere] + [vmem] * 8 + [anywhere] * 3,
        out_specs=anywhere,
        out_shape=jax.ShapeDtypeStruct(velocity.shape, F32),
        scratch_shapes=[
            pltpu.VMEM(velocity.shape, F32),
            pltpu.VMEM(forward.shape, BF16),
            pltpu.VMEM(backward.shape, BF16),
            pltpu.VMEM(deriv.shape, BF16),
            pltpu.VMEM(velocity.shape, F32),
            pltpu.VMEM(message, F32),
            pltpu.VMEM((columns, 8, group * LANES), F32),
            pltpu.VMEM((8, LANES), F32),
            pltpu.VMEM((2 * 88, EDGE), F32),
        ]
        + [pltpu.VMEM(message, F32)] * 4
        + [
            pltpu.VMEM((pairs, planes, 2 * LANES), F32),
            pltpu.VMEM((pairs, planes, 2 * LANES), F32),
            pltpu.VMEM((comps, pairs, 2 * planes, 2 * LANES), F32),
            pltpu.VMEM((comps, pairs, planes, 2 * LANES), F32),
            pltpu.VMEM((comps, 2, tiles, EDGE, LANES), F32),
            pltpu.VMEM((comps, 2 * tiles, EDGE, LANES), F32),
            pltpu.VMEM((comps, 2 * tiles, EDGE, LANES), F32),
            pltpu.VMEM((comps, 2, tiles, EDGE, LANES), F32),
            pltpu.VMEM((tiles, 40, LANES), F32),
            pltpu.VMEM((2 * tiles, 40, LANES), F32),
            pltpu.VMEM((3, 3, 2 * tiles, 8, LANES), F32),
            pltpu.VMEM((3, 2 * tiles, 8, LANES), F32),
            pltpu.VMEM((per, 8, LANES), F32),
            pltpu.VMEM((2 * EDGE, points), F32),
            pltpu.VMEM((4 * EDGE, EDGE), F32),
            pltpu.VMEM((8, LANES), F32),
            pltpu.VMEM((4 * EDGE, LANES), BF16),
            pltpu.VMEM((2 * EDGE, points), BF16),
            pltpu.VMEM((2 * EDGE, points), BF16),
            pltpu.VMEM((2 * 88, LANES), BF16),
        ]
        + [
            pltpu.SemaphoreType.DMA((2, comps, count)),
            pltpu.SemaphoreType.DMA((2, comps, count)),
            pltpu.SemaphoreType.DMA((copies,)),
            pltpu.SemaphoreType.DMA((copies,)),
            pltpu.SemaphoreType.DMA((comps + 3,)),
            pltpu.SemaphoreType.DMA((comps, 2)),
        ],
        compiler_params=pltpu.CompilerParams(
            vmem_limit_bytes=60 * 1024 * 1024, collective_id=0, has_side_effects=True
        ),
        name="advect_and_solve",
    )(*operands)

    def hand_over(source, target, held, in_sem, out_sem):
        comes = [pltpu.make_async_copy(source.at[comp], held.at[comp], in_sem.at[comp]) for comp in range(comps)]
        goes = [pltpu.make_async_copy(held.at[comp], target.at[comp], out_sem.at[comp]) for comp in range(comps)]
        for come in comes:
            come.start()
        for come, go in zip(comes, goes):
            come.wait()
            go.start()
        for go in goes:
            go.wait()

    return pl.pallas_call(
        hand_over,
        in_specs=[anywhere],
        out_specs=anywhere,
        out_shape=jax.ShapeDtypeStruct(velocity.shape, F32),
        scratch_shapes=[
            pltpu.VMEM(velocity.shape, F32),
            pltpu.SemaphoreType.DMA((comps,)),
            pltpu.SemaphoreType.DMA((comps,)),
        ],
        compiler_params=pltpu.CompilerParams(vmem_limit_bytes=60 * 1024 * 1024),
        name="hand_over",
    )(done)


def fast_device(
    velocity,
    geometry,
    element_kind,
    element_scale,
    dirichlet,
    schur_stiffness,
    schur_mass,
    lift,
    recover,
):
    count = lax.axis_size("planes")
    return advect_and_solve(
        velocity,
        geometry,
        element_kind[None],
        element_scale[None],
        dirichlet.swapaxes(0, 1),
        schur_stiffness.swapaxes(0, 1),
        schur_mass.swapaxes(0, 1),
        lift.swapaxes(0, 1),
        recover.transpose(2, 0, 1),
        count,
    )


def per_device(velocity, geometry, element_kind, *rest):
    count = lax.axis_size("planes")
    rows = velocity.shape[1]
    elems = element_kind.shape[0]
    fits = count & (count - 1) == 0 and rows == 16 and elems == LANES and elems * rows == count * LANES and lax.axis_size("elem") == 2
    body = fast_device if fits else plain_device
    return body(velocity, geometry, element_kind, *rest)


def solution(mesh):
    in_specs = (
        P(None, "planes", "elem"),
        P(None, "elem"),
        P("elem"),
        P("elem"),
        P(None, None, "elem"),
        P(),
        P(),
        P(),
        P(),
    )
    out_specs = P(None, "planes", "elem")
    return jax.shard_map(
        per_device, mesh=mesh, in_specs=in_specs, out_specs=out_specs, check_vma=False
    )
```

```python
import functools
import math

import jax
import jax.numpy as jnp
import numpy as np
from jax import lax
from jax.experimental import pallas as pl
from jax.experimental.pallas import tpu as pltpu
from jax.sharding import PartitionSpec as P

PLANES = 256
QUAD = 9
COLUMN_ELEMS = 32
CG_STEPS = 4


HIGHEST = lax.Precision.HIGHEST
SIGMA_COEF = 1.0
BETA_COEF = 0.01
STEP_DT = 0.002


def passed_along(value, axis, steps):
    count = lax.axis_size(axis)
    leading, last = (max(0, -steps), min(count, count - steps))
    return lax.ppermute(value, axis, [(source, source + steps) for source in range(leading, last)])


def gauss_derivative(points):
    nodes = -np.cos(np.pi * (2 * np.arange(points) + 1) / (2 * points))
    ident = np.eye(points)
    diffs = nodes[:, None] - nodes[None, :] + ident
    weights = 1.0 / np.prod(diffs, axis=1)
    matrix = weights[None, :] / weights[:, None] / diffs
    matrix = matrix * (1.0 - ident)
    return matrix - ident * matrix.sum(axis=1)[:, None]


def kron_tables():
    deriv = gauss_derivative(QUAD)
    identity = np.eye(QUAD)
    return (
        jnp.asarray(np.kron(deriv, identity), jnp.float32),
        jnp.asarray(np.kron(identity, deriv), jnp.float32),
    )


def fourier_tables(planes):
    zeta = jnp.arange(planes, dtype=jnp.int32)
    rows = jnp.arange(planes, dtype=jnp.int32)
    waves = (rows + 1) // 2
    phase = waves[None, :] * zeta[:, None] % planes
    angle = 2.0 * math.pi / planes * phase.astype(jnp.float32)
    cosine = jnp.cos(angle)
    sine = jnp.sin(angle)
    odd = (rows % 2 == 1)[None, :]
    first = (rows == 0)[None, :]
    last = (rows == planes - 1)[None, :]
    synth = jnp.where(first, 1.0, jnp.where(odd, cosine, sine))
    rate = BETA_COEF * waves.astype(jnp.float32)[None, :]
    slope = jnp.where(first | last, 0.0, jnp.where(odd, -rate * sine, rate * cosine))
    weight = jnp.where((rows == 0) | (rows == planes - 1), 1.0 / planes, 2.0 / planes).astype(
        jnp.float32
    )
    analysis = synth.T * weight[:, None]
    return (synth, slope, analysis)


def inner(first_pair, second_pair):
    return jnp.sum(first_pair[0] * second_pair[0], axis=(0, 2)) + jnp.sum(
        first_pair[1] * second_pair[1], axis=(0, 2)
    )


def global_total(first_pair, second_pair):
    return lax.psum(inner(first_pair, second_pair), "elem")


def global_squares(pair):
    return lax.psum(inner(pair, pair), "elem")


def assemble(outputs, incoming, free):
    left = outputs[:QUAD]
    right = outputs[QUAD : 2 * QUAD]
    bottom = outputs[2 * QUAD : 3 * QUAD]
    top = outputs[3 * QUAD :]
    vertical = left + jnp.concatenate([incoming, right[:, :, :-COLUMN_ELEMS]], axis=2)
    grid = top.reshape(top.shape[0], top.shape[1], -1, COLUMN_ELEMS)
    shifted = jnp.concatenate([jnp.zeros_like(grid[..., :1]), grid[..., :-1]], axis=3).reshape(
        bottom.shape
    )
    horizontal = bottom + shifted
    return (vertical * free[0], horizontal * free[1])


def plain_device(
    velocity,
    geometry,
    element_kind,
    element_scale,
    dirichlet,
    schur_stiffness,
    schur_mass,
    lift,
    recover,
):
    first, second = kron_tables()
    synth, slope, analysis = fourier_tables(PLANES)
    local_rows = velocity.shape[1]
    node_count = velocity.shape[2]
    share = node_count // lax.axis_size("planes")
    geo_part = lax.dynamic_slice_in_dim(geometry, lax.axis_index("planes") * share, share, 1)

    def transform(table, field):
        return jnp.einsum("zr,crm->czm", table, field, precision=HIGHEST)

    items = lax.all_to_all(velocity, "planes", split_axis=2, concat_axis=1, tiled=True)
    values = transform(synth, items)
    along_z = transform(slope, items)
    shaped = values.reshape(values.shape[:-1] + (-1, QUAD * QUAD))
    along_r = jnp.einsum("...en,mn->...em", shaped, first, precision=HIGHEST).reshape(values.shape)
    along_s = jnp.einsum("...en,mn->...em", shaped, second, precision=HIGHEST).reshape(values.shape)
    along_x = geo_part[0] * along_r + geo_part[1] * along_s
    along_y = geo_part[2] * along_r + geo_part[3] * along_s
    values, along_x, along_y, along_z = (values, along_x, along_y, along_z)
    advection = values[0] * along_x + values[1] * along_y + values[2] * along_z
    advection_hat = jnp.einsum("rz,czm->crm", analysis, advection, precision=HIGHEST)
    returned = lax.all_to_all(advection_hat, "planes", split_axis=1, concat_axis=2, tiled=True)
    intermediate = velocity - STEP_DT * returned
    elem_count = element_kind.shape[0]
    row_count = 3 * local_rows
    waves = (
        (lax.axis_index("planes") * local_rows + jnp.arange(local_rows, dtype=jnp.int32) + 1) // 2
    ).astype(jnp.float32)
    lam = jnp.tile(SIGMA_COEF + (BETA_COEF * waves) ** 2, 3)
    free = (1 - dirichlet).astype(jnp.float32)[:, :, None, :]
    chooser = (element_kind == 1).astype(jnp.float32)

    def element_apply(vector, kinds, scales):
        flat = vector.reshape(vector.shape[0], -1)
        results = []
        for kind in range(2):
            stiff = jnp.dot(schur_stiffness[kind], flat, precision=HIGHEST).reshape(vector.shape)
            massed = jnp.dot(schur_mass[kind], flat, precision=HIGHEST).reshape(vector.shape)
            results.append(stiff + lam[None, :, None] * massed)
        return scales[None, None, :] * jnp.where(kinds[None, None, :] > 0.5, results[1], results[0])

    def element_vector(vertical, horizontal):
        arriving = passed_along(vertical[:, :, :COLUMN_ELEMS], "elem", -1)
        right = jnp.concatenate([vertical[:, :, COLUMN_ELEMS:], arriving], axis=2)
        grid = horizontal.reshape(horizontal.shape[0], horizontal.shape[1], -1, COLUMN_ELEMS)
        top = jnp.concatenate([grid[..., 1:], jnp.zeros_like(grid[..., :1])], axis=3).reshape(
            horizontal.shape
        )
        return jnp.concatenate([vertical, right, horizontal, top], axis=0)

    node_values = (SIGMA_COEF * intermediate).reshape(row_count, elem_count, QUAD * QUAD)
    lifted = jnp.where(
        chooser[None, None, :] > 0.5,
        jnp.einsum("kn,ren->kre", lift[1], node_values, precision=HIGHEST),
        jnp.einsum("kn,ren->kre", lift[0], node_values, precision=HIGHEST),
    )
    lifted_right = passed_along(lifted[QUAD : 2 * QUAD, :, -COLUMN_ELEMS:], "elem", 1)
    forcing = assemble(lifted, lifted_right, free)
    trace = (jnp.zeros_like(forcing[0]), jnp.zeros_like(forcing[1]))
    residual = forcing
    direction = forcing
    norm_now = global_squares(residual)
    for sweep in range(CG_STEPS):
        outputs = element_apply(element_vector(direction[0], direction[1]), chooser, element_scale)
        operator_arriving = passed_along(outputs[QUAD : 2 * QUAD, :, -COLUMN_ELEMS:], "elem", 1)
        image = assemble(outputs, operator_arriving, free)
        alpha = (norm_now / global_total(direction, image))[None, :, None]
        trace = (trace[0] + alpha * direction[0], trace[1] + alpha * direction[1])
        residual = (residual[0] - alpha * image[0], residual[1] - alpha * image[1])
        norm_next = global_squares(residual)
        ratio = (norm_next / norm_now)[None, :, None]
        direction = (residual[0] + ratio * direction[0], residual[1] + ratio * direction[1])
        norm_now = norm_next
    vector = element_vector(trace[0], trace[1])
    recovered = jnp.where(
        chooser[None, :, None] > 0.5,
        jnp.einsum("nl,lre->ren", recover[1], vector, precision=HIGHEST),
        jnp.einsum("nl,lre->ren", recover[0], vector, precision=HIGHEST),
    )
    weight = SIGMA_COEF / (SIGMA_COEF + lam)
    result = (
        intermediate.reshape(row_count, elem_count, QUAD * QUAD) * weight[:, None, None] + recovered
    )
    return result.reshape(velocity.shape)


LANES = 128
EDGE = 40
F32 = jnp.float32
BF16 = jnp.bfloat16


def split(value):
    high = value.astype(BF16)
    return high, (value - high.astype(F32)).astype(BF16)


def np_split(value):
    high = np.asarray(value, np.float32).astype(BF16)
    low = (np.asarray(value, np.float64) - high.astype(np.float64)).astype(np.float32).astype(BF16)
    return high, low


def mm(first, second):
    return jnp.dot(first, second, preferred_element_type=F32)


def stacked_values(values):
    high, low = split(values)
    return jnp.concatenate([high, low, high], axis=0)


def advect_tables(planes):
    zeta = np.arange(planes)
    rows = np.arange(planes)
    waves = (rows + 1) // 2
    angle = 2.0 * np.pi / planes * ((waves[None, :] * zeta[:, None]) % planes)
    odd = (rows % 2 == 1)[None, :]
    first = (rows == 0)[None, :]
    last = (rows == planes - 1)[None, :]
    synth = np.where(first, 1.0, np.where(odd, np.cos(angle), np.sin(angle)))
    rate = BETA_COEF * waves[None, :]
    slope = np.where(first | last, 0.0, np.where(odd, -rate * np.sin(angle), rate * np.cos(angle)))
    weight = np.where((rows == 0) | (rows == planes - 1), 1.0 / planes, 2.0 / planes)
    analysis = synth.T * weight[:, None]
    high, low = np_split(np.concatenate([synth, slope], axis=0))
    forward = np.concatenate([high, high, low], axis=1)
    high, low = np_split(analysis)
    backward = np.concatenate([high, high, low], axis=1)
    points = QUAD * QUAD
    deriv = gauss_derivative(QUAD)
    both = np.zeros((LANES, 2 * LANES))
    both[:points, :points] = np.kron(deriv, np.eye(QUAD)).T
    both[:points, LANES : LANES + points] = np.kron(np.eye(QUAD), deriv).T
    high, low = np_split(both)
    return jnp.asarray(forward), jnp.asarray(backward), jnp.asarray(np.concatenate([high, high, low], axis=0))


def whole_spec(shape):
    return pl.BlockSpec(shape, lambda *_: (0,) * len(shape))


def params():
    return pltpu.CompilerParams(vmem_limit_bytes=60 * 1024 * 1024)


def element_at(part, slot, group):
    inner = part % group
    return part // group * COLUMN_ELEMS + slot * group + inner % 2 * (group // 2) + inner // 2


def stacked_weights(weights):
    high, low = split(weights)
    pad = jnp.zeros((weights.shape[0], LANES - 3 * EDGE), BF16)
    return jnp.concatenate([high, high, low, pad], axis=1)


def stacked_edges(value):
    high = value.astype(BF16).astype(F32)
    pad = jnp.zeros((LANES - 3 * EDGE, value.shape[1]), F32)
    return jnp.concatenate([high, value - high, high, pad], axis=0).astype(BF16)


def tree(terms):
    while len(terms) > 1:
        terms = [terms[at] + terms[at + 1] for at in range(0, len(terms), 2)]
    return terms[0]


def solve_rows(forcing, facts, lam, weights, state, image, traces):
    tiles = forcing.shape[0]
    lane = lax.broadcasted_iota(jnp.int32, (8, LANES), 1)
    sub = lax.broadcasted_iota(jnp.int32, (8, LANES), 0)
    top_edge = lane >= LANES - 8
    low_edge = lane < 8
    zero = jnp.zeros((8, LANES), F32)
    lam = jnp.concatenate([lam] * (EDGE // 8), axis=0)

    def above(tile_of, at):
        if at % 2 == 0:
            return tile_of(at + 1)
        return jnp.where(top_edge, 0.0, pltpu.roll(tile_of(at - 1), LANES - 8, 1))

    def below(tile_of, at):
        if at % 2 == 1:
            return tile_of(at - 1)
        return jnp.where(low_edge, 0.0, pltpu.roll(tile_of(at + 1), 8, 1))

    def edges(tile_of, at):
        beside = at + 2 < tiles
        right = tile_of(0, at + 2) if beside else zero
        right_rest = tile_of(2, at + 2) if beside else zero
        top = above(lambda item: tile_of(1, item), at)
        top_rest = above(lambda item: tile_of(2, item), at)
        rest = jnp.where(sub == 0, right_rest, jnp.where(sub == 2, top_rest, 0.0))
        rest = tile_of(2, at) + pltpu.roll(rest, 1, 0)
        return jnp.concatenate([tile_of(0, at), right, tile_of(1, at), top, rest], axis=0)

    def gather(parts, at):
        part = parts[at]
        fact = facts[at]
        left = part[:8]
        rest = below(lambda item: parts[item][32:40], at)
        if at >= 2:
            left = left + parts[at - 2][8:16]
            rest = jnp.where(sub == 1, parts[at - 2][32:40], jnp.where(sub == 3, rest, 0.0))
        else:
            rest = jnp.where(sub == 3, rest, 0.0)
        rest = part[32:40] + pltpu.roll(rest, 7, 0)
        bottom = part[16:24] + below(lambda item: parts[item][24:32], at)
        return left * fact[:8], bottom * fact[8:16], rest * fact[16:24]

    def total(acc):
        acc = tree([acc] + [pltpu.roll(acc, 8 * step, 1) for step in range(1, LANES // 8)])
        return tree([acc] + [pltpu.roll(acc, step, 0) for step in range(1, 8)])

    def apply():
        sums = [zero, zero, zero]
        parts = []
        for first in range(0, tiles, 2):
            both = jnp.concatenate([edges(lambda which, item: state[2, which, item], at) for at in (first, first + 1)], axis=1)
            both = mm(weights[...], stacked_edges(both))
            for at in (first, first + 1):
                lanes = slice((at - first) * LANES, (at - first + 1) * LANES)
                fact = facts[at]
                is_second = jnp.concatenate([fact[24:32]] * (EDGE // 8), axis=0) > 0.5
                scale = jnp.concatenate([fact[32:40]] * (EDGE // 8), axis=0)
                stiff = jnp.where(is_second, both[EDGE : 2 * EDGE, lanes], both[:EDGE, lanes])
                mass = jnp.where(is_second, both[3 * EDGE :, lanes], both[2 * EDGE : 3 * EDGE, lanes])
                parts.append(scale * (stiff + lam * mass))
            for at in (first, first + 1):
                for which, value in enumerate(gather(parts, at)):
                    image[which, at] = value
                    sums[which] = sums[which] + state[2, which, at] * value
        return total(sums[0] + sums[1] + sums[2])

    sums = [zero, zero, zero]
    parts = {}
    for at in range(tiles):
        parts[at] = forcing[at]
    for at in range(tiles):
        for which, value in enumerate(gather(parts, at)):
            state[0, which, at] = zero
            state[1, which, at] = value
            state[2, which, at] = value
            sums[which] = sums[which] + value * value
    now = total(sums[0] + sums[1] + sums[2])

    def sweep(_, now):
        alpha = now / apply()
        sums = [zero, zero, zero]
        for at in range(tiles):
            for which in range(3):
                state[0, which, at] = state[0, which, at] + alpha * state[2, which, at]
                rest = state[1, which, at] - alpha * image[which, at]
                state[1, which, at] = rest
                sums[which] = sums[which] + rest * rest
        fresh = total(sums[0] + sums[1] + sums[2])
        ratio = fresh / now
        for at in range(tiles):
            for which in range(3):
                state[2, which, at] = state[1, which, at] + ratio * state[2, which, at]
        return fresh

    now = lax.fori_loop(0, CG_STEPS - 1, sweep, now)
    alpha = now / apply()
    found = [[state[0, which, at] + alpha * state[2, which, at] for at in range(tiles)] for which in range(3)]
    for at in range(tiles):
        traces[at] = edges(lambda which, item: found[which][item], at)


def exact(first, second):
    return jnp.dot(first, second, precision=HIGHEST, preferred_element_type=F32)


def iota(shape, axis):
    return lax.broadcasted_iota(jnp.int32, shape, axis)


def lam_of(row):
    return SIGMA_COEF + (BETA_COEF * ((row + 1) // 2).astype(F32)) ** 2


def advect_and_solve(velocity, geometry, kind, scale, dirichlet, stiffness, mass, lift_maps, recover_maps, count):
    elems = kind.shape[1]
    comps, rows, nodes = velocity.shape
    points = QUAD * QUAD
    per = LANES // rows
    pairs = per // 2
    planes = count * rows
    half = count * LANES // 2
    forward, backward, deriv = advect_tables(planes)

    group = COLUMN_ELEMS // per
    columns = count // group
    tiles = count // 2
    chunk = tiles // columns
    ends = 2

    def kernel(
        vel_in, geo_ref, kind_ref, scale_ref, fixed_ref, stiff_ref, mass_ref, lift_in, recover_in,
        forward_in, backward_in, deriv_in,
        out,
        vel_ref, forward_ref, backward_ref, deriv_ref, result,
        mid, kinds, factor, recover_out, sent, recv, hats, ret,
        store, turned, fields, partial, pieces, forcing, traces, found, facts_out, facts,
        state, image, geo, lift_ref, mat_ref, lam_ref, weights, lift_high, lift_low, recover_all,
        send_sem, recv_sem, pair_send, pair_recv, load_sem, out_sem,
    ):
        loads = [pltpu.make_async_copy(vel_in.at[comp], vel_ref.at[comp], load_sem.at[comp]) for comp in range(comps)]
        tables = ((forward_in, forward_ref), (deriv_in, deriv_ref), (backward_in, backward_ref))
        for at, (source, target) in enumerate(tables):
            loads.append(pltpu.make_async_copy(source, target, load_sem.at[comps + at]))
        for load in loads:
            load.start()
        me = lax.axis_index("planes")
        core = lax.axis_index("elem")
        barrier = pltpu.get_barrier_semaphore()

        def peer_at(step):
            return (me + step) % count

        def source_at(step):
            return (me + count - step) % count

        def greet(step, carry):
            pl.semaphore_signal(
                barrier, inc=1, device_id={"planes": peer_at(step)}, device_id_type=pl.DeviceIdType.MESH
            )
            return carry

        lax.fori_loop(1, count, greet, 0)
        pl.semaphore_signal(barrier, inc=1, device_id={"elem": 1 - core}, device_id_type=pl.DeviceIdType.MESH)

        def copy_to(source, target, way, comp, peer):
            return pltpu.make_async_remote_copy(
                src_ref=source.at[comp, peer],
                dst_ref=target.at[comp, me],
                send_sem=send_sem.at[way, comp, peer],
                recv_sem=recv_sem.at[way, comp, me],
                device_id={"planes": peer},
                device_id_type=pl.DeviceIdType.MESH,
            )

        def copy_from(source, target, way, comp, peer):
            return pltpu.make_async_remote_copy(
                src_ref=source.at[comp, peer],
                dst_ref=target.at[comp, peer],
                send_sem=send_sem.at[way, comp, peer],
                recv_sem=recv_sem.at[way, comp, peer],
                device_id={"planes": peer},
                device_id_type=pl.DeviceIdType.MESH,
            )

        def start_all(source, target, way, comp):
            def one(step, carry):
                copy_to(source, target, way, comp, peer_at(step)).start()
                return carry

            lax.fori_loop(1, count, one, 0)

        def follow_all(source, target, way, comp, before):
            def one(step, carry):
                peer = peer_at(step)
                copy_to(source, target, way, before, peer).wait_send()
                copy_to(source, target, way, comp, peer).start()
                return carry

            lax.fori_loop(1, count, one, 0)

        def pair_copy(source, target, at):
            return pltpu.make_async_remote_copy(
                src_ref=source,
                dst_ref=target,
                send_sem=pair_send.at[at],
                recv_sem=pair_recv.at[at],
                device_id={"elem": 1 - core},
                device_id_type=pl.DeviceIdType.MESH,
            )

        def facts_copy():
            return pair_copy(facts_out, facts.at[pl.ds(core * tiles, tiles)], comps * (columns + ends))

        def facts_arrive():
            pair_copy(facts_out, facts.at[pl.ds((1 - core) * tiles, tiles)], comps * (columns + ends)).wait_recv()

        def lifted_copy(comp, column, side):
            return pair_copy(
                pieces.at[comp, 1 - core, pl.ds(column * chunk, chunk)],
                forcing.at[comp, pl.ds(side * tiles + column * chunk, chunk)],
                comp * columns + column,
            )

        def trace_copy(comp, end, side):
            width = tiles // ends
            return pair_copy(
                traces.at[comp, pl.ds((1 - core) * tiles + end * width, width)],
                found.at[comp, side, pl.ds(end * width, width)],
                comps * columns + comp * ends + end,
            )

        def pack(comp):
            for part in range(count):
                rows_of = []
                for local in range(per):
                    at = element_at(part, local, group) * points
                    rows_of.append(vel_ref[comp, :, at : at + points])
                sent[comp, part] = jnp.concatenate(rows_of, axis=0).T

        def arrive(comp, part, block):
            block = jnp.concatenate([block, jnp.zeros((LANES - points, LANES), F32)], axis=0).T
            for local in range(per):
                at = local % 2 * LANES
                store[local // 2, pl.ds(pl.multiple_of(part * rows, rows), rows), at : at + LANES] = block[
                    local * rows : (local + 1) * rows
                ]

        def arrive_all(comp):
            arrive(comp, me, sent[comp, me])

            def one(step, carry):
                for inner in range(several):
                    part = source_at(1 + step * several + inner)
                    copy_from(sent, recv, 0, comp, part).wait_recv()
                    arrive(comp, part, recv[comp, part])
                return carry

            several = 3 if (count - 1) % 3 == 0 else 1
            lax.fori_loop(0, (count - 1) // several, one, 0)

        def over_pairs(body):
            def one(pair, carry):
                body(pair)
                return carry

            lax.fori_loop(0, pairs, one, 0)

        def synthesize(comp, pair):
            fields[comp, pair] = mm(forward_ref[...], stacked_values(store[pair]))

        def slope_last(pair):
            fields[comps - 1, pair, planes:] = mm(forward_ref[planes:], stacked_values(store[pair]))

        def derive(comp, pair):
            for which in range(2):
                at = slice(which * LANES, (which + 1) * LANES)
                high, low = split(fields[comp, pair, :planes, at])
                slopes = mm(jnp.concatenate([high, low], axis=1), deriv_ref[: 2 * LANES]) + mm(
                    high, deriv_ref[2 * LANES :]
                )
                part = geo[pair * 2 + which]
                first = fields[0, pair, :planes, at]
                second = fields[1, pair, :planes, at]
                partial[comp, pair, :, at] = slopes[:, :LANES] * (first * part[0:1] + second * part[2:3]) + slopes[
                    :, LANES:
                ] * (first * part[1:2] + second * part[3:4])

        def advect(comp, pair, along):
            result = partial[comp, pair] + along * fields[comp, pair, planes:]
            turned[pair] = mm(backward_ref[...], stacked_values(result))

        def first_advect(pair):
            along = mm(forward_ref[:planes], stacked_values(store[pair]))
            fields[comps - 1, pair, :planes] = along
            advect(0, pair, along)

        def turn_back(comp):
            for part in range(count):
                block = jnp.concatenate(
                    [
                        turned[local // 2, part * rows : (part + 1) * rows, local % 2 * LANES : (local % 2 + 1) * LANES]
                        for local in range(per)
                    ],
                    axis=0,
                )
                hats[comp, part] = block.T[:points]

        def lift(comp):
            bit = lax.broadcasted_iota(jnp.int32, (EDGE, LANES), 1) // 8 % 2 == 0
            mine = me // group

            def one(step, carry):
                column = (mine // 2 + step // 2) % 2 * 2 + (mine + step) % 2
                fields_of = []
                for inner in range(group):
                    part = column * group + inner

                    @pl.when(part != me)
                    def _():
                        copy_from(hats, ret, 1, comp, part).wait_recv()

                    @pl.when(part == me)
                    def _():
                        ret[comp, part] = hats[comp, part]

                    value = sent[comp, part] - STEP_DT * ret[comp, part]
                    mid[comp, part] = value
                    fields_of.append(value)
                high, low = split(SIGMA_COEF * jnp.concatenate(fields_of, axis=1))
                both = mm(lift_high[...], high) + (mm(lift_high[...], low) + mm(lift_low[...], high))
                lifted = jnp.where(kinds[column, 0:1] > 0.5, both[EDGE:], both[:EDGE])
                for local in range(chunk):
                    even = lifted[:, 2 * local * LANES : (2 * local + 1) * LANES]
                    odd = lifted[:, (2 * local + 1) * LANES : (2 * local + 2) * LANES]
                    at = column * chunk + local
                    pieces[comp, 0, at] = jnp.where(bit, even, pltpu.roll(odd, 8, 1))
                    pieces[comp, 1, at] = jnp.where(bit, pltpu.roll(even, LANES - 8, 1), odd)
                lifted_copy(comp, column, core).start()
                for local in range(chunk):
                    at = column * chunk + local
                    forcing[comp, core * tiles + at] = pieces[comp, core, at]
                return carry

            lax.fori_loop(0, columns, one, 0)

        def solve(comp):
            for column in range(columns):
                lifted_copy(comp, column, 1 - core).wait_recv()
            solve_rows(forcing.at[comp], facts, lam_ref[...], weights, state, image, traces.at[comp])
            for end in range(ends):
                trace_copy(comp, end, core).start()
            for at in range(tiles):
                found[comp, core, at] = traces[comp, core * tiles + at]

        def leave(comp, end):
            cut = nodes // 2 // LANES * LANES
            lanes = pl.ds(end * cut, (cut, nodes - cut)[end])
            return pltpu.make_async_copy(result.at[comp, :, lanes], out.at[comp, :, lanes], out_sem.at[comp, end])

        def recover(comp):
            bit = lax.broadcasted_iota(jnp.int32, (EDGE, LANES), 1) // 8 % 2 == 0
            for column in range(columns):
                if column == columns // 2:
                    leave(comp, 0).start()
                if column % (columns // ends) == 0:
                    trace_copy(comp, column // (columns // ends), 1 - core).wait_recv()
                edges = []
                for at in range(column * chunk, (column + 1) * chunk):
                    low_rows = found[comp, 0, at]
                    high_rows = found[comp, 1, at]
                    edges.append(jnp.where(bit, low_rows, pltpu.roll(high_rows, 8, 1)))
                    edges.append(jnp.where(bit, pltpu.roll(low_rows, LANES - 8, 1), high_rows))
                both = mm(recover_all[...], stacked_edges(jnp.concatenate(edges, axis=1)))
                node = jnp.where(kinds[column, 0:1] > 0.5, both[88 : 88 + points], both[:points])
                for inner in range(group):
                    part = column * group + inner
                    block = mid[comp, part] * factor[0:1] + node[:, inner * LANES : (inner + 1) * LANES]
                    block = jnp.concatenate([block, jnp.zeros((LANES - points, LANES), F32)], axis=0).T
                    for local in range(per):
                        start = element_at(part, local, group) * points
                        result[comp, :, start : start + points] = block[local * rows : (local + 1) * rows, :points]
            leave(comp, 1).start()

        def prepare():
            def place(row):
                return jnp.where(row < 32, row // 8 * QUAD + row % 8, (row - 32) * QUAD + 8)

            widen = (place(iota((EDGE, 4 * QUAD), 0)) == iota((EDGE, 4 * QUAD), 1)).astype(F32)
            widen_cols = (place(iota((4 * QUAD, EDGE), 1)) == iota((4 * QUAD, EDGE), 0)).astype(F32)
            recover_out[...] = jnp.zeros_like(recover_out)
            for which in range(2):
                at = which * EDGE
                mat_ref[at : at + EDGE] = exact(exact(widen, stiff_ref[:, which, :]), widen_cols)
                at = at + 2 * EDGE
                mat_ref[at : at + EDGE] = exact(exact(widen, mass_ref[:, which, :]), widen_cols)
                lift_ref[which * EDGE : (which + 1) * EDGE] = exact(widen, lift_in[:, which, :])
                recover_out[which * 88 : which * 88 + points] = exact(widen, recover_in[:, which, :]).T
            weights[...] = stacked_weights(mat_ref[...])
            recover_all[...] = stacked_weights(recover_out[...])
            high, low = split(lift_ref[...])
            lift_high[...] = high
            lift_low[...] = low
            is_second = (kind_ref[...] == 1).astype(F32)
            free_v = (1 - fixed_ref[:, 0, :]).astype(F32)
            free_h = (1 - fixed_ref[:, 1, :]).astype(F32)
            none = jnp.zeros((5, elems), F32)
            rest = [free_v[8:9], none[:1], free_h[8:9], none]
            table = jnp.concatenate([free_v[:8], free_h[:8]] + rest + [is_second] * 8 + [scale_ref[...]] * 8, axis=0)
            lane = iota((elems, half), 1)
            element = element_at(lane // LANES * 2 + lane // 8 % 2, lane % LANES // 16, group)
            placed = exact(table, (element == iota((elems, half), 0)).astype(F32))
            for at in range(tiles):
                facts_out[at] = placed[:, at * LANES : (at + 1) * LANES]
                facts[core * tiles + at] = placed[:, at * LANES : (at + 1) * LANES]
            lane = iota((elems, 2 * half), 1)
            element = element_at(lane // LANES, lane % LANES // rows, group)
            spread = (element == iota((elems, 2 * half), 0)).astype(F32)
            placed = exact(jnp.broadcast_to(is_second, (8, elems)), spread)
            width = 2 * half // columns
            for column in range(columns):
                kinds[column] = placed[:, column * width : (column + 1) * width]
            lane = iota((8, LANES), 1)
            lam_ref[...] = lam_of(me * rows + core * 8 + lane % 8)
            factor[...] = SIGMA_COEF / (SIGMA_COEF + lam_of(me * rows + lane % rows))
            geo[...] = jnp.zeros_like(geo)
            for part in range(count):

                @pl.when(me == part)
                def _():
                    for local in range(per):
                        at = element_at(part, local, group) * points
                        geo[local, 0:4, 0:points] = geo_ref[:, at : at + points]

        last = comps - 1
        loads[0].wait()
        pack(0)
        pl.semaphore_wait(barrier, count)
        start_all(sent, recv, 0, 0)
        for comp in range(1, comps):
            loads[comp].wait()
            pack(comp)
            start_all(sent, recv, 0, comp)
        prepare()
        facts_copy().start()
        for load in loads[comps:]:
            load.wait()
        for comp in range(last):
            arrive_all(comp)
            over_pairs(functools.partial(synthesize, comp))
        for comp in range(last):
            over_pairs(functools.partial(derive, comp))
        arrive_all(last)
        for pair in range(pairs):
            first_advect(pair)
        turn_back(0)
        start_all(hats, ret, 1, 0)
        for comp in range(1, last):
            over_pairs(lambda pair, comp=comp: advect(comp, pair, fields[last, pair, :planes]))
            turn_back(comp)
            start_all(hats, ret, 1, comp)
        over_pairs(slope_last)
        over_pairs(functools.partial(derive, last))
        over_pairs(lambda pair: advect(last, pair, fields[last, pair, :planes]))
        turn_back(last)
        follow_all(hats, ret, 1, last, 0)
        facts_arrive()
        for comp in range(comps):
            lift(comp)
            if comp > 0:
                recover(comp - 1)
            solve(comp)
        recover(last)
        facts_copy().wait_send()
        for comp in range(comps):
            for column in range(columns):
                lifted_copy(comp, column, core).wait_send()
            for end in range(ends):
                trace_copy(comp, end, core).wait_send()

        def drain(step, carry):
            peer = peer_at(step)
            for comp in range(comps):
                copy_to(sent, recv, 0, comp, peer).wait_send()
            for comp in range(1, comps):
                copy_to(hats, ret, 1, comp, peer).wait_send()
            return carry

        lax.fori_loop(1, count, drain, 0)
        for comp in range(comps):
            for end in range(2):
                leave(comp, end).wait()

    message = (comps, count, points, LANES)
    operands = (velocity, geometry, kind, scale, dirichlet, stiffness, mass, lift_maps, recover_maps)
    operands = operands + (forward, backward, deriv)
    vmem = pl.BlockSpec(memory_space=pltpu.VMEM)
    anywhere = pl.BlockSpec(memory_space=pl.ANY)
    copies = comps * (columns + ends) + 1
    done = pl.pallas_call(
        kernel,
        in_specs=[anywhere] + [vmem] * 8 + [anywhere] * 3,
        out_specs=anywhere,
        out_shape=jax.ShapeDtypeStruct(velocity.shape, F32),
        scratch_shapes=[
            pltpu.VMEM(velocity.shape, F32),
            pltpu.VMEM(forward.shape, BF16),
            pltpu.VMEM(backward.shape, BF16),
            pltpu.VMEM(deriv.shape, BF16),
            pltpu.VMEM(velocity.shape, F32),
            pltpu.VMEM(message, F32),
            pltpu.VMEM((columns, 8, group * LANES), F32),
            pltpu.VMEM((8, LANES), F32),
            pltpu.VMEM((2 * 88, EDGE), F32),
        ]
        + [pltpu.VMEM(message, F32)] * 4
        + [
            pltpu.VMEM((pairs, planes, 2 * LANES), F32),
            pltpu.VMEM((pairs, planes, 2 * LANES), F32),
            pltpu.VMEM((comps, pairs, 2 * planes, 2 * LANES), F32),
            pltpu.VMEM((comps, pairs, planes, 2 * LANES), F32),
            pltpu.VMEM((comps, 2, tiles, EDGE, LANES), F32),
            pltpu.VMEM((comps, 2 * tiles, EDGE, LANES), F32),
            pltpu.VMEM((comps, 2 * tiles, EDGE, LANES), F32),
            pltpu.VMEM((comps, 2, tiles, EDGE, LANES), F32),
            pltpu.VMEM((tiles, 40, LANES), F32),
            pltpu.VMEM((2 * tiles, 40, LANES), F32),
            pltpu.VMEM((3, 3, 2 * tiles, 8, LANES), F32),
            pltpu.VMEM((3, 2 * tiles, 8, LANES), F32),
            pltpu.VMEM((per, 8, LANES), F32),
            pltpu.VMEM((2 * EDGE, points), F32),
            pltpu.VMEM((4 * EDGE, EDGE), F32),
            pltpu.VMEM((8, LANES), F32),
            pltpu.VMEM((4 * EDGE, LANES), BF16),
            pltpu.VMEM((2 * EDGE, points), BF16),
            pltpu.VMEM((2 * EDGE, points), BF16),
            pltpu.VMEM((2 * 88, LANES), BF16),
        ]
        + [
            pltpu.SemaphoreType.DMA((2, comps, count)),
            pltpu.SemaphoreType.DMA((2, comps, count)),
            pltpu.SemaphoreType.DMA((copies,)),
            pltpu.SemaphoreType.DMA((copies,)),
            pltpu.SemaphoreType.DMA((comps + 3,)),
            pltpu.SemaphoreType.DMA((comps, 2)),
        ],
        compiler_params=pltpu.CompilerParams(
            vmem_limit_bytes=60 * 1024 * 1024, collective_id=0, has_side_effects=True
        ),
        name="advect_and_solve",
    )(*operands)

    def hand_over(source, target, held, in_sem, out_sem):
        comes = [pltpu.make_async_copy(source.at[comp], held.at[comp], in_sem.at[comp]) for comp in range(comps)]
        goes = [pltpu.make_async_copy(held.at[comp], target.at[comp], out_sem.at[comp]) for comp in range(comps)]
        for come in comes:
            come.start()
        for come, go in zip(comes, goes):
            come.wait()
            go.start()
        for go in goes:
            go.wait()

    return pl.pallas_call(
        hand_over,
        in_specs=[anywhere],
        out_specs=anywhere,
        out_shape=jax.ShapeDtypeStruct(velocity.shape, F32),
        scratch_shapes=[
            pltpu.VMEM(velocity.shape, F32),
            pltpu.SemaphoreType.DMA((comps,)),
            pltpu.SemaphoreType.DMA((comps,)),
        ],
        compiler_params=pltpu.CompilerParams(vmem_limit_bytes=60 * 1024 * 1024),
        name="hand_over",
    )(done)


def fast_device(
    velocity,
    geometry,
    element_kind,
    element_scale,
    dirichlet,
    schur_stiffness,
    schur_mass,
    lift,
    recover,
):
    count = lax.axis_size("planes")
    return advect_and_solve(
        velocity,
        geometry,
        element_kind[None],
        element_scale[None],
        dirichlet.swapaxes(0, 1),
        schur_stiffness.swapaxes(0, 1),
        schur_mass.swapaxes(0, 1),
        lift.swapaxes(0, 1),
        recover.transpose(2, 0, 1),
        count,
    )


def per_device(velocity, geometry, element_kind, *rest):
    count = lax.axis_size("planes")
    rows = velocity.shape[1]
    elems = element_kind.shape[0]
    fits = count & (count - 1) == 0 and rows == 16 and elems == LANES and elems * rows == count * LANES and lax.axis_size("elem") == 2
    body = fast_device if fits else plain_device
    return body(velocity, geometry, element_kind, *rest)


def solution(mesh):
    in_specs = (
        P(None, "planes", "elem"),
        P(None, "elem"),
        P("elem"),
        P("elem"),
        P(None, None, "elem"),
        P(),
        P(),
        P(),
        P(),
    )
    out_specs = P(None, "planes", "elem")
    return jax.shard_map(
        per_device, mesh=mesh, in_specs=in_specs, out_specs=out_specs, check_vma=False
    )
```

```python
import functools
import math

import jax
import jax.numpy as jnp
import numpy as np
from jax import lax
from jax.experimental import pallas as pl
from jax.experimental.pallas import tpu as pltpu
from jax.sharding import PartitionSpec as P

PLANES = 256
QUAD = 9
COLUMN_ELEMS = 32
CG_STEPS = 4


HIGHEST = lax.Precision.HIGHEST
SIGMA_COEF = 1.0
BETA_COEF = 0.01
STEP_DT = 0.002


def passed_along(value, axis, steps):
    count = lax.axis_size(axis)
    leading, last = (max(0, -steps), min(count, count - steps))
    return lax.ppermute(value, axis, [(source, source + steps) for source in range(leading, last)])


def gauss_derivative(points):
    nodes = -np.cos(np.pi * (2 * np.arange(points) + 1) / (2 * points))
    ident = np.eye(points)
    diffs = nodes[:, None] - nodes[None, :] + ident
    weights = 1.0 / np.prod(diffs, axis=1)
    matrix = weights[None, :] / weights[:, None] / diffs
    matrix = matrix * (1.0 - ident)
    return matrix - ident * matrix.sum(axis=1)[:, None]


def kron_tables():
    deriv = gauss_derivative(QUAD)
    identity = np.eye(QUAD)
    return (
        jnp.asarray(np.kron(deriv, identity), jnp.float32),
        jnp.asarray(np.kron(identity, deriv), jnp.float32),
    )


def fourier_tables(planes):
    zeta = jnp.arange(planes, dtype=jnp.int32)
    rows = jnp.arange(planes, dtype=jnp.int32)
    waves = (rows + 1) // 2
    phase = waves[None, :] * zeta[:, None] % planes
    angle = 2.0 * math.pi / planes * phase.astype(jnp.float32)
    cosine = jnp.cos(angle)
    sine = jnp.sin(angle)
    odd = (rows % 2 == 1)[None, :]
    first = (rows == 0)[None, :]
    last = (rows == planes - 1)[None, :]
    synth = jnp.where(first, 1.0, jnp.where(odd, cosine, sine))
    rate = BETA_COEF * waves.astype(jnp.float32)[None, :]
    slope = jnp.where(first | last, 0.0, jnp.where(odd, -rate * sine, rate * cosine))
    weight = jnp.where((rows == 0) | (rows == planes - 1), 1.0 / planes, 2.0 / planes).astype(
        jnp.float32
    )
    analysis = synth.T * weight[:, None]
    return (synth, slope, analysis)


def inner(first_pair, second_pair):
    return jnp.sum(first_pair[0] * second_pair[0], axis=(0, 2)) + jnp.sum(
        first_pair[1] * second_pair[1], axis=(0, 2)
    )


def global_total(first_pair, second_pair):
    return lax.psum(inner(first_pair, second_pair), "elem")


def global_squares(pair):
    return lax.psum(inner(pair, pair), "elem")


def assemble(outputs, incoming, free):
    left = outputs[:QUAD]
    right = outputs[QUAD : 2 * QUAD]
    bottom = outputs[2 * QUAD : 3 * QUAD]
    top = outputs[3 * QUAD :]
    vertical = left + jnp.concatenate([incoming, right[:, :, :-COLUMN_ELEMS]], axis=2)
    grid = top.reshape(top.shape[0], top.shape[1], -1, COLUMN_ELEMS)
    shifted = jnp.concatenate([jnp.zeros_like(grid[..., :1]), grid[..., :-1]], axis=3).reshape(
        bottom.shape
    )
    horizontal = bottom + shifted
    return (vertical * free[0], horizontal * free[1])


def plain_device(
    velocity,
    geometry,
    element_kind,
    element_scale,
    dirichlet,
    schur_stiffness,
    schur_mass,
    lift,
    recover,
):
    first, second = kron_tables()
    synth, slope, analysis = fourier_tables(PLANES)
    local_rows = velocity.shape[1]
    node_count = velocity.shape[2]
    share = node_count // lax.axis_size("planes")
    geo_part = lax.dynamic_slice_in_dim(geometry, lax.axis_index("planes") * share, share, 1)

    def transform(table, field):
        return jnp.einsum("zr,crm->czm", table, field, precision=HIGHEST)

    items = lax.all_to_all(velocity, "planes", split_axis=2, concat_axis=1, tiled=True)
    values = transform(synth, items)
    along_z = transform(slope, items)
    shaped = values.reshape(values.shape[:-1] + (-1, QUAD * QUAD))
    along_r = jnp.einsum("...en,mn->...em", shaped, first, precision=HIGHEST).reshape(values.shape)
    along_s = jnp.einsum("...en,mn->...em", shaped, second, precision=HIGHEST).reshape(values.shape)
    along_x = geo_part[0] * along_r + geo_part[1] * along_s
    along_y = geo_part[2] * along_r + geo_part[3] * along_s
    values, along_x, along_y, along_z = (values, along_x, along_y, along_z)
    advection = values[0] * along_x + values[1] * along_y + values[2] * along_z
    advection_hat = jnp.einsum("rz,czm->crm", analysis, advection, precision=HIGHEST)
    returned = lax.all_to_all(advection_hat, "planes", split_axis=1, concat_axis=2, tiled=True)
    intermediate = velocity - STEP_DT * returned
    elem_count = element_kind.shape[0]
    row_count = 3 * local_rows
    waves = (
        (lax.axis_index("planes") * local_rows + jnp.arange(local_rows, dtype=jnp.int32) + 1) // 2
    ).astype(jnp.float32)
    lam = jnp.tile(SIGMA_COEF + (BETA_COEF * waves) ** 2, 3)
    free = (1 - dirichlet).astype(jnp.float32)[:, :, None, :]
    chooser = (element_kind == 1).astype(jnp.float32)

    def element_apply(vector, kinds, scales):
        flat = vector.reshape(vector.shape[0], -1)
        results = []
        for kind in range(2):
            stiff = jnp.dot(schur_stiffness[kind], flat, precision=HIGHEST).reshape(vector.shape)
            massed = jnp.dot(schur_mass[kind], flat, precision=HIGHEST).reshape(vector.shape)
            results.append(stiff + lam[None, :, None] * massed)
        return scales[None, None, :] * jnp.where(kinds[None, None, :] > 0.5, results[1], results[0])

    def element_vector(vertical, horizontal):
        arriving = passed_along(vertical[:, :, :COLUMN_ELEMS], "elem", -1)
        right = jnp.concatenate([vertical[:, :, COLUMN_ELEMS:], arriving], axis=2)
        grid = horizontal.reshape(horizontal.shape[0], horizontal.shape[1], -1, COLUMN_ELEMS)
        top = jnp.concatenate([grid[..., 1:], jnp.zeros_like(grid[..., :1])], axis=3).reshape(
            horizontal.shape
        )
        return jnp.concatenate([vertical, right, horizontal, top], axis=0)

    node_values = (SIGMA_COEF * intermediate).reshape(row_count, elem_count, QUAD * QUAD)
    lifted = jnp.where(
        chooser[None, None, :] > 0.5,
        jnp.einsum("kn,ren->kre", lift[1], node_values, precision=HIGHEST),
        jnp.einsum("kn,ren->kre", lift[0], node_values, precision=HIGHEST),
    )
    lifted_right = passed_along(lifted[QUAD : 2 * QUAD, :, -COLUMN_ELEMS:], "elem", 1)
    forcing = assemble(lifted, lifted_right, free)
    trace = (jnp.zeros_like(forcing[0]), jnp.zeros_like(forcing[1]))
    residual = forcing
    direction = forcing
    norm_now = global_squares(residual)
    for sweep in range(CG_STEPS):
        outputs = element_apply(element_vector(direction[0], direction[1]), chooser, element_scale)
        operator_arriving = passed_along(outputs[QUAD : 2 * QUAD, :, -COLUMN_ELEMS:], "elem", 1)
        image = assemble(outputs, operator_arriving, free)
        alpha = (norm_now / global_total(direction, image))[None, :, None]
        trace = (trace[0] + alpha * direction[0], trace[1] + alpha * direction[1])
        residual = (residual[0] - alpha * image[0], residual[1] - alpha * image[1])
        norm_next = global_squares(residual)
        ratio = (norm_next / norm_now)[None, :, None]
        direction = (residual[0] + ratio * direction[0], residual[1] + ratio * direction[1])
        norm_now = norm_next
    vector = element_vector(trace[0], trace[1])
    recovered = jnp.where(
        chooser[None, :, None] > 0.5,
        jnp.einsum("nl,lre->ren", recover[1], vector, precision=HIGHEST),
        jnp.einsum("nl,lre->ren", recover[0], vector, precision=HIGHEST),
    )
    weight = SIGMA_COEF / (SIGMA_COEF + lam)
    result = (
        intermediate.reshape(row_count, elem_count, QUAD * QUAD) * weight[:, None, None] + recovered
    )
    return result.reshape(velocity.shape)


LANES = 128
EDGE = 40
F32 = jnp.float32
BF16 = jnp.bfloat16


def split(value):
    high = value.astype(BF16)
    return high, (value - high.astype(F32)).astype(BF16)


def np_split(value):
    high = np.asarray(value, np.float32).astype(BF16)
    low = (np.asarray(value, np.float64) - high.astype(np.float64)).astype(np.float32).astype(BF16)
    return high, low


def mm(first, second):
    return jnp.dot(first, second, preferred_element_type=F32)


def stacked_values(values):
    high, low = split(values)
    return jnp.concatenate([high, low, high], axis=0)


def advect_tables(planes):
    zeta = np.arange(planes)
    rows = np.arange(planes)
    waves = (rows + 1) // 2
    angle = 2.0 * np.pi / planes * ((waves[None, :] * zeta[:, None]) % planes)
    odd = (rows % 2 == 1)[None, :]
    first = (rows == 0)[None, :]
    last = (rows == planes - 1)[None, :]
    synth = np.where(first, 1.0, np.where(odd, np.cos(angle), np.sin(angle)))
    rate = BETA_COEF * waves[None, :]
    slope = np.where(first | last, 0.0, np.where(odd, -rate * np.sin(angle), rate * np.cos(angle)))
    weight = np.where((rows == 0) | (rows == planes - 1), 1.0 / planes, 2.0 / planes)
    analysis = synth.T * weight[:, None]
    high, low = np_split(np.concatenate([synth, slope], axis=0))
    forward = np.concatenate([high, high, low], axis=1)
    high, low = np_split(analysis)
    backward = np.concatenate([high, high, low], axis=1)
    points = QUAD * QUAD
    deriv = gauss_derivative(QUAD)
    both = np.zeros((LANES, 2 * LANES))
    both[:points, :points] = np.kron(deriv, np.eye(QUAD)).T
    both[:points, LANES : LANES + points] = np.kron(np.eye(QUAD), deriv).T
    high, low = np_split(both)
    return jnp.asarray(forward), jnp.asarray(backward), jnp.asarray(np.concatenate([high, high, low], axis=0))


def whole_spec(shape):
    return pl.BlockSpec(shape, lambda *_: (0,) * len(shape))


def params():
    return pltpu.CompilerParams(vmem_limit_bytes=60 * 1024 * 1024)


def element_at(part, slot, group):
    inner = part % group
    return part // group * COLUMN_ELEMS + slot * group + inner % 2 * (group // 2) + inner // 2


def stacked_weights(weights):
    high, low = split(weights)
    pad = jnp.zeros((weights.shape[0], LANES - 3 * EDGE), BF16)
    return jnp.concatenate([high, high, low, pad], axis=1)


def stacked_edges(value):
    high = value.astype(BF16).astype(F32)
    pad = jnp.zeros((LANES - 3 * EDGE, value.shape[1]), F32)
    return jnp.concatenate([high, value - high, high, pad], axis=0).astype(BF16)


def tree(terms):
    while len(terms) > 1:
        terms = [terms[at] + terms[at + 1] for at in range(0, len(terms), 2)]
    return terms[0]


def solve_rows(forcing, facts, lam, weights, state, image, traces):
    tiles = forcing.shape[0]
    lane = lax.broadcasted_iota(jnp.int32, (8, LANES), 1)
    sub = lax.broadcasted_iota(jnp.int32, (8, LANES), 0)
    top_edge = lane >= LANES - 8
    low_edge = lane < 8
    zero = jnp.zeros((8, LANES), F32)
    lam = jnp.concatenate([lam] * (EDGE // 8), axis=0)

    def above(tile_of, at):
        if at % 2 == 0:
            return tile_of(at + 1)
        return jnp.where(top_edge, 0.0, pltpu.roll(tile_of(at - 1), LANES - 8, 1))

    def below(tile_of, at):
        if at % 2 == 1:
            return tile_of(at - 1)
        return jnp.where(low_edge, 0.0, pltpu.roll(tile_of(at + 1), 8, 1))

    def edges(tile_of, at):
        beside = at + 2 < tiles
        right = tile_of(0, at + 2) if beside else zero
        right_rest = tile_of(2, at + 2) if beside else zero
        top = above(lambda item: tile_of(1, item), at)
        top_rest = above(lambda item: tile_of(2, item), at)
        rest = jnp.where(sub == 0, right_rest, jnp.where(sub == 2, top_rest, 0.0))
        rest = tile_of(2, at) + pltpu.roll(rest, 1, 0)
        return jnp.concatenate([tile_of(0, at), right, tile_of(1, at), top, rest], axis=0)

    def gather(parts, at):
        part = parts[at]
        fact = facts[at]
        left = part[:8]
        rest = below(lambda item: parts[item][32:40], at)
        if at >= 2:
            left = left + parts[at - 2][8:16]
            rest = jnp.where(sub == 1, parts[at - 2][32:40], jnp.where(sub == 3, rest, 0.0))
        else:
            rest = jnp.where(sub == 3, rest, 0.0)
        rest = part[32:40] + pltpu.roll(rest, 7, 0)
        bottom = part[16:24] + below(lambda item: parts[item][24:32], at)
        return left * fact[:8], bottom * fact[8:16], rest * fact[16:24]

    def total(acc):
        acc = tree([acc] + [pltpu.roll(acc, 8 * step, 1) for step in range(1, LANES // 8)])
        return tree([acc] + [pltpu.roll(acc, step, 0) for step in range(1, 8)])

    def apply():
        sums = [zero, zero, zero]
        parts = []
        for first in range(0, tiles, 2):
            both = jnp.concatenate([edges(lambda which, item: state[2, which, item], at) for at in (first, first + 1)], axis=1)
            both = mm(weights[...], stacked_edges(both))
            for at in (first, first + 1):
                lanes = slice((at - first) * LANES, (at - first + 1) * LANES)
                fact = facts[at]
                is_second = jnp.concatenate([fact[24:32]] * (EDGE // 8), axis=0) > 0.5
                scale = jnp.concatenate([fact[32:40]] * (EDGE // 8), axis=0)
                stiff = jnp.where(is_second, both[EDGE : 2 * EDGE, lanes], both[:EDGE, lanes])
                mass = jnp.where(is_second, both[3 * EDGE :, lanes], both[2 * EDGE : 3 * EDGE, lanes])
                parts.append(scale * (stiff + lam * mass))
            for at in (first, first + 1):
                for which, value in enumerate(gather(parts, at)):
                    image[which, at] = value
                    sums[which] = sums[which] + state[2, which, at] * value
        return total(sums[0] + sums[1] + sums[2])

    sums = [zero, zero, zero]
    parts = {}
    for at in range(tiles):
        parts[at] = forcing[at]
    for at in range(tiles):
        for which, value in enumerate(gather(parts, at)):
            state[0, which, at] = zero
            state[1, which, at] = value
            state[2, which, at] = value
            sums[which] = sums[which] + value * value
    now = total(sums[0] + sums[1] + sums[2])

    def sweep(_, now):
        alpha = now / apply()
        sums = [zero, zero, zero]
        for at in range(tiles):
            for which in range(3):
                state[0, which, at] = state[0, which, at] + alpha * state[2, which, at]
                rest = state[1, which, at] - alpha * image[which, at]
                state[1, which, at] = rest
                sums[which] = sums[which] + rest * rest
        fresh = total(sums[0] + sums[1] + sums[2])
        ratio = fresh / now
        for at in range(tiles):
            for which in range(3):
                state[2, which, at] = state[1, which, at] + ratio * state[2, which, at]
        return fresh

    now = lax.fori_loop(0, CG_STEPS - 1, sweep, now)
    alpha = now / apply()
    found = [[state[0, which, at] + alpha * state[2, which, at] for at in range(tiles)] for which in range(3)]
    for at in range(tiles):
        traces[at] = edges(lambda which, item: found[which][item], at)


def exact(first, second):
    return jnp.dot(first, second, precision=HIGHEST, preferred_element_type=F32)


def iota(shape, axis):
    return lax.broadcasted_iota(jnp.int32, shape, axis)


def lam_of(row):
    return SIGMA_COEF + (BETA_COEF * ((row + 1) // 2).astype(F32)) ** 2


def advect_and_solve(velocity, geometry, kind, scale, dirichlet, stiffness, mass, lift_maps, recover_maps, count):
    elems = kind.shape[1]
    comps, rows, nodes = velocity.shape
    points = QUAD * QUAD
    per = LANES // rows
    pairs = per // 2
    planes = count * rows
    half = count * LANES // 2
    forward, backward, deriv = advect_tables(planes)

    group = COLUMN_ELEMS // per
    columns = count // group
    tiles = count // 2
    chunk = tiles // columns
    ends = 2

    def kernel(
        vel_in, geo_ref, kind_ref, scale_ref, fixed_ref, stiff_ref, mass_ref, lift_in, recover_in,
        forward_in, backward_in, deriv_in,
        out,
        vel_ref, forward_ref, backward_ref, deriv_ref, result,
        mid, kinds, factor, recover_out, sent, recv, hats, ret,
        store, turned, fields, partial, pieces, forcing, traces, found, facts_out, facts,
        state, image, geo, lift_ref, mat_ref, lam_ref, weights, lift_high, lift_low, recover_all,
        send_sem, recv_sem, pair_send, pair_recv, load_sem, out_sem,
    ):
        loads = [pltpu.make_async_copy(vel_in.at[comp], vel_ref.at[comp], load_sem.at[comp]) for comp in range(comps)]
        tables = ((forward_in, forward_ref), (deriv_in, deriv_ref), (backward_in, backward_ref))
        for at, (source, target) in enumerate(tables):
            loads.append(pltpu.make_async_copy(source, target, load_sem.at[comps + at]))
        for load in loads:
            load.start()
        me = lax.axis_index("planes")
        core = lax.axis_index("elem")
        barrier = pltpu.get_barrier_semaphore()

        def peer_at(step):
            return (me + step) % count

        def source_at(step):
            return (me + count - step) % count

        def greet(step, carry):
            pl.semaphore_signal(
                barrier, inc=1, device_id={"planes": peer_at(step)}, device_id_type=pl.DeviceIdType.MESH
            )
            return carry

        lax.fori_loop(1, count, greet, 0)
        pl.semaphore_signal(barrier, inc=1, device_id={"elem": 1 - core}, device_id_type=pl.DeviceIdType.MESH)

        def copy_to(source, target, way, comp, peer):
            return pltpu.make_async_remote_copy(
                src_ref=source.at[comp, peer],
                dst_ref=target.at[comp, me],
                send_sem=send_sem.at[way, comp, peer],
                recv_sem=recv_sem.at[way, comp, me],
                device_id={"planes": peer},
                device_id_type=pl.DeviceIdType.MESH,
            )

        def copy_from(source, target, way, comp, peer):
            return pltpu.make_async_remote_copy(
                src_ref=source.at[comp, peer],
                dst_ref=target.at[comp, peer],
                send_sem=send_sem.at[way, comp, peer],
                recv_sem=recv_sem.at[way, comp, peer],
                device_id={"planes": peer},
                device_id_type=pl.DeviceIdType.MESH,
            )

        def start_all(source, target, way, comp):
            def one(step, carry):
                copy_to(source, target, way, comp, peer_at(step)).start()
                return carry

            lax.fori_loop(1, count, one, 0)

        def pair_copy(source, target, at):
            return pltpu.make_async_remote_copy(
                src_ref=source,
                dst_ref=target,
                send_sem=pair_send.at[at],
                recv_sem=pair_recv.at[at],
                device_id={"elem": 1 - core},
                device_id_type=pl.DeviceIdType.MESH,
            )

        def facts_copy():
            return pair_copy(facts_out, facts.at[pl.ds(core * tiles, tiles)], comps * (columns + ends))

        def facts_arrive():
            pair_copy(facts_out, facts.at[pl.ds((1 - core) * tiles, tiles)], comps * (columns + ends)).wait_recv()

        def lifted_copy(comp, column, side):
            return pair_copy(
                pieces.at[comp, 1 - core, pl.ds(column * chunk, chunk)],
                forcing.at[comp, pl.ds(side * tiles + column * chunk, chunk)],
                comp * columns + column,
            )

        def trace_copy(comp, end, side):
            width = tiles // ends
            return pair_copy(
                traces.at[comp, pl.ds((1 - core) * tiles + end * width, width)],
                found.at[comp, side, pl.ds(end * width, width)],
                comps * columns + comp * ends + end,
            )

        def pack(comp):
            for part in range(count):
                rows_of = []
                for local in range(per):
                    at = element_at(part, local, group) * points
                    rows_of.append(vel_ref[comp, :, at : at + points])
                sent[comp, part] = jnp.concatenate(rows_of, axis=0).T

        def arrive(comp, part, block):
            block = jnp.concatenate([block, jnp.zeros((LANES - points, LANES), F32)], axis=0).T
            for local in range(per):
                at = local % 2 * LANES
                store[local // 2, pl.ds(pl.multiple_of(part * rows, rows), rows), at : at + LANES] = block[
                    local * rows : (local + 1) * rows
                ]

        def arrive_all(comp):
            arrive(comp, me, sent[comp, me])

            def one(step, carry):
                for inner in range(several):
                    part = source_at(1 + step * several + inner)
                    copy_from(sent, recv, 0, comp, part).wait_recv()
                    arrive(comp, part, recv[comp, part])
                return carry

            several = 3 if (count - 1) % 3 == 0 else 1
            lax.fori_loop(0, (count - 1) // several, one, 0)

        def over_pairs(body):
            def one(pair, carry):
                body(pair)
                return carry

            lax.fori_loop(0, pairs, one, 0)

        def synthesize(comp, pair):
            fields[comp, pair] = mm(forward_ref[...], stacked_values(store[pair]))

        def slope_last(pair):
            fields[comps - 1, pair, planes:] = mm(forward_ref[planes:], stacked_values(store[pair]))

        def derive(comp, pair):
            for which in range(2):
                at = slice(which * LANES, (which + 1) * LANES)
                high, low = split(fields[comp, pair, :planes, at])
                slopes = mm(jnp.concatenate([high, low], axis=1), deriv_ref[: 2 * LANES]) + mm(
                    high, deriv_ref[2 * LANES :]
                )
                part = geo[pair * 2 + which]
                first = fields[0, pair, :planes, at]
                second = fields[1, pair, :planes, at]
                partial[comp, pair, :, at] = slopes[:, :LANES] * (first * part[0:1] + second * part[2:3]) + slopes[
                    :, LANES:
                ] * (first * part[1:2] + second * part[3:4])

        def advect(comp, pair, along):
            result = partial[comp, pair] + along * fields[comp, pair, planes:]
            turned[pair] = mm(backward_ref[...], stacked_values(result))

        def first_advect(pair):
            along = mm(forward_ref[:planes], stacked_values(store[pair]))
            fields[comps - 1, pair, :planes] = along
            advect(0, pair, along)

        def turn_back(comp):
            for part in range(count):
                block = jnp.concatenate(
                    [
                        turned[local // 2, part * rows : (part + 1) * rows, local % 2 * LANES : (local % 2 + 1) * LANES]
                        for local in range(per)
                    ],
                    axis=0,
                )
                hats[comp, part] = block.T[:points]

        def lift(comp):
            bit = lax.broadcasted_iota(jnp.int32, (EDGE, LANES), 1) // 8 % 2 == 0
            mine = me // group

            def one(step, carry):
                column = (mine // 2 + step // 2) % 2 * 2 + (mine + step) % 2
                fields_of = []
                for inner in range(group):
                    part = column * group + inner

                    @pl.when(part != me)
                    def _():
                        copy_from(hats, ret, 1, comp, part).wait_recv()

                    @pl.when(part == me)
                    def _():
                        ret[comp, part] = hats[comp, part]

                    value = sent[comp, part] - STEP_DT * ret[comp, part]
                    mid[comp, part] = value
                    fields_of.append(value)
                high, low = split(SIGMA_COEF * jnp.concatenate(fields_of, axis=1))
                both = mm(lift_high[...], high) + (mm(lift_high[...], low) + mm(lift_low[...], high))
                lifted = jnp.where(kinds[column, 0:1] > 0.5, both[EDGE:], both[:EDGE])
                for local in range(chunk):
                    even = lifted[:, 2 * local * LANES : (2 * local + 1) * LANES]
                    odd = lifted[:, (2 * local + 1) * LANES : (2 * local + 2) * LANES]
                    at = column * chunk + local
                    pieces[comp, 0, at] = jnp.where(bit, even, pltpu.roll(odd, 8, 1))
                    pieces[comp, 1, at] = jnp.where(bit, pltpu.roll(even, LANES - 8, 1), odd)
                lifted_copy(comp, column, core).start()
                for local in range(chunk):
                    at = column * chunk + local
                    forcing[comp, core * tiles + at] = pieces[comp, core, at]
                return carry

            lax.fori_loop(0, columns, one, 0)

        def solve(comp):
            for column in range(columns):
                lifted_copy(comp, column, 1 - core).wait_recv()
            solve_rows(forcing.at[comp], facts, lam_ref[...], weights, state, image, traces.at[comp])
            for end in range(ends):
                trace_copy(comp, end, core).start()
            for at in range(tiles):
                found[comp, core, at] = traces[comp, core * tiles + at]

        def leave(comp, end):
            cut = nodes // 2 // LANES * LANES
            lanes = pl.ds(end * cut, (cut, nodes - cut)[end])
            return pltpu.make_async_copy(result.at[comp, :, lanes], out.at[comp, :, lanes], out_sem.at[comp, end])

        def recover(comp):
            bit = lax.broadcasted_iota(jnp.int32, (EDGE, LANES), 1) // 8 % 2 == 0
            for column in range(columns):
                if column == columns // 2:
                    leave(comp, 0).start()
                if column % (columns // ends) == 0:
                    trace_copy(comp, column // (columns // ends), 1 - core).wait_recv()
                edges = []
                for at in range(column * chunk, (column + 1) * chunk):
                    low_rows = found[comp, 0, at]
                    high_rows = found[comp, 1, at]
                    edges.append(jnp.where(bit, low_rows, pltpu.roll(high_rows, 8, 1)))
                    edges.append(jnp.where(bit, pltpu.roll(low_rows, LANES - 8, 1), high_rows))
                both = mm(recover_all[...], stacked_edges(jnp.concatenate(edges, axis=1)))
                node = jnp.where(kinds[column, 0:1] > 0.5, both[88 : 88 + points], both[:points])
                for inner in range(group):
                    part = column * group + inner
                    block = mid[comp, part] * factor[0:1] + node[:, inner * LANES : (inner + 1) * LANES]
                    block = jnp.concatenate([block, jnp.zeros((LANES - points, LANES), F32)], axis=0).T
                    for local in range(per):
                        start = element_at(part, local, group) * points
                        result[comp, :, start : start + points] = block[local * rows : (local + 1) * rows, :points]
            leave(comp, 1).start()

        def prepare():
            def place(row):
                return jnp.where(row < 32, row // 8 * QUAD + row % 8, (row - 32) * QUAD + 8)

            widen = (place(iota((EDGE, 4 * QUAD), 0)) == iota((EDGE, 4 * QUAD), 1)).astype(F32)
            widen_cols = (place(iota((4 * QUAD, EDGE), 1)) == iota((4 * QUAD, EDGE), 0)).astype(F32)
            recover_out[...] = jnp.zeros_like(recover_out)
            for which in range(2):
                at = which * EDGE
                mat_ref[at : at + EDGE] = exact(exact(widen, stiff_ref[:, which, :]), widen_cols)
                at = at + 2 * EDGE
                mat_ref[at : at + EDGE] = exact(exact(widen, mass_ref[:, which, :]), widen_cols)
                lift_ref[which * EDGE : (which + 1) * EDGE] = exact(widen, lift_in[:, which, :])
                recover_out[which * 88 : which * 88 + points] = exact(widen, recover_in[:, which, :]).T
            weights[...] = stacked_weights(mat_ref[...])
            recover_all[...] = stacked_weights(recover_out[...])
            high, low = split(lift_ref[...])
            lift_high[...] = high
            lift_low[...] = low
            is_second = (kind_ref[...] == 1).astype(F32)
            free_v = (1 - fixed_ref[:, 0, :]).astype(F32)
            free_h = (1 - fixed_ref[:, 1, :]).astype(F32)
            none = jnp.zeros((5, elems), F32)
            rest = [free_v[8:9], none[:1], free_h[8:9], none]
            table = jnp.concatenate([free_v[:8], free_h[:8]] + rest + [is_second] * 8 + [scale_ref[...]] * 8, axis=0)
            lane = iota((elems, half), 1)
            element = element_at(lane // LANES * 2 + lane // 8 % 2, lane % LANES // 16, group)
            placed = exact(table, (element == iota((elems, half), 0)).astype(F32))
            for at in range(tiles):
                facts_out[at] = placed[:, at * LANES : (at + 1) * LANES]
                facts[core * tiles + at] = placed[:, at * LANES : (at + 1) * LANES]
            lane = iota((elems, 2 * half), 1)
            element = element_at(lane // LANES, lane % LANES // rows, group)
            spread = (element == iota((elems, 2 * half), 0)).astype(F32)
            placed = exact(jnp.broadcast_to(is_second, (8, elems)), spread)
            width = 2 * half // columns
            for column in range(columns):
                kinds[column] = placed[:, column * width : (column + 1) * width]
            lane = iota((8, LANES), 1)
            lam_ref[...] = lam_of(me * rows + core * 8 + lane % 8)
            factor[...] = SIGMA_COEF / (SIGMA_COEF + lam_of(me * rows + lane % rows))
            geo[...] = jnp.zeros_like(geo)
            for part in range(count):

                @pl.when(me == part)
                def _():
                    for local in range(per):
                        at = element_at(part, local, group) * points
                        geo[local, 0:4, 0:points] = geo_ref[:, at : at + points]

        last = comps - 1
        loads[0].wait()
        pack(0)
        pl.semaphore_wait(barrier, count)
        start_all(sent, recv, 0, 0)
        for comp in range(1, comps):
            loads[comp].wait()
            pack(comp)
            start_all(sent, recv, 0, comp)
        prepare()
        facts_copy().start()
        for load in loads[comps:]:
            load.wait()
        for comp in range(last):
            arrive_all(comp)
            over_pairs(functools.partial(synthesize, comp))
        for comp in range(last):
            over_pairs(functools.partial(derive, comp))
        arrive_all(last)
        for pair in range(pairs):
            first_advect(pair)
        turn_back(0)
        start_all(hats, ret, 1, 0)
        for comp in range(1, last):
            over_pairs(lambda pair, comp=comp: advect(comp, pair, fields[last, pair, :planes]))
            turn_back(comp)
            start_all(hats, ret, 1, comp)
        over_pairs(slope_last)
        over_pairs(functools.partial(derive, last))
        over_pairs(lambda pair: advect(last, pair, fields[last, pair, :planes]))
        turn_back(last)
        start_all(hats, ret, 1, last)
        facts_arrive()
        for comp in range(comps):
            lift(comp)
            if comp > 0:
                recover(comp - 1)
            solve(comp)
        recover(last)
        facts_copy().wait_send()
        for comp in range(comps):
            for column in range(columns):
                lifted_copy(comp, column, core).wait_send()
            for end in range(ends):
                trace_copy(comp, end, core).wait_send()

        def drain(step, carry):
            peer = peer_at(step)
            for comp in range(comps):
                copy_to(sent, recv, 0, comp, peer).wait_send()
            for comp in range(comps):
                copy_to(hats, ret, 1, comp, peer).wait_send()
            return carry

        lax.fori_loop(1, count, drain, 0)
        for comp in range(comps):
            for end in range(2):
                leave(comp, end).wait()

    message = (comps, count, points, LANES)
    operands = (velocity, geometry, kind, scale, dirichlet, stiffness, mass, lift_maps, recover_maps)
    operands = operands + (forward, backward, deriv)
    vmem = pl.BlockSpec(memory_space=pltpu.VMEM)
    anywhere = pl.BlockSpec(memory_space=pl.ANY)
    copies = comps * (columns + ends) + 1
    done = pl.pallas_call(
        kernel,
        in_specs=[anywhere] + [vmem] * 8 + [anywhere] * 3,
        out_specs=anywhere,
        out_shape=jax.ShapeDtypeStruct(velocity.shape, F32),
        scratch_shapes=[
            pltpu.VMEM(velocity.shape, F32),
            pltpu.VMEM(forward.shape, BF16),
            pltpu.VMEM(backward.shape, BF16),
            pltpu.VMEM(deriv.shape, BF16),
            pltpu.VMEM(velocity.shape, F32),
            pltpu.VMEM(message, F32),
            pltpu.VMEM((columns, 8, group * LANES), F32),
            pltpu.VMEM((8, LANES), F32),
            pltpu.VMEM((2 * 88, EDGE), F32),
        ]
        + [pltpu.VMEM(message, F32)] * 4
        + [
            pltpu.VMEM((pairs, planes, 2 * LANES), F32),
            pltpu.VMEM((pairs, planes, 2 * LANES), F32),
            pltpu.VMEM((comps, pairs, 2 * planes, 2 * LANES), F32),
            pltpu.VMEM((comps, pairs, planes, 2 * LANES), F32),
            pltpu.VMEM((comps, 2, tiles, EDGE, LANES), F32),
            pltpu.VMEM((comps, 2 * tiles, EDGE, LANES), F32),
            pltpu.VMEM((comps, 2 * tiles, EDGE, LANES), F32),
            pltpu.VMEM((comps, 2, tiles, EDGE, LANES), F32),
            pltpu.VMEM((tiles, 40, LANES), F32),
            pltpu.VMEM((2 * tiles, 40, LANES), F32),
            pltpu.VMEM((3, 3, 2 * tiles, 8, LANES), F32),
            pltpu.VMEM((3, 2 * tiles, 8, LANES), F32),
            pltpu.VMEM((per, 8, LANES), F32),
            pltpu.VMEM((2 * EDGE, points), F32),
            pltpu.VMEM((4 * EDGE, EDGE), F32),
            pltpu.VMEM((8, LANES), F32),
            pltpu.VMEM((4 * EDGE, LANES), BF16),
            pltpu.VMEM((2 * EDGE, points), BF16),
            pltpu.VMEM((2 * EDGE, points), BF16),
            pltpu.VMEM((2 * 88, LANES), BF16),
        ]
        + [
            pltpu.SemaphoreType.DMA((2, comps, count)),
            pltpu.SemaphoreType.DMA((2, comps, count)),
            pltpu.SemaphoreType.DMA((copies,)),
            pltpu.SemaphoreType.DMA((copies,)),
            pltpu.SemaphoreType.DMA((comps + 3,)),
            pltpu.SemaphoreType.DMA((comps, 2)),
        ],
        compiler_params=pltpu.CompilerParams(
            vmem_limit_bytes=60 * 1024 * 1024, collective_id=0, has_side_effects=True
        ),
        name="advect_and_solve",
    )(*operands)

    def hand_over(source, target, held, in_sem, out_sem):
        comes = [pltpu.make_async_copy(source.at[comp], held.at[comp], in_sem.at[comp]) for comp in range(comps)]
        goes = [pltpu.make_async_copy(held.at[comp], target.at[comp], out_sem.at[comp]) for comp in range(comps)]
        for come in comes:
            come.start()
        for come, go in zip(comes, goes):
            come.wait()
            go.start()
        for go in goes:
            go.wait()

    return pl.pallas_call(
        hand_over,
        in_specs=[anywhere],
        out_specs=anywhere,
        out_shape=jax.ShapeDtypeStruct(velocity.shape, F32),
        scratch_shapes=[
            pltpu.VMEM(velocity.shape, F32),
            pltpu.SemaphoreType.DMA((comps,)),
            pltpu.SemaphoreType.DMA((comps,)),
        ],
        compiler_params=pltpu.CompilerParams(vmem_limit_bytes=60 * 1024 * 1024),
        name="hand_over",
    )(done)


def fast_device(
    velocity,
    geometry,
    element_kind,
    element_scale,
    dirichlet,
    schur_stiffness,
    schur_mass,
    lift,
    recover,
):
    count = lax.axis_size("planes")
    return advect_and_solve(
        velocity,
        geometry,
        element_kind[None],
        element_scale[None],
        dirichlet.swapaxes(0, 1),
        schur_stiffness.swapaxes(0, 1),
        schur_mass.swapaxes(0, 1),
        lift.swapaxes(0, 1),
        recover.transpose(2, 0, 1),
        count,
    )


def per_device(velocity, geometry, element_kind, *rest):
    count = lax.axis_size("planes")
    rows = velocity.shape[1]
    elems = element_kind.shape[0]
    fits = count & (count - 1) == 0 and rows == 16 and elems == LANES and elems * rows == count * LANES and lax.axis_size("elem") == 2
    body = fast_device if fits else plain_device
    return body(velocity, geometry, element_kind, *rest)


def solution(mesh):
    in_specs = (
        P(None, "planes", "elem"),
        P(None, "elem"),
        P("elem"),
        P("elem"),
        P(None, None, "elem"),
        P(),
        P(),
        P(),
        P(),
    )
    out_specs = P(None, "planes", "elem")
    return jax.shard_map(
        per_device, mesh=mesh, in_specs=in_specs, out_specs=out_specs, check_vma=False
    )
```
